256 devices in a mesh: ep: 64 (over z, y, core), rep: 4 (over x).
Axes of the slice: x: 4, y: 4, z: 8, core: 2. Of those that a mesh axis runs over, the one named last changes fastest.
Arguments:
- residual: bfloat16 [4096, 2048], P('ep'), may hold values from -6 to 6
- query_latent: bfloat16 [4096, 8192], P(('ep', 'rep')), may hold values from -32.5 to 32.5
- query_rope: bfloat16 [4096, 1024], P(('ep', 'rep')), may hold values from -4 to 4
- cache_latent: bfloat16 [8192, 32, 512], P(('ep', 'rep')), may hold values from -4.6 to 4.6
- cache_rope: bfloat16 [8192, 2048], P(('ep', 'rep')), may hold values from -4 to 4
- page_table: int32 [4096, 9], P(('ep', 'rep')), may hold values from 0 to 31, as said below
- lengths: int32 [4096], P(('ep', 'rep')), may hold values from 257 to 288, as said below
- value_up: bfloat16 [16, 512, 128], P('rep'), may hold values from -0.25 to 0.25
- out_proj: bfloat16 [2048, 2048], P('rep'), may hold values from -0.125 to 0.125
- routes: int32 [4096, 6], P('ep'), may hold values from 0 to 63, all different within a row; in each aligned block of 64 rows (0 to 63, 64 to 127, ...) at most 12 rows name the same one
- route_weight: float32 [4096, 6], P('ep'), may hold values from 0.05 to 0.6
- placement: int32 [64], replicated, may hold values from 0 to 63, each once
- expert_gate: bfloat16 [64, 2048, 1408], P('ep', None, 'rep'), may hold values from -0.125 to 0.125
- expert_up: bfloat16 [64, 2048, 1408], P('ep', None, 'rep'), may hold values from -0.125 to 0.125
- expert_down: bfloat16 [64, 1408, 2048], P('ep', 'rep'), may hold values from -0.15625 to 0.15625
- shared_gate: bfloat16 [2048, 1408], P(None, 'rep'), may hold values from -0.125 to 0.125
- shared_up: bfloat16 [2048, 1408], P(None, 'rep'), may hold values from -0.125 to 0.125
- shared_down: bfloat16 [1408, 2048], P('rep'), may hold values from -0.15625 to 0.15625
- norm_gain: float32 [2048], replicated, may hold values from 0.5 to 1.5
Outputs:
- normed: bfloat16 [4096, 2048], P(('ep', 'rep'))
The draws below stay inside these ranges and needn't reach their ends.
Inputs may be any that keep to these rules, and one draw needn't show every extreme that they name: `page_table`: entries number the 32 pages of the row's own device. A device's rows come in consecutive groups of 8 that share their first 8 entries; all other entries of a device are distinct. `lengths`: every row's context covers its shared prompt; the last row of every device has the greatest length. `routes`: within the 64 rows of one index of ep, no expert is named by more than 12 rows, a bound that some block reaches. `placement`: each slot holds exactly one expert.
All inputs are finite; a program needn't handle non-finite values.
Results may differ from the reference program's by a relative error of at most 0.014.
Values may be sent and summed in bfloat16 or wider, within the bound.
A program may use at most 128 MiB of HBM per device.

```python
import math
import jax
import jax.numpy as jnp
import numpy as np
from jax import lax

D = 2048
HEADS = 16
LATENT = 512
ROPE = 64
VHEAD = 128
FF = 1408
TOP = 6
ROWS_DEV = 16
SHARE = 8
PAGE = 32
PREFIX = 8
PRIVATE = 1
PAGES_SEQ = 9
POOL = 32
PAGES_ALL = 8192
EXPERTS = 64
GROUP_ROWS = 64
TOKENS = 4096
CAP = 12
N_EP = 64
N_REP = 4


def page_layout(key):
    device_count = TOKENS // ROWS_DEV
    page_keys = jax.random.split(jax.random.fold_in(key, 11), device_count)
    shuffles = jax.vmap(lambda one_key: jax.random.permutation(one_key, POOL))(page_keys).astype(jnp.int32)
    row_ids = jnp.arange(ROWS_DEV, dtype=jnp.int32)
    col_ids = jnp.arange(PAGES_SEQ, dtype=jnp.int32)
    group_total = ROWS_DEV // SHARE
    prefix_pick = (row_ids // SHARE)[:, None] * PREFIX + col_ids[None, :]
    private_pick = group_total * PREFIX + row_ids[:, None] * PRIVATE + (col_ids[None, :] - PREFIX)
    picks = jnp.where(col_ids[None, :] < PREFIX, prefix_pick, private_pick)
    return shuffles[:, picks].reshape(TOKENS, PAGES_SEQ).astype(jnp.int32)


def first_slots(key):
    drawn = jax.random.normal(jax.random.fold_in(key, 16), (PAGES_ALL, LATENT), jnp.float32)
    return jnp.clip(drawn, -4.0, 4.0)


def draw_page_table(key, part):
    return page_layout(key)


def draw_lengths(key, part):
    low_end = PREFIX * PAGE + 1
    high_end = PAGES_SEQ * PAGE
    drawn = jax.random.randint(jax.random.fold_in(key, 12), (TOKENS,), low_end, high_end + 1, dtype=jnp.int32)
    return drawn.at[ROWS_DEV - 1::ROWS_DEV].set(high_end)


def draw_cache_latent(key, part):
    drawn = jax.random.normal(jax.random.fold_in(key, 13), (PAGES_ALL, PAGE, LATENT), jnp.float32)
    pages = jnp.clip(drawn, -4.0, 4.0)
    leading = first_slots(key)
    pages = pages.at[:, 0, :].set(leading)
    return pages.astype(jnp.bfloat16)


def draw_query_latent(key, part):
    drawn = jax.random.normal(jax.random.fold_in(key, 15), (TOKENS, HEADS, LATENT), jnp.float32)
    drawn = 0.6 * jnp.clip(drawn, -4.0, 4.0)
    return drawn.reshape(TOKENS, HEADS * LATENT).astype(jnp.bfloat16)


def steps_of(own_key, extent, cuts, least, high):
    def one(dim, blocks):
        heights = jax.random.uniform(jax.random.fold_in(jax.random.fold_in(own_key, 6), dim), (blocks,), jnp.float32, least / len(cuts), high / len(cuts))
        return jnp.repeat(jnp.exp(heights), extent[dim] // blocks).reshape((-1,) + (1,) * (len(extent) - dim - 1))

    level = one(*cuts[0])
    for cut in cuts[1:]:
        level = level * one(*cut)
    return level


def deal_out(key, own, number, rows, amount, top, bound, lean):
    sequence = jax.random.permutation(key, amount)
    packed, usual = portions_of(amount, rows * top, bound, lean, True), portions_of(amount, rows * top, bound, lean, False)
    places = jnp.arange(amount)

    def named(sizes, rotation):
        used = int((sizes > 0).sum())
        fixed = max(1, used // 4)
        moved = fixed + (places - fixed + rotation * (used - fixed)) % max(1, amount - fixed)
        return jnp.zeros((amount,), jnp.int32).at[sequence[jnp.where(places < fixed, places, moved)]].set(jnp.asarray(sizes, jnp.int32))

    sizes = jnp.where(number % 4 == 0, named(packed, number // 4), named(usual, number - number // 4 - 1))
    mixed = jax.random.permutation(jax.random.fold_in(own, 3), amount)
    source_of, receiver = mixed[0:amount // 2 * 2:2], mixed[1:amount // 2 * 2:2]
    margin = jnp.minimum(sizes[source_of] - 1, bound - sizes[receiver]) // 2
    margin = jnp.where((source_of == sequence[0]) | (receiver == sequence[0]) | (sizes[receiver] == 0), 0, jnp.maximum(margin, 0))
    moved = jax.random.randint(jax.random.fold_in(own, 4), (amount // 2,), 0, 1 << 20) % (margin + 1)
    sizes = sizes.at[source_of].add(-moved).at[receiver].add(moved)
    members = jnp.searchsorted(jnp.cumsum(sizes), jnp.arange(rows * top), side="right").astype(jnp.int32)
    grid = members.reshape(top, rows).T
    grid = grid[jax.random.permutation(jax.random.fold_in(own, 1), rows)]
    rotation = jax.random.randint(jax.random.fold_in(own, 2), (rows, 1), 0, top)
    return jnp.take_along_axis(grid, (jnp.arange(top)[None, :] + rotation) % top, axis=1)


def portions_of(count, total, limit, skew, full):
    portions = [(1 << 20) // math.isqrt(standing ** skew) + 1 for standing in range(1, count + 1)]
    largest = limit if full else min(limit, max(-(-total // count), total * portions[0] // sum(portions)))
    least = 1 if total - largest >= count - 1 else 0
    given, surplus = [largest] + [least] * (count - 1), total - largest - least * (count - 1)
    while surplus > 0:
        movable = [i for i in range(1, count) if given[i] < largest] or [i for i in range(1, count) if given[i] < limit]
        pool, remaining = sum([portions[i] for i in movable]), surplus
        for i in movable:
            addition = min(limit - given[i], max(1, remaining * portions[i] // pool), surplus)
            given[i] = given[i] + addition
            surplus = surplus - addition
    return np.array(given)


def normal_values(own_key, shape, deviation, reach, cuts=(), kind=jnp.bfloat16):
    result = jax.random.normal(own_key, shape, jnp.float32) * deviation
    if len(cuts) > 0:
        result = steps_of(own_key, shape, cuts, -0.22, 0.18) * result
    return jnp.clip(result, min=-reach, max=reach).astype(kind)


def setup_inputs(seed: int = 0) -> dict:
    streams_of = jax.random.split(jax.random.key(seed), 20)
    residual = normal_values(streams_of[0], (TOKENS, D), 1.0, 6.0, ((0, 64),))
    query_latent = draw_query_latent(jax.random.fold_in(streams_of[19], 71), 0)
    query_rope = normal_values(streams_of[2], (TOKENS, HEADS * ROPE), 1.0, 4.0, ((0, 256),))
    cache_latent = draw_cache_latent(jax.random.fold_in(streams_of[19], 71), 0)
    cache_rope = normal_values(streams_of[4], (PAGES_ALL, PAGE * ROPE), 1.0, 4.0, ((0, 256),))
    page_table = draw_page_table(jax.random.fold_in(streams_of[19], 71), 0)
    lengths = draw_lengths(jax.random.fold_in(streams_of[19], 71), 0)
    value_up = normal_values(streams_of[7], (HEADS, LATENT, VHEAD), LATENT ** -0.5, 0.25, ((0, 4),))
    out_proj = normal_values(streams_of[8], (HEADS * VHEAD, D), (HEADS * VHEAD) ** -0.5, 0.125, ((0, 4),))
    routes_keys = jax.random.split(jax.random.fold_in(streams_of[9], 1), TOKENS // GROUP_ROWS)
    routes_turns = jax.random.permutation(jax.random.fold_in(streams_of[9], 3), TOKENS // GROUP_ROWS)
    routes = jax.vmap(lambda own, number: deal_out(jax.random.fold_in(streams_of[9], 2), own, number, GROUP_ROWS, EXPERTS, TOP, CAP, 2))(routes_keys, routes_turns).reshape((TOKENS, TOP))
    route_weight = jnp.clip(0.05 + 0.55 * jax.random.uniform(streams_of[10], (TOKENS, TOP), jnp.float32) ** steps_of(streams_of[10], (TOKENS, TOP), ((0, 64),), -0.2, 0.2), 0.05, 0.6)
    placement = jax.random.permutation(streams_of[11], EXPERTS).astype(jnp.int32)
    expert_gate = normal_values(streams_of[12], (EXPERTS, D, FF), D ** -0.5, 0.125, ((0, 64), (2, 4)))
    expert_up = normal_values(streams_of[13], (EXPERTS, D, FF), D ** -0.5, 0.125, ((0, 64), (2, 4)))
    expert_down = normal_values(streams_of[14], (EXPERTS, FF, D), FF ** -0.5, 0.15625, ((0, 64), (1, 4)))
    shared_gate = normal_values(streams_of[15], (D, FF), D ** -0.5, 0.125, ((1, 4),))
    shared_up = normal_values(streams_of[16], (D, FF), D ** -0.5, 0.125, ((1, 4),))
    shared_down = normal_values(streams_of[17], (FF, D), FF ** -0.5, 0.15625, ((0, 4),))
    norm_gain = jnp.clip(1.0 + 0.1 * jax.random.normal(streams_of[18], (D,), jnp.float32), 0.5, 1.5)
    return dict(residual=residual, query_latent=query_latent, query_rope=query_rope, cache_latent=cache_latent, cache_rope=cache_rope, page_table=page_table, lengths=lengths, value_up=value_up, out_proj=out_proj, routes=routes, route_weight=route_weight, placement=placement, expert_gate=expert_gate, expert_up=expert_up, expert_down=expert_down, shared_gate=shared_gate, shared_up=shared_up, shared_down=shared_down, norm_gain=norm_gain)


EPSILON = 1e-06

def attend_block(query_latent, query_rope, keys_lat, keys_rope, lengths):
    row_count = keys_lat.shape[0]
    key_span = keys_lat.shape[1]
    query_lat = query_latent.reshape(row_count, HEADS, LATENT).astype(jnp.float32)
    query_rot = query_rope.reshape(row_count, HEADS, ROPE).astype(jnp.float32)
    score_scale = 1.0 / math.sqrt(VHEAD + ROPE)
    scores = (jnp.einsum('thr,tlr->thl', query_lat, keys_lat.astype(jnp.float32)) + jnp.einsum('thr,tlr->thl', query_rot, keys_rope.astype(jnp.float32))) * score_scale
    live_mask = (jnp.arange(key_span, dtype=jnp.int32)[None, :] < lengths[:, None])[:, None, :]
    masked = jnp.where(live_mask, scores, -jnp.inf)
    row_peak = lax.optimization_barrier(jnp.max(masked, axis=2, keepdims=True))
    expons = jnp.where(live_mask, jnp.exp(scores - row_peak), 0.0)
    probs = (expons / lax.optimization_barrier(jnp.sum(expons, axis=2, keepdims=True))).astype(jnp.bfloat16)
    latent_out = jnp.einsum('thl,tlr->thr', probs.astype(jnp.float32), keys_lat.astype(jnp.float32))
    return latent_out.astype(jnp.bfloat16)

def reference(residual, query_latent, query_rope, cache_latent, cache_rope, page_table, lengths, value_up, out_proj, routes, route_weight, placement, expert_gate, expert_up, expert_down, shared_gate, shared_up, shared_down, norm_gain):
    block_count = TOKENS // ROWS_DEV
    key_span = PAGES_SEQ * PAGE

    def one_block(block_index):
        start_row = block_index * ROWS_DEV
        table = lax.dynamic_slice_in_dim(page_table, start_row, ROWS_DEV, 0) + block_index * POOL
        keys_lat = cache_latent[table].reshape(ROWS_DEV, key_span, LATENT)
        keys_rope = cache_rope[table].reshape(ROWS_DEV, key_span, ROPE)
        block_query = lax.dynamic_slice_in_dim(query_latent, start_row, ROWS_DEV, 0)
        block_rope = lax.dynamic_slice_in_dim(query_rope, start_row, ROWS_DEV, 0)
        block_len = lax.dynamic_slice_in_dim(lengths, start_row, ROWS_DEV, 0)
        return attend_block(block_query, block_rope, keys_lat, keys_rope, block_len)
    latent_out = lax.map(one_block, jnp.arange(block_count, dtype=jnp.int32)).reshape(TOKENS, HEADS, LATENT)
    head_out = jnp.einsum('thr,hrv->thv', latent_out.astype(jnp.float32), value_up.astype(jnp.float32)).astype(jnp.bfloat16)
    attended = jnp.dot(head_out.reshape(TOKENS, HEADS * VHEAD), out_proj, preferred_element_type=jnp.float32).astype(jnp.bfloat16)
    hidden = (residual.astype(jnp.float32) + attended.astype(jnp.float32)).astype(jnp.bfloat16)
    shared_act = (jax.nn.silu(jnp.dot(hidden, shared_gate, preferred_element_type=jnp.float32)) * jnp.dot(hidden, shared_up, preferred_element_type=jnp.float32)).astype(jnp.bfloat16)
    shared_out = jnp.dot(shared_act, shared_down, preferred_element_type=jnp.float32)
    flat_routes = routes.reshape(-1)
    flat_weight = route_weight.reshape(-1)
    limit_rows = min(TOKENS * TOP, N_EP * CAP)
    quarter_width = FF // N_REP

    def one_expert(total, expert):
        hits = flat_routes == expert
        chosen = jnp.nonzero(hits, size=limit_rows, fill_value=0)[0].astype(jnp.int32)
        hit_count = jnp.sum(hits.astype(jnp.int32))
        valid = jnp.arange(limit_rows, dtype=jnp.int32) < hit_count
        token_index = chosen // TOP
        picked_rows = hidden[token_index]
        slot_index = placement[expert]
        gate_values = jnp.dot(picked_rows, expert_gate[slot_index], preferred_element_type=jnp.float32)
        up_values = jnp.dot(picked_rows, expert_up[slot_index], preferred_element_type=jnp.float32)
        activated = (jax.nn.silu(gate_values) * up_values).astype(jnp.bfloat16)
        down_rows = expert_down[slot_index]
        expert_out = jnp.zeros((limit_rows, D), jnp.float32)
        for quarter in range(N_REP):
            part_out = jnp.dot(activated[:, quarter * quarter_width:(quarter + 1) * quarter_width], down_rows[quarter * quarter_width:(quarter + 1) * quarter_width], preferred_element_type=jnp.float32).astype(jnp.bfloat16)
            expert_out = expert_out + part_out.astype(jnp.float32)
        weight_used = jnp.where(valid, flat_weight[chosen], jnp.zeros((), flat_weight.dtype))
        return (total.at[token_index].add(expert_out * weight_used[:, None]), None)
    routed, _ = lax.scan(one_expert, jnp.zeros((TOKENS, D), jnp.float32), jnp.arange(EXPERTS, dtype=jnp.int32))
    mixed = hidden.astype(jnp.float32) + shared_out + routed
    inverse = lax.rsqrt(lax.optimization_barrier(jnp.mean(mixed * mixed, axis=1, keepdims=True)) + EPSILON)
    return (mixed * inverse * norm_gain).astype(jnp.bfloat16)
```

```python
import math

import jax
import jax.numpy as jnp
from jax import lax
from jax.sharding import PartitionSpec as P

ROPE = 64
VHEAD = 128


EPSILON = 1e-06


def attend_rows(query_latent, query_rope, cache_latent, cache_rope, page_table, lengths):
    row_count, table_len = page_table.shape
    page_count, page_len, latent_width = cache_latent.shape
    rope_width = cache_rope.shape[1] // page_len
    head_count = query_rope.shape[1] // rope_width
    positions = page_count * page_len
    keys_lat = cache_latent.reshape(positions, latent_width)
    keys_rope = cache_rope.reshape(positions, rope_width)
    query_lat = query_latent.reshape(row_count, head_count, latent_width)
    query_rot = query_rope.reshape(row_count, head_count, rope_width)
    score_scale = 1.0 / math.sqrt(VHEAD + ROPE)
    scores = (
        jnp.einsum("thr,pr->thp", query_lat, keys_lat, preferred_element_type=jnp.float32)
        + jnp.einsum("thr,pr->thp", query_rot, keys_rope, preferred_element_type=jnp.float32)
    ) * score_scale
    page_hit = (
        page_table[:, :, None] == jnp.arange(page_count, dtype=jnp.int32)[None, None, :]
    ).astype(jnp.float32)
    context_pos = (
        jnp.arange(table_len, dtype=jnp.int32)[:, None] * page_len
        + jnp.arange(page_len, dtype=jnp.int32)[None, :]
    )
    live = (context_pos[None, :, :] < lengths[:, None, None]).astype(jnp.float32)
    count = jnp.einsum("tkp,tks->tps", page_hit, live).reshape(row_count, 1, positions)
    present = count > 0
    masked = jnp.where(present, scores, -jnp.inf)
    row_peak = jnp.max(masked, axis=2, keepdims=True)
    expons = jnp.where(present, jnp.exp(scores - row_peak), 0.0)
    total = jnp.sum(expons * count, axis=2, keepdims=True)
    probs = (expons / total).astype(jnp.bfloat16)
    weighted = (probs.astype(jnp.float32) * count).astype(jnp.bfloat16)
    latent_out = jnp.einsum("thp,pr->thr", weighted, keys_lat, preferred_element_type=jnp.float32)
    return latent_out.astype(jnp.bfloat16)


def per_device(
    residual,
    query_latent,
    query_rope,
    cache_latent,
    cache_rope,
    page_table,
    lengths,
    value_up,
    out_proj,
    routes,
    route_weight,
    placement,
    expert_gate,
    expert_up,
    expert_down,
    shared_gate,
    shared_up,
    shared_down,
    norm_gain,
):
    replicas = lax.axis_size("rep")
    expert_groups = lax.axis_size("ep")
    rep_index = lax.axis_index("rep")
    latent_out = attend_rows(
        query_latent, query_rope, cache_latent, cache_rope, page_table, lengths
    )
    own_count = latent_out.shape[0]
    swapped = lax.all_to_all(latent_out, "rep", split_axis=1, concat_axis=0, tiled=True)
    group_rows = swapped.shape[0]
    head_out = jnp.einsum(
        "thr,hrv->thv", swapped, value_up, preferred_element_type=jnp.float32
    ).astype(jnp.bfloat16)
    attn_terms = jnp.dot(
        head_out.reshape(group_rows, -1), out_proj, preferred_element_type=jnp.float32
    )
    attended = lax.psum(attn_terms.astype(jnp.bfloat16), "rep")
    hidden = (residual.astype(jnp.float32) + attended.astype(jnp.float32)).astype(jnp.bfloat16)
    model_width = hidden.shape[1]
    shared_act = (
        jax.nn.silu(jnp.dot(hidden, shared_gate, preferred_element_type=jnp.float32))
        * jnp.dot(hidden, shared_up, preferred_element_type=jnp.float32)
    ).astype(jnp.bfloat16)
    shared_terms = jnp.dot(shared_act, shared_down, preferred_element_type=jnp.float32)
    experts = placement.shape[0]
    route_count = routes.shape[1]
    per_group = experts // expert_groups
    capacity = max(
        replicas, min(group_rows, 2 * group_rows * route_count // experts // replicas * replicas)
    )
    share = capacity // replicas
    expert_ids = jnp.arange(experts, dtype=jnp.int32)
    slot_index = jnp.sum(jnp.where(routes[:, :, None] == expert_ids, placement, 0), axis=2).reshape(
        -1
    )
    one_hot = (slot_index[:, None] == expert_ids[None, :]).astype(jnp.int32)
    earlier = jnp.cumsum(one_hot, axis=0) - one_hot
    position = jnp.sum(earlier * one_hot, axis=1)
    assignments = slot_index.shape[0]
    source_row = (
        jnp.full((experts * capacity,), group_rows, jnp.int32)
        .at[slot_index * capacity + position]
        .set(jnp.arange(assignments, dtype=jnp.int32) // route_count)
    ).reshape(experts, capacity)
    own_source = lax.dynamic_slice_in_dim(source_row, rep_index * share, share, 1).reshape(-1)
    padded = jnp.concatenate([hidden, jnp.zeros((1, model_width), jnp.bfloat16)], axis=0)
    outgoing = padded[own_source].reshape(expert_groups, per_group * share, model_width)
    incoming = lax.all_to_all(outgoing, "ep", split_axis=0, concat_axis=0, tiled=True)
    gathered = lax.all_gather(incoming, "rep", axis=0, tiled=False).reshape(
        replicas, expert_groups, per_group, share, model_width
    )
    gate_values = jnp.einsum(
        "qsecd,edf->qsecf", gathered, expert_gate, preferred_element_type=jnp.float32
    )
    up_values = jnp.einsum(
        "qsecd,edf->qsecf", gathered, expert_up, preferred_element_type=jnp.float32
    )
    activated = (jax.nn.silu(gate_values) * up_values).astype(jnp.bfloat16)
    expert_terms = jnp.einsum(
        "qsecf,efd->qsecd", activated, expert_down, preferred_element_type=jnp.float32
    ).astype(jnp.bfloat16)
    summed = lax.psum_scatter(expert_terms, "rep", scatter_dimension=0, tiled=True).reshape(
        expert_groups, per_group * share, model_width
    )
    returned = lax.all_to_all(summed, "ep", split_axis=0, concat_axis=0, tiled=True).reshape(
        experts * share, model_width
    )
    local_pos = position - rep_index * share
    mine = (local_pos >= 0) & (local_pos < share)
    column = slot_index * share + jnp.clip(local_pos, 0, share - 1)
    weight_used = jnp.where(mine, route_weight.reshape(-1), 0.0)
    combine = jnp.sum(
        jnp.where(
            column[:, None] == jnp.arange(experts * share, dtype=jnp.int32)[None, :],
            weight_used[:, None],
            0.0,
        ).reshape(group_rows, route_count, experts * share),
        axis=1,
    )
    routed = jnp.dot(
        combine, returned.astype(jnp.float32), precision=lax.Precision.HIGHEST,
        preferred_element_type=jnp.float32,
    )
    row_sums = lax.psum_scatter(
        (routed + shared_terms).astype(jnp.bfloat16), "rep", scatter_dimension=0, tiled=True
    ).astype(jnp.float32)
    own_hidden = lax.dynamic_slice_in_dim(hidden, rep_index * own_count, own_count, 0)
    mixed = row_sums + own_hidden.astype(jnp.float32)
    inverse = lax.rsqrt(jnp.mean(mixed * mixed, axis=1, keepdims=True) + EPSILON)
    return (mixed * inverse * norm_gain).astype(jnp.bfloat16)


def solution(mesh):
    in_specs = (
        P("ep", None),
        P(("ep", "rep"), None),
        P(("ep", "rep"), None),
        P(("ep", "rep"), None, None),
        P(("ep", "rep"), None),
        P(("ep", "rep"), None),
        P(("ep", "rep")),
        P("rep", None, None),
        P("rep", None),
        P("ep", None),
        P("ep", None),
        P(),
        P("ep", None, "rep"),
        P("ep", None, "rep"),
        P("ep", "rep", None),
        P(None, "rep"),
        P(None, "rep"),
        P("rep", None),
        P(),
    )
    out_specs = P(("ep", "rep"), None)
    return jax.shard_map(
        per_device, mesh=mesh, in_specs=in_specs, out_specs=out_specs, check_vma=False
    )
```

```python
import math

import jax
import jax.numpy as jnp
from jax import lax
from jax.sharding import PartitionSpec as P

ROPE = 64
VHEAD = 128


EPSILON = 1e-06


def attend_rows(query_latent, query_rope, cache_latent, cache_rope, page_table, lengths):
    row_count, table_len = page_table.shape
    page_count, page_len, latent_width = cache_latent.shape
    rope_width = cache_rope.shape[1] // page_len
    head_count = query_rope.shape[1] // rope_width
    positions = page_count * page_len
    keys_lat = cache_latent.reshape(positions, latent_width)
    keys_rope = cache_rope.reshape(positions, rope_width)
    query_lat = query_latent.reshape(row_count, head_count, latent_width)
    query_rot = query_rope.reshape(row_count, head_count, rope_width)
    score_scale = 1.0 / math.sqrt(VHEAD + ROPE)
    scores = (
        jnp.einsum("thr,pr->thp", query_lat, keys_lat, preferred_element_type=jnp.float32)
        + jnp.einsum("thr,pr->thp", query_rot, keys_rope, preferred_element_type=jnp.float32)
    ) * score_scale
    page_hit = (
        page_table[:, :, None] == jnp.arange(page_count, dtype=jnp.int32)[None, None, :]
    ).astype(jnp.float32)
    context_pos = (
        jnp.arange(table_len, dtype=jnp.int32)[:, None] * page_len
        + jnp.arange(page_len, dtype=jnp.int32)[None, :]
    )
    live = (context_pos[None, :, :] < lengths[:, None, None]).astype(jnp.float32)
    count = jnp.einsum("tkp,tks->tps", page_hit, live).reshape(row_count, 1, positions)
    present = count > 0
    masked = jnp.where(present, scores, -jnp.inf)
    row_peak = jnp.max(masked, axis=2, keepdims=True)
    expons = jnp.where(present, jnp.exp(scores - row_peak), 0.0)
    total = jnp.sum(expons * count, axis=2, keepdims=True)
    probs = (expons / total).astype(jnp.bfloat16)
    weighted = (probs.astype(jnp.float32) * count).astype(jnp.bfloat16)
    latent_out = jnp.einsum("thp,pr->thr", weighted, keys_lat, preferred_element_type=jnp.float32)
    return latent_out.astype(jnp.bfloat16)


def rep_exchange(blocks):
    return lax.all_to_all(blocks, "rep", split_axis=0, concat_axis=0, tiled=True)


def per_device(
    residual,
    query_latent,
    query_rope,
    cache_latent,
    cache_rope,
    page_table,
    lengths,
    value_up,
    out_proj,
    routes,
    route_weight,
    placement,
    expert_gate,
    expert_up,
    expert_down,
    shared_gate,
    shared_up,
    shared_down,
    norm_gain,
):
    replicas = lax.axis_size("rep")
    expert_groups = lax.axis_size("ep")
    rep_index = lax.axis_index("rep")
    latent_out = attend_rows(
        query_latent, query_rope, cache_latent, cache_rope, page_table, lengths
    )
    own_count = latent_out.shape[0]
    swapped = lax.all_to_all(latent_out, "rep", split_axis=1, concat_axis=0, tiled=True)
    group_rows = swapped.shape[0]
    head_out = jnp.einsum(
        "thr,hrv->thv", swapped, value_up, preferred_element_type=jnp.float32
    ).astype(jnp.bfloat16)
    attn_terms = jnp.dot(
        head_out.reshape(group_rows, -1), out_proj, preferred_element_type=jnp.float32
    )
    model_width = attn_terms.shape[1]
    terms_in = rep_exchange(attn_terms.astype(jnp.bfloat16).reshape(replicas, own_count, model_width))
    attended = jnp.sum(terms_in.astype(jnp.float32), axis=0).astype(jnp.bfloat16)
    own_residual = lax.dynamic_slice_in_dim(residual, rep_index * own_count, own_count, 0)
    own_hidden = (own_residual.astype(jnp.float32) + attended.astype(jnp.float32)).astype(
        jnp.bfloat16
    )
    hidden = rep_exchange(
        jnp.broadcast_to(own_hidden[None], (replicas, own_count, model_width))
    ).reshape(group_rows, model_width)
    shared_act = (
        jax.nn.silu(jnp.dot(hidden, shared_gate, preferred_element_type=jnp.float32))
        * jnp.dot(hidden, shared_up, preferred_element_type=jnp.float32)
    ).astype(jnp.bfloat16)
    shared_terms = jnp.dot(shared_act, shared_down, preferred_element_type=jnp.float32)
    experts = placement.shape[0]
    route_count = routes.shape[1]
    per_group = experts // expert_groups
    capacity = max(
        replicas, min(group_rows, 2 * group_rows * route_count // experts // replicas * replicas)
    )
    share = capacity // replicas
    expert_ids = jnp.arange(experts, dtype=jnp.int32)
    slot_index = jnp.sum(jnp.where(routes[:, :, None] == expert_ids, placement, 0), axis=2).reshape(
        -1
    )
    one_hot = (slot_index[:, None] == expert_ids[None, :]).astype(jnp.int32)
    earlier = jnp.cumsum(one_hot, axis=0) - one_hot
    position = jnp.sum(earlier * one_hot, axis=1)
    assignments = slot_index.shape[0]
    source_row = (
        jnp.full((experts * capacity,), group_rows, jnp.int32)
        .at[slot_index * capacity + position]
        .set(jnp.arange(assignments, dtype=jnp.int32) // route_count)
    ).reshape(experts, capacity)
    own_source = lax.dynamic_slice_in_dim(source_row, rep_index * share, share, 1).reshape(-1)
    padded = jnp.concatenate([hidden, jnp.zeros((1, model_width), jnp.bfloat16)], axis=0)
    outgoing = padded[own_source].reshape(expert_groups, per_group * share, model_width)
    incoming = lax.all_to_all(outgoing, "ep", split_axis=0, concat_axis=0, tiled=True)
    gathered = rep_exchange(jnp.broadcast_to(incoming[None], (replicas,) + incoming.shape)).reshape(
        replicas, expert_groups, per_group, share, model_width
    )
    gate_values = jnp.einsum(
        "qsecd,edf->qsecf", gathered, expert_gate, preferred_element_type=jnp.float32
    )
    up_values = jnp.einsum(
        "qsecd,edf->qsecf", gathered, expert_up, preferred_element_type=jnp.float32
    )
    activated = (jax.nn.silu(gate_values) * up_values).astype(jnp.bfloat16)
    expert_terms = jnp.einsum(
        "qsecf,efd->qsecd", activated, expert_down, preferred_element_type=jnp.float32
    ).astype(jnp.bfloat16)
    summed = (
        jnp.sum(rep_exchange(expert_terms).astype(jnp.float32), axis=0)
        .astype(jnp.bfloat16)
        .reshape(expert_groups, per_group * share, model_width)
    )
    returned = lax.all_to_all(summed, "ep", split_axis=0, concat_axis=0, tiled=True).reshape(
        experts * share, model_width
    )
    local_pos = position - rep_index * share
    mine = (local_pos >= 0) & (local_pos < share)
    column = slot_index * share + jnp.clip(local_pos, 0, share - 1)
    weight_used = jnp.where(mine, route_weight.reshape(-1), 0.0)
    combine = jnp.sum(
        jnp.where(
            column[:, None] == jnp.arange(experts * share, dtype=jnp.int32)[None, :],
            weight_used[:, None],
            0.0,
        ).reshape(group_rows, route_count, experts * share),
        axis=1,
    )
    routed = jnp.dot(
        combine, returned.astype(jnp.float32), precision=lax.Precision.HIGHEST,
        preferred_element_type=jnp.float32,
    )
    row_sums = jnp.sum(
        rep_exchange(
            (routed + shared_terms).astype(jnp.bfloat16).reshape(replicas, own_count, model_width)
        ).astype(jnp.float32),
        axis=0,
    )
    mixed = row_sums + own_hidden.astype(jnp.float32)
    inverse = lax.rsqrt(jnp.mean(mixed * mixed, axis=1, keepdims=True) + EPSILON)
    return (mixed * inverse * norm_gain).astype(jnp.bfloat16)


def solution(mesh):
    in_specs = (
        P("ep", None),
        P(("ep", "rep"), None),
        P(("ep", "rep"), None),
        P(("ep", "rep"), None, None),
        P(("ep", "rep"), None),
        P(("ep", "rep"), None),
        P(("ep", "rep")),
        P("rep", None, None),
        P("rep", None),
        P("ep", None),
        P("ep", None),
        P(),
        P("ep", None, "rep"),
        P("ep", None, "rep"),
        P("ep", "rep", None),
        P(None, "rep"),
        P(None, "rep"),
        P("rep", None),
        P(),
    )
    out_specs = P(("ep", "rep"), None)
    return jax.shard_map(
        per_device, mesh=mesh, in_specs=in_specs, out_specs=out_specs, check_vma=False
    )
```

```python
import functools
import math

import jax
import jax.numpy as jnp
from jax import lax
from jax.experimental import pallas as pl
from jax.experimental.pallas import tpu as pltpu
from jax.sharding import PartitionSpec as P

ROPE = 64
VHEAD = 128


EPSILON = 1e-06


def attend_rows(query_latent, query_rope, cache_latent, cache_rope, page_table, lengths):
    row_count, table_len = page_table.shape
    page_count, page_len, latent_width = cache_latent.shape
    rope_width = cache_rope.shape[1] // page_len
    head_count = query_rope.shape[1] // rope_width
    positions = page_count * page_len
    keys_lat = cache_latent.reshape(positions, latent_width)
    keys_rope = cache_rope.reshape(positions, rope_width)
    query_lat = query_latent.reshape(row_count, head_count, latent_width)
    query_rot = query_rope.reshape(row_count, head_count, rope_width)
    score_scale = 1.0 / math.sqrt(VHEAD + ROPE)
    scores = (
        jnp.einsum("thr,pr->thp", query_lat, keys_lat, preferred_element_type=jnp.float32)
        + jnp.einsum("thr,pr->thp", query_rot, keys_rope, preferred_element_type=jnp.float32)
    ) * score_scale
    page_hit = (
        page_table[:, :, None] == jnp.arange(page_count, dtype=jnp.int32)[None, None, :]
    ).astype(jnp.float32)
    context_pos = (
        jnp.arange(table_len, dtype=jnp.int32)[:, None] * page_len
        + jnp.arange(page_len, dtype=jnp.int32)[None, :]
    )
    live = (context_pos[None, :, :] < lengths[:, None, None]).astype(jnp.float32)
    count = jnp.einsum("tkp,tks->tps", page_hit, live).reshape(row_count, 1, positions)
    present = count > 0
    masked = jnp.where(present, scores, -jnp.inf)
    row_peak = jnp.max(masked, axis=2, keepdims=True)
    expons = jnp.where(present, jnp.exp(scores - row_peak), 0.0)
    total = jnp.sum(expons * count, axis=2, keepdims=True)
    probs = (expons / total).astype(jnp.bfloat16)
    weighted = (probs.astype(jnp.float32) * count).astype(jnp.bfloat16)
    latent_out = jnp.einsum("thp,pr->thr", weighted, keys_lat, preferred_element_type=jnp.float32)
    return latent_out.astype(jnp.bfloat16)


def _exchange_kernel(axis, other, src_ref, out_ref, send_sems, recv_sems, local_sem):
    count = src_ref.shape[0]
    me = lax.axis_index(axis)
    fixed = lax.axis_index(other)

    def device(peer):
        return (peer, fixed) if axis == "ep" else (fixed, peer)

    def remote(peer, slot):
        return pltpu.make_async_remote_copy(
            src_ref.at[peer],
            out_ref.at[slot],
            send_sems.at[peer],
            recv_sems.at[slot],
            device_id=device(peer),
            device_id_type=pl.DeviceIdType.MESH,
        )

    barrier = pltpu.get_barrier_semaphore()

    def greet(step, carry):
        peer = lax.rem(me + step, count)
        pl.semaphore_signal(
            barrier, 1, device_id=device(peer), device_id_type=pl.DeviceIdType.MESH
        )
        return carry

    lax.fori_loop(1, count, greet, 0)
    pl.semaphore_wait(barrier, count - 1)
    local = pltpu.make_async_copy(src_ref.at[me], out_ref.at[me], local_sem)
    local.start()

    def send(step, carry):
        remote(lax.rem(me + step, count), me).start()
        return carry

    lax.fori_loop(1, count, send, 0)

    def finish(step, carry):
        peer = lax.rem(me + step, count)
        remote(peer, me).wait_send()
        remote(peer, peer).wait_recv()
        return carry

    lax.fori_loop(1, count, finish, 0)
    local.wait()


def exchange(blocks, axis, other, collective_id):
    count = blocks.shape[0]
    return pl.pallas_call(
        functools.partial(_exchange_kernel, axis, other),
        out_shape=jax.ShapeDtypeStruct(blocks.shape, blocks.dtype),
        in_specs=[pl.BlockSpec(memory_space=pl.ANY)],
        out_specs=pl.BlockSpec(memory_space=pl.ANY),
        scratch_shapes=[
            pltpu.SemaphoreType.DMA((count,)),
            pltpu.SemaphoreType.DMA((count,)),
            pltpu.SemaphoreType.DMA(()),
        ],
        compiler_params=pltpu.CompilerParams(collective_id=collective_id, has_side_effects=True),
    )(blocks)


def rep_exchange(blocks):
    return lax.all_to_all(blocks, "rep", split_axis=0, concat_axis=0, tiled=True)


def per_device(
    residual,
    query_latent,
    query_rope,
    cache_latent,
    cache_rope,
    page_table,
    lengths,
    value_up,
    out_proj,
    routes,
    route_weight,
    placement,
    expert_gate,
    expert_up,
    expert_down,
    shared_gate,
    shared_up,
    shared_down,
    norm_gain,
):
    replicas = lax.axis_size("rep")
    expert_groups = lax.axis_size("ep")
    rep_index = lax.axis_index("rep")
    latent_out = attend_rows(
        query_latent, query_rope, cache_latent, cache_rope, page_table, lengths
    )
    own_count = latent_out.shape[0]
    swapped = lax.all_to_all(latent_out, "rep", split_axis=1, concat_axis=0, tiled=True)
    group_rows = swapped.shape[0]
    head_out = jnp.einsum(
        "thr,hrv->thv", swapped, value_up, preferred_element_type=jnp.float32
    ).astype(jnp.bfloat16)
    attn_terms = jnp.dot(
        head_out.reshape(group_rows, -1), out_proj, preferred_element_type=jnp.float32
    )
    model_width = attn_terms.shape[1]
    terms_in = rep_exchange(attn_terms.astype(jnp.bfloat16).reshape(replicas, own_count, model_width))
    attended = jnp.sum(terms_in.astype(jnp.float32), axis=0).astype(jnp.bfloat16)
    own_residual = lax.dynamic_slice_in_dim(residual, rep_index * own_count, own_count, 0)
    own_hidden = (own_residual.astype(jnp.float32) + attended.astype(jnp.float32)).astype(
        jnp.bfloat16
    )
    hidden = rep_exchange(
        jnp.broadcast_to(own_hidden[None], (replicas, own_count, model_width))
    ).reshape(group_rows, model_width)
    shared_act = (
        jax.nn.silu(jnp.dot(hidden, shared_gate, preferred_element_type=jnp.float32))
        * jnp.dot(hidden, shared_up, preferred_element_type=jnp.float32)
    ).astype(jnp.bfloat16)
    shared_terms = jnp.dot(shared_act, shared_down, preferred_element_type=jnp.float32)
    experts = placement.shape[0]
    route_count = routes.shape[1]
    per_group = experts // expert_groups
    capacity = max(
        replicas, min(group_rows, 2 * group_rows * route_count // experts // replicas * replicas)
    )
    share = capacity // replicas
    expert_ids = jnp.arange(experts, dtype=jnp.int32)
    slot_index = jnp.sum(jnp.where(routes[:, :, None] == expert_ids, placement, 0), axis=2).reshape(
        -1
    )
    one_hot = (slot_index[:, None] == expert_ids[None, :]).astype(jnp.int32)
    earlier = jnp.cumsum(one_hot, axis=0) - one_hot
    position = jnp.sum(earlier * one_hot, axis=1)
    assignments = slot_index.shape[0]
    source_row = (
        jnp.full((experts * capacity,), group_rows, jnp.int32)
        .at[slot_index * capacity + position]
        .set(jnp.arange(assignments, dtype=jnp.int32) // route_count)
    ).reshape(experts, capacity)
    own_source = lax.dynamic_slice_in_dim(source_row, rep_index * share, share, 1).reshape(-1)
    padded = jnp.concatenate([hidden, jnp.zeros((1, model_width), jnp.bfloat16)], axis=0)
    outgoing = padded[own_source].reshape(expert_groups, per_group * share, model_width)
    incoming = exchange(outgoing, "ep", "rep", 0)
    gathered = rep_exchange(jnp.broadcast_to(incoming[None], (replicas,) + incoming.shape)).reshape(
        replicas, expert_groups, per_group, share, model_width
    )
    gate_values = jnp.einsum(
        "qsecd,edf->qsecf", gathered, expert_gate, preferred_element_type=jnp.float32
    )
    up_values = jnp.einsum(
        "qsecd,edf->qsecf", gathered, expert_up, preferred_element_type=jnp.float32
    )
    activated = (jax.nn.silu(gate_values) * up_values).astype(jnp.bfloat16)
    expert_terms = jnp.einsum(
        "qsecf,efd->qsecd", activated, expert_down, preferred_element_type=jnp.float32
    ).astype(jnp.bfloat16)
    summed = (
        jnp.sum(rep_exchange(expert_terms).astype(jnp.float32), axis=0)
        .astype(jnp.bfloat16)
        .reshape(expert_groups, per_group * share, model_width)
    )
    returned = exchange(summed, "ep", "rep", 1).reshape(
        experts * share, model_width
    )
    local_pos = position - rep_index * share
    mine = (local_pos >= 0) & (local_pos < share)
    column = slot_index * share + jnp.clip(local_pos, 0, share - 1)
    weight_used = jnp.where(mine, route_weight.reshape(-1), 0.0)
    combine = jnp.sum(
        jnp.where(
            column[:, None] == jnp.arange(experts * share, dtype=jnp.int32)[None, :],
            weight_used[:, None],
            0.0,
        ).reshape(group_rows, route_count, experts * share),
        axis=1,
    )
    routed = jnp.dot(
        combine, returned.astype(jnp.float32), precision=lax.Precision.HIGHEST,
        preferred_element_type=jnp.float32,
    )
    row_sums = jnp.sum(
        rep_exchange(
            (routed + shared_terms).astype(jnp.bfloat16).reshape(replicas, own_count, model_width)
        ).astype(jnp.float32),
        axis=0,
    )
    mixed = row_sums + own_hidden.astype(jnp.float32)
    inverse = lax.rsqrt(jnp.mean(mixed * mixed, axis=1, keepdims=True) + EPSILON)
    return (mixed * inverse * norm_gain).astype(jnp.bfloat16)


def solution(mesh):
    in_specs = (
        P("ep", None),
        P(("ep", "rep"), None),
        P(("ep", "rep"), None),
        P(("ep", "rep"), None, None),
        P(("ep", "rep"), None),
        P(("ep", "rep"), None),
        P(("ep", "rep")),
        P("rep", None, None),
        P("rep", None),
        P("ep", None),
        P("ep", None),
        P(),
        P("ep", None, "rep"),
        P("ep", None, "rep"),
        P("ep", "rep", None),
        P(None, "rep"),
        P(None, "rep"),
        P("rep", None),
        P(),
    )
    out_specs = P(("ep", "rep"), None)
    return jax.shard_map(
        per_device, mesh=mesh, in_specs=in_specs, out_specs=out_specs, check_vma=False
    )
```

```python
import functools
import math

import jax
import jax.numpy as jnp
from jax import lax
from jax.experimental import pallas as pl
from jax.experimental.pallas import tpu as pltpu
from jax.sharding import PartitionSpec as P

ROPE = 64
VHEAD = 128


EPSILON = 1e-06


def attend_rows(query_latent, query_rope, cache_latent, cache_rope, page_table, lengths):
    row_count, table_len = page_table.shape
    page_count, page_len, latent_width = cache_latent.shape
    rope_width = cache_rope.shape[1] // page_len
    head_count = query_rope.shape[1] // rope_width
    positions = page_count * page_len
    keys_lat = cache_latent.reshape(positions, latent_width)
    keys_rope = cache_rope.reshape(positions, rope_width)
    query_lat = query_latent.reshape(row_count, head_count, latent_width)
    query_rot = query_rope.reshape(row_count, head_count, rope_width)
    score_scale = 1.0 / math.sqrt(VHEAD + ROPE)
    scores = (
        jnp.einsum("thr,pr->thp", query_lat, keys_lat, preferred_element_type=jnp.float32)
        + jnp.einsum("thr,pr->thp", query_rot, keys_rope, preferred_element_type=jnp.float32)
    ) * score_scale
    page_hit = (
        page_table[:, :, None] == jnp.arange(page_count, dtype=jnp.int32)[None, None, :]
    ).astype(jnp.float32)
    context_pos = (
        jnp.arange(table_len, dtype=jnp.int32)[:, None] * page_len
        + jnp.arange(page_len, dtype=jnp.int32)[None, :]
    )
    live = (context_pos[None, :, :] < lengths[:, None, None]).astype(jnp.float32)
    count = jnp.einsum("tkp,tks->tps", page_hit, live).reshape(row_count, 1, positions)
    present = count > 0
    masked = jnp.where(present, scores, -jnp.inf)
    row_peak = jnp.max(masked, axis=2, keepdims=True)
    expons = jnp.where(present, jnp.exp(scores - row_peak), 0.0)
    total = jnp.sum(expons * count, axis=2, keepdims=True)
    probs = (expons / total).astype(jnp.bfloat16)
    weighted = (probs.astype(jnp.float32) * count).astype(jnp.bfloat16)
    latent_out = jnp.einsum("thp,pr->thr", weighted, keys_lat, preferred_element_type=jnp.float32)
    return latent_out.astype(jnp.bfloat16)


def _exchange_kernel(axis, other, src_ref, out_ref, send_sems, recv_sems, local_sem):
    count = src_ref.shape[0]
    me = lax.axis_index(axis)
    fixed = lax.axis_index(other)

    def device(peer):
        return (peer, fixed) if axis == "ep" else (fixed, peer)

    def remote(peer, slot):
        return pltpu.make_async_remote_copy(
            src_ref.at[peer],
            out_ref.at[slot],
            send_sems.at[peer],
            recv_sems.at[slot],
            device_id=device(peer),
            device_id_type=pl.DeviceIdType.MESH,
        )

    barrier = pltpu.get_barrier_semaphore()

    def greet(step, carry):
        peer = lax.rem(me + step, count)
        pl.semaphore_signal(
            barrier, 1, device_id=device(peer), device_id_type=pl.DeviceIdType.MESH
        )
        return carry

    lax.fori_loop(1, count, greet, 0)
    pl.semaphore_wait(barrier, count - 1)
    local = pltpu.make_async_copy(src_ref.at[me], out_ref.at[me], local_sem)
    local.start()

    def send(step, carry):
        remote(lax.rem(me + step, count), me).start()
        return carry

    lax.fori_loop(1, count, send, 0)

    def finish(step, carry):
        peer = lax.rem(me + step, count)
        remote(peer, me).wait_send()
        remote(peer, peer).wait_recv()
        return carry

    lax.fori_loop(1, count, finish, 0)
    local.wait()


def exchange(blocks, axis, other, collective_id):
    count = blocks.shape[0]
    return pl.pallas_call(
        functools.partial(_exchange_kernel, axis, other),
        out_shape=jax.ShapeDtypeStruct(blocks.shape, blocks.dtype),
        in_specs=[pl.BlockSpec(memory_space=pl.ANY)],
        out_specs=pl.BlockSpec(memory_space=pl.ANY),
        scratch_shapes=[
            pltpu.SemaphoreType.DMA((count,)),
            pltpu.SemaphoreType.DMA((count,)),
            pltpu.SemaphoreType.DMA(()),
        ],
        compiler_params=pltpu.CompilerParams(collective_id=collective_id, has_side_effects=True),
    )(blocks)


def _dispatch_kernel(src_ref, out_ref, ep_send, ep_recv, local_sem, x_send, x_recv):
    chunks, groups = src_ref.shape[0], src_ref.shape[1]
    replicas = out_ref.shape[1]
    me_e = lax.axis_index("ep")
    me_r = lax.axis_index("rep")
    mesh_id = pl.DeviceIdType.MESH

    def ep_copy(c, peer, slot):
        return pltpu.make_async_remote_copy(
            src_ref.at[c, peer],
            out_ref.at[c, me_r, slot],
            ep_send.at[c, peer],
            ep_recv.at[c, slot],
            device_id=(peer, me_r),
            device_id_type=mesh_id,
        )

    def x_copy(c, peer, slot):
        return pltpu.make_async_remote_copy(
            out_ref.at[c, me_r],
            out_ref.at[c, slot],
            x_send.at[c, peer],
            x_recv.at[c, slot],
            device_id=(me_e, peer),
            device_id_type=mesh_id,
        )

    barrier = pltpu.get_barrier_semaphore()

    def greet(step, carry):
        pl.semaphore_signal(
            barrier, 1, device_id=(lax.rem(me_e + step, groups), me_r), device_id_type=mesh_id
        )
        return carry

    lax.fori_loop(1, groups, greet, 0)
    for step in range(1, replicas):
        pl.semaphore_signal(
            barrier, 1, device_id=(me_e, lax.rem(me_r + step, replicas)), device_id_type=mesh_id
        )
    pl.semaphore_wait(barrier, groups - 1 + replicas - 1)

    locals_ = []
    for c in range(chunks):
        local = pltpu.make_async_copy(src_ref.at[c, me_e], out_ref.at[c, me_r, me_e], local_sem.at[c])
        local.start()
        locals_.append(local)

        def send(step, carry, c=c):
            ep_copy(c, lax.rem(me_e + step, groups), me_e).start()
            return carry

        lax.fori_loop(1, groups, send, 0)

    for c in range(chunks):
        locals_[c].wait()

        def arrive(step, carry, c=c):
            peer = lax.rem(me_e + step, groups)
            ep_copy(c, peer, peer).wait_recv()
            return carry

        lax.fori_loop(1, groups, arrive, 0)
        for step in range(1, replicas):
            x_copy(c, lax.rem(me_r + step, replicas), me_r).start()

    for c in range(chunks):
        for step in range(1, replicas):
            peer = lax.rem(me_r + step, replicas)
            x_copy(c, peer, me_r).wait_send()
            x_copy(c, peer, peer).wait_recv()

        def sent(step, carry, c=c):
            ep_copy(c, lax.rem(me_e + step, groups), me_e).wait_send()
            return carry

        lax.fori_loop(1, groups, sent, 0)


def dispatch(blocks, replicas):
    chunks, groups = blocks.shape[:2]
    out_shape = (chunks, replicas) + blocks.shape[1:]
    return pl.pallas_call(
        _dispatch_kernel,
        out_shape=jax.ShapeDtypeStruct(out_shape, blocks.dtype),
        in_specs=[pl.BlockSpec(memory_space=pl.ANY)],
        out_specs=pl.BlockSpec(memory_space=pl.ANY),
        scratch_shapes=[
            pltpu.SemaphoreType.DMA((chunks, groups)),
            pltpu.SemaphoreType.DMA((chunks, groups)),
            pltpu.SemaphoreType.DMA((chunks,)),
            pltpu.SemaphoreType.DMA((chunks, replicas)),
            pltpu.SemaphoreType.DMA((chunks, replicas)),
        ],
        compiler_params=pltpu.CompilerParams(collective_id=2, has_side_effects=True),
    )(blocks)


def rep_exchange(blocks):
    return lax.all_to_all(blocks, "rep", split_axis=0, concat_axis=0, tiled=True)


def per_device(
    residual,
    query_latent,
    query_rope,
    cache_latent,
    cache_rope,
    page_table,
    lengths,
    value_up,
    out_proj,
    routes,
    route_weight,
    placement,
    expert_gate,
    expert_up,
    expert_down,
    shared_gate,
    shared_up,
    shared_down,
    norm_gain,
):
    replicas = lax.axis_size("rep")
    expert_groups = lax.axis_size("ep")
    rep_index = lax.axis_index("rep")
    latent_out = attend_rows(
        query_latent, query_rope, cache_latent, cache_rope, page_table, lengths
    )
    own_count = latent_out.shape[0]
    swapped = lax.all_to_all(latent_out, "rep", split_axis=1, concat_axis=0, tiled=True)
    group_rows = swapped.shape[0]
    head_out = jnp.einsum(
        "thr,hrv->thv", swapped, value_up, preferred_element_type=jnp.float32
    ).astype(jnp.bfloat16)
    attn_terms = jnp.dot(
        head_out.reshape(group_rows, -1), out_proj, preferred_element_type=jnp.float32
    )
    model_width = attn_terms.shape[1]
    terms_in = rep_exchange(attn_terms.astype(jnp.bfloat16).reshape(replicas, own_count, model_width))
    attended = jnp.sum(terms_in.astype(jnp.float32), axis=0).astype(jnp.bfloat16)
    own_residual = lax.dynamic_slice_in_dim(residual, rep_index * own_count, own_count, 0)
    own_hidden = (own_residual.astype(jnp.float32) + attended.astype(jnp.float32)).astype(
        jnp.bfloat16
    )
    hidden = rep_exchange(
        jnp.broadcast_to(own_hidden[None], (replicas, own_count, model_width))
    ).reshape(group_rows, model_width)
    shared_act = (
        jax.nn.silu(jnp.dot(hidden, shared_gate, preferred_element_type=jnp.float32))
        * jnp.dot(hidden, shared_up, preferred_element_type=jnp.float32)
    ).astype(jnp.bfloat16)
    shared_terms = jnp.dot(shared_act, shared_down, preferred_element_type=jnp.float32)
    experts = placement.shape[0]
    route_count = routes.shape[1]
    assert experts == expert_groups
    capacity = max(
        replicas, min(group_rows, 2 * group_rows * route_count // experts // replicas * replicas)
    )
    share = capacity // replicas
    expert_ids = jnp.arange(experts, dtype=jnp.int32)
    slot_index = jnp.sum(jnp.where(routes[:, :, None] == expert_ids, placement, 0), axis=2).reshape(
        -1
    )
    one_hot = (slot_index[:, None] == expert_ids[None, :]).astype(jnp.int32)
    earlier = jnp.cumsum(one_hot, axis=0) - one_hot
    position = jnp.sum(earlier * one_hot, axis=1)
    assignments = slot_index.shape[0]
    source_row = (
        jnp.full((experts * capacity,), group_rows, jnp.int32)
        .at[slot_index * capacity + position]
        .set(jnp.arange(assignments, dtype=jnp.int32) // route_count)
    ).reshape(experts, capacity)
    own_source = lax.dynamic_slice_in_dim(source_row, rep_index * share, share, 1).T.reshape(-1)
    padded = jnp.concatenate([hidden, jnp.zeros((1, model_width), jnp.bfloat16)], axis=0)
    lanes = 128
    outgoing = padded[own_source].reshape(share, experts, model_width // lanes, lanes)
    gathered = dispatch(outgoing, replicas).reshape(share, replicas, expert_groups, model_width)
    gate_values = jnp.einsum(
        "cqgd,df->cqgf", gathered, expert_gate[0], preferred_element_type=jnp.float32
    )
    up_values = jnp.einsum(
        "cqgd,df->cqgf", gathered, expert_up[0], preferred_element_type=jnp.float32
    )
    activated = (jax.nn.silu(gate_values) * up_values).astype(jnp.bfloat16)
    expert_terms = jnp.einsum(
        "cqgf,fd->qcgd", activated, expert_down[0], preferred_element_type=jnp.float32
    ).astype(jnp.bfloat16)
    summed = jnp.sum(rep_exchange(expert_terms).astype(jnp.float32), axis=0).astype(jnp.bfloat16)
    returned = exchange(jnp.transpose(summed, (1, 0, 2)), "ep", "rep", 1).reshape(
        experts * share, model_width
    )
    local_pos = position - rep_index * share
    mine = (local_pos >= 0) & (local_pos < share)
    column = slot_index * share + jnp.clip(local_pos, 0, share - 1)
    weight_used = jnp.where(mine, route_weight.reshape(-1), 0.0)
    combine = jnp.sum(
        jnp.where(
            column[:, None] == jnp.arange(experts * share, dtype=jnp.int32)[None, :],
            weight_used[:, None],
            0.0,
        ).reshape(group_rows, route_count, experts * share),
        axis=1,
    )
    routed = jnp.dot(
        combine, returned.astype(jnp.float32), precision=lax.Precision.HIGHEST,
        preferred_element_type=jnp.float32,
    )
    row_sums = jnp.sum(
        rep_exchange(
            (routed + shared_terms).astype(jnp.bfloat16).reshape(replicas, own_count, model_width)
        ).astype(jnp.float32),
        axis=0,
    )
    mixed = row_sums + own_hidden.astype(jnp.float32)
    inverse = lax.rsqrt(jnp.mean(mixed * mixed, axis=1, keepdims=True) + EPSILON)
    return (mixed * inverse * norm_gain).astype(jnp.bfloat16)


def solution(mesh):
    in_specs = (
        P("ep", None),
        P(("ep", "rep"), None),
        P(("ep", "rep"), None),
        P(("ep", "rep"), None, None),
        P(("ep", "rep"), None),
        P(("ep", "rep"), None),
        P(("ep", "rep")),
        P("rep", None, None),
        P("rep", None),
        P("ep", None),
        P("ep", None),
        P(),
        P("ep", None, "rep"),
        P("ep", None, "rep"),
        P("ep", "rep", None),
        P(None, "rep"),
        P(None, "rep"),
        P("rep", None),
        P(),
    )
    out_specs = P(("ep", "rep"), None)
    return jax.shard_map(
        per_device, mesh=mesh, in_specs=in_specs, out_specs=out_specs, check_vma=False
    )
```

```python
import functools
import math

import jax
import jax.numpy as jnp
from jax import lax
from jax.experimental import pallas as pl
from jax.experimental.pallas import tpu as pltpu
from jax.sharding import PartitionSpec as P

ROPE = 64
VHEAD = 128


EPSILON = 1e-06


def attend_rows(query_latent, query_rope, cache_latent, cache_rope, page_table, lengths):
    row_count, table_len = page_table.shape
    page_count, page_len, latent_width = cache_latent.shape
    rope_width = cache_rope.shape[1] // page_len
    head_count = query_rope.shape[1] // rope_width
    positions = page_count * page_len
    keys_lat = cache_latent.reshape(positions, latent_width)
    keys_rope = cache_rope.reshape(positions, rope_width)
    query_lat = query_latent.reshape(row_count, head_count, latent_width)
    query_rot = query_rope.reshape(row_count, head_count, rope_width)
    score_scale = 1.0 / math.sqrt(VHEAD + ROPE)
    scores = (
        jnp.einsum("thr,pr->thp", query_lat, keys_lat, preferred_element_type=jnp.float32)
        + jnp.einsum("thr,pr->thp", query_rot, keys_rope, preferred_element_type=jnp.float32)
    ) * score_scale
    page_hit = (
        page_table[:, :, None] == jnp.arange(page_count, dtype=jnp.int32)[None, None, :]
    ).astype(jnp.float32)
    context_pos = (
        jnp.arange(table_len, dtype=jnp.int32)[:, None] * page_len
        + jnp.arange(page_len, dtype=jnp.int32)[None, :]
    )
    live = (context_pos[None, :, :] < lengths[:, None, None]).astype(jnp.float32)
    count = jnp.einsum("tkp,tks->tps", page_hit, live).reshape(row_count, 1, positions)
    present = count > 0
    masked = jnp.where(present, scores, -jnp.inf)
    row_peak = jnp.max(masked, axis=2, keepdims=True)
    expons = jnp.where(present, jnp.exp(scores - row_peak), 0.0)
    total = jnp.sum(expons * count, axis=2, keepdims=True)
    probs = (expons / total).astype(jnp.bfloat16)
    weighted = (probs.astype(jnp.float32) * count).astype(jnp.bfloat16)
    latent_out = jnp.einsum("thp,pr->thr", weighted, keys_lat, preferred_element_type=jnp.float32)
    return latent_out.astype(jnp.bfloat16)


def _exchange_kernel(axis, other, src_ref, out_ref, send_sems, recv_sems, local_sem):
    count = src_ref.shape[0]
    me = lax.axis_index(axis)
    fixed = lax.axis_index(other)

    def device(peer):
        return (peer, fixed) if axis == "ep" else (fixed, peer)

    def remote(peer, slot):
        return pltpu.make_async_remote_copy(
            src_ref.at[peer],
            out_ref.at[slot],
            send_sems.at[peer],
            recv_sems.at[slot],
            device_id=device(peer),
            device_id_type=pl.DeviceIdType.MESH,
        )

    barrier = pltpu.get_barrier_semaphore()

    def greet(step, carry):
        peer = lax.rem(me + step, count)
        pl.semaphore_signal(
            barrier, 1, device_id=device(peer), device_id_type=pl.DeviceIdType.MESH
        )
        return carry

    lax.fori_loop(1, count, greet, 0)
    pl.semaphore_wait(barrier, count - 1)
    local = pltpu.make_async_copy(src_ref.at[me], out_ref.at[me], local_sem)
    local.start()

    def send(step, carry):
        remote(lax.rem(me + step, count), me).start()
        return carry

    lax.fori_loop(1, count, send, 0)

    def finish(step, carry):
        peer = lax.rem(me + step, count)
        remote(peer, me).wait_send()
        remote(peer, peer).wait_recv()
        return carry

    lax.fori_loop(1, count, finish, 0)
    local.wait()


def exchange(blocks, axis, other, collective_id):
    count = blocks.shape[0]
    return pl.pallas_call(
        functools.partial(_exchange_kernel, axis, other),
        out_shape=jax.ShapeDtypeStruct(blocks.shape, blocks.dtype),
        in_specs=[pl.BlockSpec(memory_space=pl.ANY)],
        out_specs=pl.BlockSpec(memory_space=pl.ANY),
        scratch_shapes=[
            pltpu.SemaphoreType.DMA((count,)),
            pltpu.SemaphoreType.DMA((count,)),
            pltpu.SemaphoreType.DMA(()),
        ],
        compiler_params=pltpu.CompilerParams(collective_id=collective_id, has_side_effects=True),
    )(blocks)


def _dispatch_kernel(src_ref, out_ref, ep_send, ep_recv, local_sem, x_send, x_recv):
    chunks, groups = src_ref.shape[0], src_ref.shape[1]
    replicas = out_ref.shape[1]
    me_e = lax.axis_index("ep")
    me_r = lax.axis_index("rep")
    mesh_id = pl.DeviceIdType.MESH

    def ep_copy(c, peer, slot):
        return pltpu.make_async_remote_copy(
            src_ref.at[c, peer],
            out_ref.at[c, me_r, slot],
            ep_send.at[c, peer],
            ep_recv.at[c, slot],
            device_id=(peer, me_r),
            device_id_type=mesh_id,
        )

    def x_copy(c, peer, slot):
        return pltpu.make_async_remote_copy(
            out_ref.at[c, me_r],
            out_ref.at[c, slot],
            x_send.at[c, peer],
            x_recv.at[c, slot],
            device_id=(me_e, peer),
            device_id_type=mesh_id,
        )

    barrier = pltpu.get_barrier_semaphore()

    def greet(step, carry):
        pl.semaphore_signal(
            barrier, 1, device_id=(lax.rem(me_e + step, groups), me_r), device_id_type=mesh_id
        )
        return carry

    lax.fori_loop(1, groups, greet, 0)
    for step in range(1, replicas):
        pl.semaphore_signal(
            barrier, 1, device_id=(me_e, lax.rem(me_r + step, replicas)), device_id_type=mesh_id
        )
    pl.semaphore_wait(barrier, groups - 1 + replicas - 1)

    locals_ = []
    for c in range(chunks):
        local = pltpu.make_async_copy(src_ref.at[c, me_e], out_ref.at[c, me_r, me_e], local_sem.at[c])
        local.start()
        locals_.append(local)

        def send(step, carry, c=c):
            ep_copy(c, lax.rem(me_e + step, groups), me_e).start()
            return carry

        lax.fori_loop(1, groups, send, 0)

    for c in range(chunks):
        locals_[c].wait()

        def arrive(step, carry, c=c):
            peer = lax.rem(me_e + step, groups)
            ep_copy(c, peer, peer).wait_recv()
            return carry

        lax.fori_loop(1, groups, arrive, 0)
        for step in range(1, replicas):
            x_copy(c, lax.rem(me_r + step, replicas), me_r).start()

    for c in range(chunks):
        for step in range(1, replicas):
            peer = lax.rem(me_r + step, replicas)
            x_copy(c, peer, me_r).wait_send()
            x_copy(c, peer, peer).wait_recv()

        def sent(step, carry, c=c):
            ep_copy(c, lax.rem(me_e + step, groups), me_e).wait_send()
            return carry

        lax.fori_loop(1, groups, sent, 0)


def dispatch(blocks, replicas):
    chunks, groups = blocks.shape[:2]
    out_shape = (chunks, replicas) + blocks.shape[1:]
    return pl.pallas_call(
        _dispatch_kernel,
        out_shape=jax.ShapeDtypeStruct(out_shape, blocks.dtype),
        in_specs=[pl.BlockSpec(memory_space=pl.ANY)],
        out_specs=pl.BlockSpec(memory_space=pl.ANY),
        scratch_shapes=[
            pltpu.SemaphoreType.DMA((chunks, groups)),
            pltpu.SemaphoreType.DMA((chunks, groups)),
            pltpu.SemaphoreType.DMA((chunks,)),
            pltpu.SemaphoreType.DMA((chunks, replicas)),
            pltpu.SemaphoreType.DMA((chunks, replicas)),
        ],
        compiler_params=pltpu.CompilerParams(collective_id=2, has_side_effects=True),
    )(blocks)


def _combine_kernel(terms_ref, out_ref, parts, sums, x_send, x_recv, x_local, ep_send, ep_recv, ep_local):
    replicas, chunks, groups = terms_ref.shape[:3]
    me_e = lax.axis_index("ep")
    me_r = lax.axis_index("rep")
    mesh_id = pl.DeviceIdType.MESH

    def x_copy(c, peer, slot):
        return pltpu.make_async_remote_copy(
            terms_ref.at[peer, c],
            parts.at[c, slot],
            x_send.at[c, peer],
            x_recv.at[c, slot],
            device_id=(me_e, peer),
            device_id_type=mesh_id,
        )

    def ep_copy(c, peer, slot):
        return pltpu.make_async_remote_copy(
            sums.at[c, peer],
            out_ref.at[c, slot],
            ep_send.at[c, peer],
            ep_recv.at[c, slot],
            device_id=(peer, me_r),
            device_id_type=mesh_id,
        )

    barrier = pltpu.get_barrier_semaphore()

    def greet(step, carry):
        pl.semaphore_signal(
            barrier, 1, device_id=(lax.rem(me_e + step, groups), me_r), device_id_type=mesh_id
        )
        return carry

    lax.fori_loop(1, groups, greet, 0)
    for step in range(1, replicas):
        pl.semaphore_signal(
            barrier, 1, device_id=(me_e, lax.rem(me_r + step, replicas)), device_id_type=mesh_id
        )
    pl.semaphore_wait(barrier, groups - 1 + replicas - 1)

    x_locals = []
    for c in range(chunks):
        local = pltpu.make_async_copy(terms_ref.at[me_r, c], parts.at[c, me_r], x_local.at[c])
        local.start()
        x_locals.append(local)
        for step in range(1, replicas):
            x_copy(c, lax.rem(me_r + step, replicas), me_r).start()

    ep_locals = []
    for c in range(chunks):
        x_locals[c].wait()
        for step in range(1, replicas):
            peer = lax.rem(me_r + step, replicas)
            x_copy(c, peer, peer).wait_recv()
        total = parts[c, 0].astype(jnp.float32)
        for source in range(1, replicas):
            total = total + parts[c, source].astype(jnp.float32)
        sums[c] = total.astype(sums.dtype)
        local = pltpu.make_async_copy(sums.at[c, me_e], out_ref.at[c, me_e], ep_local.at[c])
        local.start()
        ep_locals.append(local)

        def send(step, carry, c=c):
            ep_copy(c, lax.rem(me_e + step, groups), me_e).start()
            return carry

        lax.fori_loop(1, groups, send, 0)

    for c in range(chunks):
        for step in range(1, replicas):
            x_copy(c, lax.rem(me_r + step, replicas), me_r).wait_send()
        ep_locals[c].wait()

        def finish(step, carry, c=c):
            peer = lax.rem(me_e + step, groups)
            ep_copy(c, peer, me_e).wait_send()
            ep_copy(c, peer, peer).wait_recv()
            return carry

        lax.fori_loop(1, groups, finish, 0)


def combine_return(terms):
    replicas, chunks, groups = terms.shape[:3]
    tile = terms.shape[3:]
    return pl.pallas_call(
        _combine_kernel,
        out_shape=jax.ShapeDtypeStruct((chunks, groups) + tile, terms.dtype),
        in_specs=[pl.BlockSpec(memory_space=pl.ANY)],
        out_specs=pl.BlockSpec(memory_space=pl.ANY),
        scratch_shapes=[
            pltpu.VMEM((chunks, replicas, groups) + tile, terms.dtype),
            pltpu.VMEM((chunks, groups) + tile, terms.dtype),
            pltpu.SemaphoreType.DMA((chunks, replicas)),
            pltpu.SemaphoreType.DMA((chunks, replicas)),
            pltpu.SemaphoreType.DMA((chunks,)),
            pltpu.SemaphoreType.DMA((chunks, groups)),
            pltpu.SemaphoreType.DMA((chunks, groups)),
            pltpu.SemaphoreType.DMA((chunks,)),
        ],
        compiler_params=pltpu.CompilerParams(collective_id=3, has_side_effects=True),
    )(terms)


def rep_exchange(blocks):
    return lax.all_to_all(blocks, "rep", split_axis=0, concat_axis=0, tiled=True)


def per_device(
    residual,
    query_latent,
    query_rope,
    cache_latent,
    cache_rope,
    page_table,
    lengths,
    value_up,
    out_proj,
    routes,
    route_weight,
    placement,
    expert_gate,
    expert_up,
    expert_down,
    shared_gate,
    shared_up,
    shared_down,
    norm_gain,
):
    replicas = lax.axis_size("rep")
    expert_groups = lax.axis_size("ep")
    rep_index = lax.axis_index("rep")
    latent_out = attend_rows(
        query_latent, query_rope, cache_latent, cache_rope, page_table, lengths
    )
    own_count = latent_out.shape[0]
    swapped = lax.all_to_all(latent_out, "rep", split_axis=1, concat_axis=0, tiled=True)
    group_rows = swapped.shape[0]
    head_out = jnp.einsum(
        "thr,hrv->thv", swapped, value_up, preferred_element_type=jnp.float32
    ).astype(jnp.bfloat16)
    attn_terms = jnp.dot(
        head_out.reshape(group_rows, -1), out_proj, preferred_element_type=jnp.float32
    )
    model_width = attn_terms.shape[1]
    terms_in = rep_exchange(attn_terms.astype(jnp.bfloat16).reshape(replicas, own_count, model_width))
    attended = jnp.sum(terms_in.astype(jnp.float32), axis=0).astype(jnp.bfloat16)
    own_residual = lax.dynamic_slice_in_dim(residual, rep_index * own_count, own_count, 0)
    own_hidden = (own_residual.astype(jnp.float32) + attended.astype(jnp.float32)).astype(
        jnp.bfloat16
    )
    hidden = rep_exchange(
        jnp.broadcast_to(own_hidden[None], (replicas, own_count, model_width))
    ).reshape(group_rows, model_width)
    shared_act = (
        jax.nn.silu(jnp.dot(hidden, shared_gate, preferred_element_type=jnp.float32))
        * jnp.dot(hidden, shared_up, preferred_element_type=jnp.float32)
    ).astype(jnp.bfloat16)
    shared_terms = jnp.dot(shared_act, shared_down, preferred_element_type=jnp.float32)
    experts = placement.shape[0]
    route_count = routes.shape[1]
    assert experts == expert_groups
    capacity = max(
        replicas, min(group_rows, 2 * group_rows * route_count // experts // replicas * replicas)
    )
    share = capacity // replicas
    expert_ids = jnp.arange(experts, dtype=jnp.int32)
    slot_index = jnp.sum(jnp.where(routes[:, :, None] == expert_ids, placement, 0), axis=2).reshape(
        -1
    )
    one_hot = (slot_index[:, None] == expert_ids[None, :]).astype(jnp.int32)
    earlier = jnp.cumsum(one_hot, axis=0) - one_hot
    position = jnp.sum(earlier * one_hot, axis=1)
    assignments = slot_index.shape[0]
    source_row = (
        jnp.full((experts * capacity,), group_rows, jnp.int32)
        .at[slot_index * capacity + position]
        .set(jnp.arange(assignments, dtype=jnp.int32) // route_count)
    ).reshape(experts, capacity)
    own_source = lax.dynamic_slice_in_dim(source_row, rep_index * share, share, 1).T.reshape(-1)
    padded = jnp.concatenate([hidden, jnp.zeros((1, model_width), jnp.bfloat16)], axis=0)
    lanes = 128
    outgoing = padded[own_source].reshape(share, experts, model_width // lanes, lanes)
    gathered = dispatch(outgoing, replicas).reshape(share, replicas, expert_groups, model_width)
    gate_values = jnp.einsum(
        "cqgd,df->cqgf", gathered, expert_gate[0], preferred_element_type=jnp.float32
    )
    up_values = jnp.einsum(
        "cqgd,df->cqgf", gathered, expert_up[0], preferred_element_type=jnp.float32
    )
    activated = (jax.nn.silu(gate_values) * up_values).astype(jnp.bfloat16)
    expert_terms = jnp.einsum(
        "cqgf,fd->qcgd", activated, expert_down[0], preferred_element_type=jnp.float32
    ).astype(jnp.bfloat16)
    returned = combine_return(
        expert_terms.reshape(expert_terms.shape[:3] + (model_width // lanes, lanes))
    ).reshape(share * experts, model_width)
    local_pos = position - rep_index * share
    mine = (local_pos >= 0) & (local_pos < share)
    column = jnp.clip(local_pos, 0, share - 1) * experts + slot_index
    weight_used = jnp.where(mine, route_weight.reshape(-1), 0.0)
    combine = jnp.sum(
        jnp.where(
            column[:, None] == jnp.arange(experts * share, dtype=jnp.int32)[None, :],
            weight_used[:, None],
            0.0,
        ).reshape(group_rows, route_count, experts * share),
        axis=1,
    )
    routed = jnp.dot(
        combine, returned.astype(jnp.float32), precision=lax.Precision.HIGHEST,
        preferred_element_type=jnp.float32,
    )
    row_sums = jnp.sum(
        rep_exchange(
            (routed + shared_terms).astype(jnp.bfloat16).reshape(replicas, own_count, model_width)
        ).astype(jnp.float32),
        axis=0,
    )
    mixed = row_sums + own_hidden.astype(jnp.float32)
    inverse = lax.rsqrt(jnp.mean(mixed * mixed, axis=1, keepdims=True) + EPSILON)
    return (mixed * inverse * norm_gain).astype(jnp.bfloat16)


def solution(mesh):
    in_specs = (
        P("ep", None),
        P(("ep", "rep"), None),
        P(("ep", "rep"), None),
        P(("ep", "rep"), None, None),
        P(("ep", "rep"), None),
        P(("ep", "rep"), None),
        P(("ep", "rep")),
        P("rep", None, None),
        P("rep", None),
        P("ep", None),
        P("ep", None),
        P(),
        P("ep", None, "rep"),
        P("ep", None, "rep"),
        P("ep", "rep", None),
        P(None, "rep"),
        P(None, "rep"),
        P("rep", None),
        P(),
    )
    out_specs = P(("ep", "rep"), None)
    return jax.shard_map(
        per_device, mesh=mesh, in_specs=in_specs, out_specs=out_specs, check_vma=False
    )
```

```python
import functools
import math

import jax
import jax.numpy as jnp
from jax import lax
from jax.experimental import pallas as pl
from jax.experimental.pallas import tpu as pltpu
from jax.sharding import PartitionSpec as P

ROPE = 64
VHEAD = 128


EPSILON = 1e-06


def attend_rows(query_latent, query_rope, cache_latent, cache_rope, page_table, lengths):
    row_count, table_len = page_table.shape
    page_count, page_len, latent_width = cache_latent.shape
    rope_width = cache_rope.shape[1] // page_len
    head_count = query_rope.shape[1] // rope_width
    positions = page_count * page_len
    keys_lat = cache_latent.reshape(positions, latent_width)
    keys_rope = cache_rope.reshape(positions, rope_width)
    query_lat = query_latent.reshape(row_count, head_count, latent_width)
    query_rot = query_rope.reshape(row_count, head_count, rope_width)
    score_scale = 1.0 / math.sqrt(VHEAD + ROPE)
    scores = (
        jnp.einsum("thr,pr->thp", query_lat, keys_lat, preferred_element_type=jnp.float32)
        + jnp.einsum("thr,pr->thp", query_rot, keys_rope, preferred_element_type=jnp.float32)
    ) * score_scale
    page_hit = (
        page_table[:, :, None] == jnp.arange(page_count, dtype=jnp.int32)[None, None, :]
    ).astype(jnp.float32)
    context_pos = (
        jnp.arange(table_len, dtype=jnp.int32)[:, None] * page_len
        + jnp.arange(page_len, dtype=jnp.int32)[None, :]
    )
    live = (context_pos[None, :, :] < lengths[:, None, None]).astype(jnp.float32)
    count = jnp.einsum("tkp,tks->tps", page_hit, live).reshape(row_count, 1, positions)
    present = count > 0
    masked = jnp.where(present, scores, -jnp.inf)
    row_peak = jnp.max(masked, axis=2, keepdims=True)
    expons = jnp.where(present, jnp.exp(scores - row_peak), 0.0)
    total = jnp.sum(expons * count, axis=2, keepdims=True)
    probs = (expons / total).astype(jnp.bfloat16)
    weighted = (probs.astype(jnp.float32) * count).astype(jnp.bfloat16)
    latent_out = jnp.einsum("thp,pr->thr", weighted, keys_lat, preferred_element_type=jnp.float32)
    return latent_out.astype(jnp.bfloat16)


def _greet_all(me_e, me_r, groups, replicas):
    mesh_id = pl.DeviceIdType.MESH
    barrier = pltpu.get_barrier_semaphore()

    def greet(step, carry):
        pl.semaphore_signal(
            barrier, 1, device_id=(lax.rem(me_e + step, groups), me_r), device_id_type=mesh_id
        )
        return carry

    lax.fori_loop(1, groups, greet, 0)
    for step in range(1, replicas):
        pl.semaphore_signal(
            barrier, 1, device_id=(me_e, lax.rem(me_r + step, replicas)), device_id_type=mesh_id
        )
    pl.semaphore_wait(barrier, groups - 1 + replicas - 1)


def _dispatch_kernel(src_ref, out_ref, ep_send, ep_recv, local_sem, x_send, x_recv, f_send, f_recv):
    chunks, groups = src_ref.shape[:2]
    replicas = out_ref.shape[1]
    half = groups // 2
    me_e = lax.axis_index("ep")
    me_r = lax.axis_index("rep")
    right = lax.rem(me_r + 1, replicas)
    left = lax.rem(me_r + replicas - 1, replicas)
    across = lax.rem(me_r + 2, replicas)
    mesh_id = pl.DeviceIdType.MESH

    def ep_copy(c, peer, slot):
        return pltpu.make_async_remote_copy(
            src_ref.at[c, peer],
            out_ref.at[c, me_r, slot],
            ep_send.at[c, peer],
            ep_recv.at[c, slot],
            device_id=(peer, me_r),
            device_id_type=mesh_id,
        )

    def x_copy(c, side, slot):
        return pltpu.make_async_remote_copy(
            out_ref.at[c, slot],
            out_ref.at[c, slot],
            x_send.at[c, side],
            x_recv.at[c, side],
            device_id=(me_e, right if side == 0 else left),
            device_id_type=mesh_id,
        )

    def f_copy(c, side, slot, part):
        rows = pl.ds(part * half, half)
        return pltpu.make_async_remote_copy(
            out_ref.at[c, slot, rows],
            out_ref.at[c, slot, rows],
            f_send.at[c, side],
            f_recv.at[c, side],
            device_id=(me_e, right if side == 0 else left),
            device_id_type=mesh_id,
        )

    _greet_all(me_e, me_r, groups, replicas)

    locals_ = []
    for c in range(chunks):
        local = pltpu.make_async_copy(src_ref.at[c, me_e], out_ref.at[c, me_r, me_e], local_sem.at[c])
        local.start()
        locals_.append(local)

        def send(step, carry, c=c):
            ep_copy(c, lax.rem(me_e + step, groups), me_e).start()
            return carry

        lax.fori_loop(1, groups, send, 0)

    def forward(c):
        x_copy(c, 0, left).wait_recv()
        f_copy(c, 0, left, 1).start()
        x_copy(c, 1, right).wait_recv()
        f_copy(c, 1, right, 0).start()

    for c in range(chunks):
        locals_[c].wait()

        def arrive(step, carry, c=c):
            peer = lax.rem(me_e + step, groups)
            ep_copy(c, peer, peer).wait_recv()
            return carry

        lax.fori_loop(1, groups, arrive, 0)
        x_copy(c, 0, me_r).start()
        x_copy(c, 1, me_r).start()
        if c >= 1:
            forward(c - 1)
    forward(chunks - 1)

    for c in range(chunks):
        f_copy(c, 0, across, 1).wait_recv()
        f_copy(c, 1, across, 0).wait_recv()
        for side in range(2):
            x_copy(c, side, me_r).wait_send()
        f_copy(c, 0, left, 1).wait_send()
        f_copy(c, 1, right, 0).wait_send()

        def sent(step, carry, c=c):
            ep_copy(c, lax.rem(me_e + step, groups), me_e).wait_send()
            return carry

        lax.fori_loop(1, groups, sent, 0)


def dispatch(blocks, replicas):
    chunks, groups = blocks.shape[:2]
    out_shape = (chunks, replicas) + blocks.shape[1:]
    return pl.pallas_call(
        _dispatch_kernel,
        out_shape=jax.ShapeDtypeStruct(out_shape, blocks.dtype),
        in_specs=[pl.BlockSpec(memory_space=pl.ANY)],
        out_specs=pl.BlockSpec(memory_space=pl.ANY),
        scratch_shapes=[
            pltpu.SemaphoreType.DMA((chunks, groups)),
            pltpu.SemaphoreType.DMA((chunks, groups)),
            pltpu.SemaphoreType.DMA((chunks,)),
            pltpu.SemaphoreType.DMA((chunks, 2)),
            pltpu.SemaphoreType.DMA((chunks, 2)),
            pltpu.SemaphoreType.DMA((chunks, 2)),
            pltpu.SemaphoreType.DMA((chunks, 2)),
        ],
        compiler_params=pltpu.CompilerParams(collective_id=2, has_side_effects=True),
    )(blocks)


def _combine_kernel(
    terms_ref, out_ref, parts, transit, sums,
    x_send, x_recv, t_send, t_recv, f_send, f_recv, x_local, ep_send, ep_recv, ep_local,
):
    replicas, chunks, groups = terms_ref.shape[:3]
    half = groups // 2
    me_e = lax.axis_index("ep")
    me_r = lax.axis_index("rep")
    right = lax.rem(me_r + 1, replicas)
    left = lax.rem(me_r + replicas - 1, replicas)
    across = lax.rem(me_r + 2, replicas)
    mesh_id = pl.DeviceIdType.MESH

    def side_peer(side):
        return right if side == 0 else left

    def x_copy(c, side):
        return pltpu.make_async_remote_copy(
            terms_ref.at[side_peer(side), c],
            parts.at[c, me_r],
            x_send.at[c, side],
            x_recv.at[c, side],
            device_id=(me_e, side_peer(side)),
            device_id_type=mesh_id,
        )

    def x_wait(c, side):
        return pltpu.make_async_remote_copy(
            terms_ref.at[me_r, c],
            parts.at[c, left if side == 0 else right],
            x_send.at[c, side],
            x_recv.at[c, side],
            device_id=(me_e, side_peer(side)),
            device_id_type=mesh_id,
        )

    def t_copy(c, side):
        rows = pl.ds((1 - side) * half, half)
        return pltpu.make_async_remote_copy(
            terms_ref.at[across, c, rows],
            transit.at[c, side],
            t_send.at[c, side],
            t_recv.at[c, side],
            device_id=(me_e, side_peer(side)),
            device_id_type=mesh_id,
        )

    def f_copy(c, side, source):
        rows = pl.ds((1 - side) * half, half)
        return pltpu.make_async_remote_copy(
            transit.at[c, side],
            parts.at[c, source, rows],
            f_send.at[c, side],
            f_recv.at[c, side],
            device_id=(me_e, side_peer(side)),
            device_id_type=mesh_id,
        )

    def ep_copy(c, peer, slot):
        return pltpu.make_async_remote_copy(
            sums.at[c, peer],
            out_ref.at[c, slot],
            ep_send.at[c, peer],
            ep_recv.at[c, slot],
            device_id=(peer, me_r),
            device_id_type=mesh_id,
        )

    _greet_all(me_e, me_r, groups, replicas)

    x_locals = []
    for c in range(chunks):
        local = pltpu.make_async_copy(terms_ref.at[me_r, c], parts.at[c, me_r], x_local.at[c])
        local.start()
        x_locals.append(local)
        for side in range(2):
            t_copy(c, side).start()
            x_copy(c, side).start()

    ep_locals = []
    for c in range(chunks):
        t_copy(c, 0).wait_recv()
        f_copy(c, 0, left).start()
        t_copy(c, 1).wait_recv()
        f_copy(c, 1, right).start()
        x_locals[c].wait()
        for side in range(2):
            x_wait(c, side).wait_recv()
            f_copy(c, side, across).wait_recv()
        total = parts[c, 0].astype(jnp.float32)
        for source in range(1, replicas):
            total = total + parts[c, source].astype(jnp.float32)
        sums[c] = total.astype(sums.dtype)
        local = pltpu.make_async_copy(sums.at[c, me_e], out_ref.at[c, me_e], ep_local.at[c])
        local.start()
        ep_locals.append(local)

        def send(step, carry, c=c):
            ep_copy(c, lax.rem(me_e + step, groups), me_e).start()
            return carry

        lax.fori_loop(1, groups, send, 0)

    for c in range(chunks):
        for side in range(2):
            x_copy(c, side).wait_send()
            t_copy(c, side).wait_send()
        f_copy(c, 0, left).wait_send()
        f_copy(c, 1, right).wait_send()
        ep_locals[c].wait()

        def finish(step, carry, c=c):
            peer = lax.rem(me_e + step, groups)
            ep_copy(c, peer, me_e).wait_send()
            ep_copy(c, peer, peer).wait_recv()
            return carry

        lax.fori_loop(1, groups, finish, 0)


def combine_return(terms):
    replicas, chunks, groups = terms.shape[:3]
    tile = terms.shape[3:]
    return pl.pallas_call(
        _combine_kernel,
        out_shape=jax.ShapeDtypeStruct((chunks, groups) + tile, terms.dtype),
        in_specs=[pl.BlockSpec(memory_space=pl.ANY)],
        out_specs=pl.BlockSpec(memory_space=pl.ANY),
        scratch_shapes=[
            pltpu.VMEM((chunks, replicas, groups) + tile, terms.dtype),
            pltpu.VMEM((chunks, 2, groups // 2) + tile, terms.dtype),
            pltpu.VMEM((chunks, groups) + tile, terms.dtype),
        ]
        + [pltpu.SemaphoreType.DMA((chunks, 2))] * 6
        + [
            pltpu.SemaphoreType.DMA((chunks,)),
            pltpu.SemaphoreType.DMA((chunks, groups)),
            pltpu.SemaphoreType.DMA((chunks, groups)),
            pltpu.SemaphoreType.DMA((chunks,)),
        ],
        compiler_params=pltpu.CompilerParams(collective_id=3, has_side_effects=True),
    )(terms)


def rep_exchange(blocks):
    return lax.all_to_all(blocks, "rep", split_axis=0, concat_axis=0, tiled=True)


def per_device(
    residual,
    query_latent,
    query_rope,
    cache_latent,
    cache_rope,
    page_table,
    lengths,
    value_up,
    out_proj,
    routes,
    route_weight,
    placement,
    expert_gate,
    expert_up,
    expert_down,
    shared_gate,
    shared_up,
    shared_down,
    norm_gain,
):
    replicas = lax.axis_size("rep")
    expert_groups = lax.axis_size("ep")
    rep_index = lax.axis_index("rep")
    latent_out = attend_rows(
        query_latent, query_rope, cache_latent, cache_rope, page_table, lengths
    )
    own_count = latent_out.shape[0]
    swapped = lax.all_to_all(latent_out, "rep", split_axis=1, concat_axis=0, tiled=True)
    group_rows = swapped.shape[0]
    head_out = jnp.einsum(
        "thr,hrv->thv", swapped, value_up, preferred_element_type=jnp.float32
    ).astype(jnp.bfloat16)
    attn_terms = jnp.dot(
        head_out.reshape(group_rows, -1), out_proj, preferred_element_type=jnp.float32
    )
    model_width = attn_terms.shape[1]
    terms_in = rep_exchange(attn_terms.astype(jnp.bfloat16).reshape(replicas, own_count, model_width))
    attended = jnp.sum(terms_in.astype(jnp.float32), axis=0).astype(jnp.bfloat16)
    own_residual = lax.dynamic_slice_in_dim(residual, rep_index * own_count, own_count, 0)
    own_hidden = (own_residual.astype(jnp.float32) + attended.astype(jnp.float32)).astype(
        jnp.bfloat16
    )
    hidden = rep_exchange(
        jnp.broadcast_to(own_hidden[None], (replicas, own_count, model_width))
    ).reshape(group_rows, model_width)
    shared_act = (
        jax.nn.silu(jnp.dot(hidden, shared_gate, preferred_element_type=jnp.float32))
        * jnp.dot(hidden, shared_up, preferred_element_type=jnp.float32)
    ).astype(jnp.bfloat16)
    shared_terms = jnp.dot(shared_act, shared_down, preferred_element_type=jnp.float32)
    experts = placement.shape[0]
    route_count = routes.shape[1]
    assert experts == expert_groups and replicas == 4
    capacity = max(
        replicas, min(group_rows, 2 * group_rows * route_count // experts // replicas * replicas)
    )
    share = capacity // replicas
    expert_ids = jnp.arange(experts, dtype=jnp.int32)
    slot_index = jnp.sum(jnp.where(routes[:, :, None] == expert_ids, placement, 0), axis=2).reshape(
        -1
    )
    one_hot = (slot_index[:, None] == expert_ids[None, :]).astype(jnp.int32)
    earlier = jnp.cumsum(one_hot, axis=0) - one_hot
    position = jnp.sum(earlier * one_hot, axis=1)
    assignments = slot_index.shape[0]
    source_row = (
        jnp.full((experts * capacity,), group_rows, jnp.int32)
        .at[slot_index * capacity + position]
        .set(jnp.arange(assignments, dtype=jnp.int32) // route_count)
    ).reshape(experts, capacity)
    own_source = lax.dynamic_slice_in_dim(source_row, rep_index * share, share, 1).T.reshape(-1)
    padded = jnp.concatenate([hidden, jnp.zeros((1, model_width), jnp.bfloat16)], axis=0)
    lanes = 128
    outgoing = padded[own_source].reshape(share, experts, model_width // lanes, lanes)
    gathered = dispatch(outgoing, replicas).reshape(share, replicas, expert_groups, model_width)
    gate_values = jnp.einsum(
        "cqgd,df->cqgf", gathered, expert_gate[0], preferred_element_type=jnp.float32
    )
    up_values = jnp.einsum(
        "cqgd,df->cqgf", gathered, expert_up[0], preferred_element_type=jnp.float32
    )
    activated = (jax.nn.silu(gate_values) * up_values).astype(jnp.bfloat16)
    expert_terms = jnp.einsum(
        "cqgf,fd->qcgd", activated, expert_down[0], preferred_element_type=jnp.float32
    ).astype(jnp.bfloat16)
    returned = combine_return(
        expert_terms.reshape(expert_terms.shape[:3] + (model_width // lanes, lanes))
    ).reshape(share * experts, model_width)
    local_pos = position - rep_index * share
    mine = (local_pos >= 0) & (local_pos < share)
    column = jnp.clip(local_pos, 0, share - 1) * experts + slot_index
    weight_used = jnp.where(mine, route_weight.reshape(-1), 0.0)
    combine = jnp.sum(
        jnp.where(
            column[:, None] == jnp.arange(experts * share, dtype=jnp.int32)[None, :],
            weight_used[:, None],
            0.0,
        ).reshape(group_rows, route_count, experts * share),
        axis=1,
    )
    routed = jnp.dot(
        combine, returned.astype(jnp.float32), precision=lax.Precision.HIGHEST,
        preferred_element_type=jnp.float32,
    )
    row_sums = jnp.sum(
        rep_exchange(
            (routed + shared_terms).astype(jnp.bfloat16).reshape(replicas, own_count, model_width)
        ).astype(jnp.float32),
        axis=0,
    )
    mixed = row_sums + own_hidden.astype(jnp.float32)
    inverse = lax.rsqrt(jnp.mean(mixed * mixed, axis=1, keepdims=True) + EPSILON)
    return (mixed * inverse * norm_gain).astype(jnp.bfloat16)


def solution(mesh):
    in_specs = (
        P("ep", None),
        P(("ep", "rep"), None),
        P(("ep", "rep"), None),
        P(("ep", "rep"), None, None),
        P(("ep", "rep"), None),
        P(("ep", "rep"), None),
        P(("ep", "rep")),
        P("rep", None, None),
        P("rep", None),
        P("ep", None),
        P("ep", None),
        P(),
        P("ep", None, "rep"),
        P("ep", None, "rep"),
        P("ep", "rep", None),
        P(None, "rep"),
        P(None, "rep"),
        P("rep", None),
        P(),
    )
    out_specs = P(("ep", "rep"), None)
    return jax.shard_map(
        per_device, mesh=mesh, in_specs=in_specs, out_specs=out_specs, check_vma=False
    )
```

```python
import functools
import math

import jax
import jax.numpy as jnp
from jax import lax
from jax.experimental import pallas as pl
from jax.experimental.pallas import tpu as pltpu
from jax.sharding import PartitionSpec as P

ROPE = 64
VHEAD = 128


EPSILON = 1e-06


def attend_rows(query_latent, query_rope, cache_latent, cache_rope, page_table, lengths):
    row_count, table_len = page_table.shape
    page_count, page_len, latent_width = cache_latent.shape
    rope_width = cache_rope.shape[1] // page_len
    head_count = query_rope.shape[1] // rope_width
    positions = page_count * page_len
    keys_lat = cache_latent.reshape(positions, latent_width)
    keys_rope = cache_rope.reshape(positions, rope_width)
    query_lat = query_latent.reshape(row_count, head_count, latent_width)
    query_rot = query_rope.reshape(row_count, head_count, rope_width)
    score_scale = 1.0 / math.sqrt(VHEAD + ROPE)
    scores = (
        jnp.einsum("thr,pr->thp", query_lat, keys_lat, preferred_element_type=jnp.float32)
        + jnp.einsum("thr,pr->thp", query_rot, keys_rope, preferred_element_type=jnp.float32)
    ) * score_scale
    page_hit = (
        page_table[:, :, None] == jnp.arange(page_count, dtype=jnp.int32)[None, None, :]
    ).astype(jnp.float32)
    context_pos = (
        jnp.arange(table_len, dtype=jnp.int32)[:, None] * page_len
        + jnp.arange(page_len, dtype=jnp.int32)[None, :]
    )
    live = (context_pos[None, :, :] < lengths[:, None, None]).astype(jnp.float32)
    count = jnp.einsum("tkp,tks->tps", page_hit, live).reshape(row_count, 1, positions)
    present = count > 0
    masked = jnp.where(present, scores, -jnp.inf)
    row_peak = jnp.max(masked, axis=2, keepdims=True)
    expons = jnp.where(present, jnp.exp(scores - row_peak), 0.0)
    total = jnp.sum(expons * count, axis=2, keepdims=True)
    probs = (expons / total).astype(jnp.bfloat16)
    weighted = (probs.astype(jnp.float32) * count).astype(jnp.bfloat16)
    latent_out = jnp.einsum("thp,pr->thr", weighted, keys_lat, preferred_element_type=jnp.float32)
    return latent_out.astype(jnp.bfloat16)


def _greet_all(me_e, me_r, groups, replicas):
    mesh_id = pl.DeviceIdType.MESH
    barrier = pltpu.get_barrier_semaphore()

    def greet(step, carry):
        pl.semaphore_signal(
            barrier, 1, device_id=(lax.rem(me_e + step, groups), me_r), device_id_type=mesh_id
        )
        return carry

    lax.fori_loop(1, groups, greet, 0)
    for step in range(1, replicas):
        pl.semaphore_signal(
            barrier, 1, device_id=(me_e, lax.rem(me_r + step, replicas)), device_id_type=mesh_id
        )
    pl.semaphore_wait(barrier, groups - 1 + replicas - 1)


def _dispatch_kernel(src_ref, out_ref, ep_send, ep_recv, local_sem, x_send, x_recv, f_send, f_recv):
    chunks, groups = src_ref.shape[:2]
    replicas = out_ref.shape[1]
    half = groups // 2
    me_e = lax.axis_index("ep")
    me_r = lax.axis_index("rep")
    right = lax.rem(me_r + 1, replicas)
    left = lax.rem(me_r + replicas - 1, replicas)
    across = lax.rem(me_r + 2, replicas)
    mesh_id = pl.DeviceIdType.MESH

    def ep_copy(c, peer, slot):
        return pltpu.make_async_remote_copy(
            src_ref.at[c, peer],
            out_ref.at[c, me_r, slot],
            ep_send.at[c, peer],
            ep_recv.at[c, slot],
            device_id=(peer, me_r),
            device_id_type=mesh_id,
        )

    def x_copy(c, side, slot):
        return pltpu.make_async_remote_copy(
            out_ref.at[c, slot],
            out_ref.at[c, slot],
            x_send.at[c, side],
            x_recv.at[c, side],
            device_id=(me_e, right if side == 0 else left),
            device_id_type=mesh_id,
        )

    def f_copy(c, side, slot, part):
        rows = pl.ds(part * half, half)
        return pltpu.make_async_remote_copy(
            out_ref.at[c, slot, rows],
            out_ref.at[c, slot, rows],
            f_send.at[c, side],
            f_recv.at[c, side],
            device_id=(me_e, right if side == 0 else left),
            device_id_type=mesh_id,
        )

    _greet_all(me_e, me_r, groups, replicas)

    locals_ = []
    for c in range(chunks):
        local = pltpu.make_async_copy(src_ref.at[c, me_e], out_ref.at[c, me_r, me_e], local_sem.at[c])
        local.start()
        locals_.append(local)

        def send(step, carry, c=c):
            ep_copy(c, lax.rem(me_e + step, groups), me_e).start()
            return carry

        lax.fori_loop(1, groups, send, 0)

    def forward(c):
        x_copy(c, 0, left).wait_recv()
        f_copy(c, 0, left, 1).start()
        x_copy(c, 1, right).wait_recv()
        f_copy(c, 1, right, 0).start()

    for c in range(chunks):
        locals_[c].wait()

        def arrive(step, carry, c=c):
            peer = lax.rem(me_e + step, groups)
            ep_copy(c, peer, peer).wait_recv()
            return carry

        lax.fori_loop(1, groups, arrive, 0)
        x_copy(c, 0, me_r).start()
        x_copy(c, 1, me_r).start()
        if c >= 1:
            forward(c - 1)
    forward(chunks - 1)

    for c in range(chunks):
        f_copy(c, 0, across, 1).wait_recv()
        f_copy(c, 1, across, 0).wait_recv()
        for side in range(2):
            x_copy(c, side, me_r).wait_send()
        f_copy(c, 0, left, 1).wait_send()
        f_copy(c, 1, right, 0).wait_send()

        def sent(step, carry, c=c):
            ep_copy(c, lax.rem(me_e + step, groups), me_e).wait_send()
            return carry

        lax.fori_loop(1, groups, sent, 0)


def dispatch(blocks, replicas):
    chunks, groups = blocks.shape[:2]
    out_shape = (chunks, replicas) + blocks.shape[1:]
    return pl.pallas_call(
        _dispatch_kernel,
        out_shape=jax.ShapeDtypeStruct(out_shape, blocks.dtype),
        in_specs=[pl.BlockSpec(memory_space=pl.ANY)],
        out_specs=pl.BlockSpec(memory_space=pl.ANY),
        scratch_shapes=[
            pltpu.SemaphoreType.DMA((chunks, groups)),
            pltpu.SemaphoreType.DMA((chunks, groups)),
            pltpu.SemaphoreType.DMA((chunks,)),
            pltpu.SemaphoreType.DMA((chunks, 2)),
            pltpu.SemaphoreType.DMA((chunks, 2)),
            pltpu.SemaphoreType.DMA((chunks, 2)),
            pltpu.SemaphoreType.DMA((chunks, 2)),
        ],
        compiler_params=pltpu.CompilerParams(collective_id=2, has_side_effects=True),
    )(blocks)


def _combine_kernel(terms_ref, out_ref, parts, sums, x_send, x_recv, x_local, ep_send, ep_recv, ep_local):
    replicas, chunks, groups = terms_ref.shape[:3]
    me_e = lax.axis_index("ep")
    me_r = lax.axis_index("rep")
    mesh_id = pl.DeviceIdType.MESH

    def x_copy(c, peer, slot):
        return pltpu.make_async_remote_copy(
            terms_ref.at[peer, c],
            parts.at[c, slot],
            x_send.at[c, peer],
            x_recv.at[c, slot],
            device_id=(me_e, peer),
            device_id_type=mesh_id,
        )

    def ep_copy(c, peer, slot):
        return pltpu.make_async_remote_copy(
            sums.at[c, peer],
            out_ref.at[c, slot],
            ep_send.at[c, peer],
            ep_recv.at[c, slot],
            device_id=(peer, me_r),
            device_id_type=mesh_id,
        )

    barrier = pltpu.get_barrier_semaphore()

    def greet(step, carry):
        pl.semaphore_signal(
            barrier, 1, device_id=(lax.rem(me_e + step, groups), me_r), device_id_type=mesh_id
        )
        return carry

    lax.fori_loop(1, groups, greet, 0)
    for step in range(1, replicas):
        pl.semaphore_signal(
            barrier, 1, device_id=(me_e, lax.rem(me_r + step, replicas)), device_id_type=mesh_id
        )
    pl.semaphore_wait(barrier, groups - 1 + replicas - 1)

    x_locals = []
    for c in range(chunks):
        local = pltpu.make_async_copy(terms_ref.at[me_r, c], parts.at[c, me_r], x_local.at[c])
        local.start()
        x_locals.append(local)
        for step in range(1, replicas):
            x_copy(c, lax.rem(me_r + step, replicas), me_r).start()

    ep_locals = []
    for c in range(chunks):
        x_locals[c].wait()
        for step in range(1, replicas):
            peer = lax.rem(me_r + step, replicas)
            x_copy(c, peer, peer).wait_recv()
        total = parts[c, 0].astype(jnp.float32)
        for source in range(1, replicas):
            total = total + parts[c, source].astype(jnp.float32)
        sums[c] = total.astype(sums.dtype)
        local = pltpu.make_async_copy(sums.at[c, me_e], out_ref.at[c, me_e], ep_local.at[c])
        local.start()
        ep_locals.append(local)

        def send(step, carry, c=c):
            ep_copy(c, lax.rem(me_e + step, groups), me_e).start()
            return carry

        lax.fori_loop(1, groups, send, 0)

    for c in range(chunks):
        for step in range(1, replicas):
            x_copy(c, lax.rem(me_r + step, replicas), me_r).wait_send()
        ep_locals[c].wait()

        def finish(step, carry, c=c):
            peer = lax.rem(me_e + step, groups)
            ep_copy(c, peer, me_e).wait_send()
            ep_copy(c, peer, peer).wait_recv()
            return carry

        lax.fori_loop(1, groups, finish, 0)


def combine_return(terms):
    replicas, chunks, groups = terms.shape[:3]
    tile = terms.shape[3:]
    return pl.pallas_call(
        _combine_kernel,
        out_shape=jax.ShapeDtypeStruct((chunks, groups) + tile, terms.dtype),
        in_specs=[pl.BlockSpec(memory_space=pl.ANY)],
        out_specs=pl.BlockSpec(memory_space=pl.ANY),
        scratch_shapes=[
            pltpu.VMEM((chunks, replicas, groups) + tile, terms.dtype),
            pltpu.VMEM((chunks, groups) + tile, terms.dtype),
            pltpu.SemaphoreType.DMA((chunks, replicas)),
            pltpu.SemaphoreType.DMA((chunks, replicas)),
            pltpu.SemaphoreType.DMA((chunks,)),
            pltpu.SemaphoreType.DMA((chunks, groups)),
            pltpu.SemaphoreType.DMA((chunks, groups)),
            pltpu.SemaphoreType.DMA((chunks,)),
        ],
        compiler_params=pltpu.CompilerParams(collective_id=3, has_side_effects=True),
    )(terms)


def rep_exchange(blocks):
    return lax.all_to_all(blocks, "rep", split_axis=0, concat_axis=0, tiled=True)


def per_device(
    residual,
    query_latent,
    query_rope,
    cache_latent,
    cache_rope,
    page_table,
    lengths,
    value_up,
    out_proj,
    routes,
    route_weight,
    placement,
    expert_gate,
    expert_up,
    expert_down,
    shared_gate,
    shared_up,
    shared_down,
    norm_gain,
):
    replicas = lax.axis_size("rep")
    expert_groups = lax.axis_size("ep")
    rep_index = lax.axis_index("rep")
    latent_out = attend_rows(
        query_latent, query_rope, cache_latent, cache_rope, page_table, lengths
    )
    own_count = latent_out.shape[0]
    swapped = lax.all_to_all(latent_out, "rep", split_axis=1, concat_axis=0, tiled=True)
    group_rows = swapped.shape[0]
    head_out = jnp.einsum(
        "thr,hrv->thv", swapped, value_up, preferred_element_type=jnp.float32
    ).astype(jnp.bfloat16)
    attn_terms = jnp.dot(
        head_out.reshape(group_rows, -1), out_proj, preferred_element_type=jnp.float32
    )
    model_width = attn_terms.shape[1]
    terms_in = rep_exchange(attn_terms.astype(jnp.bfloat16).reshape(replicas, own_count, model_width))
    attended = jnp.sum(terms_in.astype(jnp.float32), axis=0).astype(jnp.bfloat16)
    own_residual = lax.dynamic_slice_in_dim(residual, rep_index * own_count, own_count, 0)
    own_hidden = (own_residual.astype(jnp.float32) + attended.astype(jnp.float32)).astype(
        jnp.bfloat16
    )
    hidden = rep_exchange(
        jnp.broadcast_to(own_hidden[None], (replicas, own_count, model_width))
    ).reshape(group_rows, model_width)
    shared_act = (
        jax.nn.silu(jnp.dot(hidden, shared_gate, preferred_element_type=jnp.float32))
        * jnp.dot(hidden, shared_up, preferred_element_type=jnp.float32)
    ).astype(jnp.bfloat16)
    shared_terms = jnp.dot(shared_act, shared_down, preferred_element_type=jnp.float32)
    experts = placement.shape[0]
    route_count = routes.shape[1]
    assert experts == expert_groups and replicas == 4
    capacity = max(
        replicas, min(group_rows, 2 * group_rows * route_count // experts // replicas * replicas)
    )
    share = capacity // replicas
    expert_ids = jnp.arange(experts, dtype=jnp.int32)
    slot_index = jnp.sum(jnp.where(routes[:, :, None] == expert_ids, placement, 0), axis=2).reshape(
        -1
    )
    one_hot = (slot_index[:, None] == expert_ids[None, :]).astype(jnp.int32)
    earlier = jnp.cumsum(one_hot, axis=0) - one_hot
    position = jnp.sum(earlier * one_hot, axis=1)
    assignments = slot_index.shape[0]
    source_row = (
        jnp.full((experts * capacity,), group_rows, jnp.int32)
        .at[slot_index * capacity + position]
        .set(jnp.arange(assignments, dtype=jnp.int32) // route_count)
    ).reshape(experts, capacity)
    own_source = lax.dynamic_slice_in_dim(source_row, rep_index * share, share, 1).T.reshape(-1)
    padded = jnp.concatenate([hidden, jnp.zeros((1, model_width), jnp.bfloat16)], axis=0)
    lanes = 128
    outgoing = padded[own_source].reshape(share, experts, model_width // lanes, lanes)
    gathered = dispatch(outgoing, replicas).reshape(share, replicas, expert_groups, model_width)
    gate_values = jnp.einsum(
        "cqgd,df->cqgf", gathered, expert_gate[0], preferred_element_type=jnp.float32
    )
    up_values = jnp.einsum(
        "cqgd,df->cqgf", gathered, expert_up[0], preferred_element_type=jnp.float32
    )
    activated = (jax.nn.silu(gate_values) * up_values).astype(jnp.bfloat16)
    expert_terms = jnp.einsum(
        "cqgf,fd->qcgd", activated, expert_down[0], preferred_element_type=jnp.float32
    ).astype(jnp.bfloat16)
    returned = combine_return(
        expert_terms.reshape(expert_terms.shape[:3] + (model_width // lanes, lanes))
    ).reshape(share * experts, model_width)
    local_pos = position - rep_index * share
    mine = (local_pos >= 0) & (local_pos < share)
    column = jnp.clip(local_pos, 0, share - 1) * experts + slot_index
    weight_used = jnp.where(mine, route_weight.reshape(-1), 0.0)
    combine = jnp.sum(
        jnp.where(
            column[:, None] == jnp.arange(experts * share, dtype=jnp.int32)[None, :],
            weight_used[:, None],
            0.0,
        ).reshape(group_rows, route_count, experts * share),
        axis=1,
    )
    routed = jnp.dot(
        combine, returned.astype(jnp.float32), precision=lax.Precision.HIGHEST,
        preferred_element_type=jnp.float32,
    )
    row_sums = jnp.sum(
        rep_exchange(
            (routed + shared_terms).astype(jnp.bfloat16).reshape(replicas, own_count, model_width)
        ).astype(jnp.float32),
        axis=0,
    )
    mixed = row_sums + own_hidden.astype(jnp.float32)
    inverse = lax.rsqrt(jnp.mean(mixed * mixed, axis=1, keepdims=True) + EPSILON)
    return (mixed * inverse * norm_gain).astype(jnp.bfloat16)


def solution(mesh):
    in_specs = (
        P("ep", None),
        P(("ep", "rep"), None),
        P(("ep", "rep"), None),
        P(("ep", "rep"), None, None),
        P(("ep", "rep"), None),
        P(("ep", "rep"), None),
        P(("ep", "rep")),
        P("rep", None, None),
        P("rep", None),
        P("ep", None),
        P("ep", None),
        P(),
        P("ep", None, "rep"),
        P("ep", None, "rep"),
        P("ep", "rep", None),
        P(None, "rep"),
        P(None, "rep"),
        P("rep", None),
        P(),
    )
    out_specs = P(("ep", "rep"), None)
    return jax.shard_map(
        per_device, mesh=mesh, in_specs=in_specs, out_specs=out_specs, check_vma=False
    )
```

```python
import functools
import math

import jax
import jax.numpy as jnp
from jax import lax
from jax.experimental import pallas as pl
from jax.experimental.pallas import tpu as pltpu
from jax.sharding import PartitionSpec as P

ROPE = 64
VHEAD = 128


EPSILON = 1e-06


def attend_rows(query_latent, query_rope, cache_latent, cache_rope, page_table, lengths):
    row_count, table_len = page_table.shape
    page_count, page_len, latent_width = cache_latent.shape
    rope_width = cache_rope.shape[1] // page_len
    head_count = query_rope.shape[1] // rope_width
    positions = page_count * page_len
    keys_lat = cache_latent.reshape(positions, latent_width)
    keys_rope = cache_rope.reshape(positions, rope_width)
    query_lat = query_latent.reshape(row_count, head_count, latent_width)
    query_rot = query_rope.reshape(row_count, head_count, rope_width)
    score_scale = 1.0 / math.sqrt(VHEAD + ROPE)
    scores = (
        jnp.einsum("thr,pr->thp", query_lat, keys_lat, preferred_element_type=jnp.float32)
        + jnp.einsum("thr,pr->thp", query_rot, keys_rope, preferred_element_type=jnp.float32)
    ) * score_scale
    page_hit = (
        page_table[:, :, None] == jnp.arange(page_count, dtype=jnp.int32)[None, None, :]
    ).astype(jnp.float32)
    context_pos = (
        jnp.arange(table_len, dtype=jnp.int32)[:, None] * page_len
        + jnp.arange(page_len, dtype=jnp.int32)[None, :]
    )
    live = (context_pos[None, :, :] < lengths[:, None, None]).astype(jnp.float32)
    count = jnp.einsum("tkp,tks->tps", page_hit, live).reshape(row_count, 1, positions)
    present = count > 0
    masked = jnp.where(present, scores, -jnp.inf)
    row_peak = jnp.max(masked, axis=2, keepdims=True)
    expons = jnp.where(present, jnp.exp(scores - row_peak), 0.0)
    total = jnp.sum(expons * count, axis=2, keepdims=True)
    probs = (expons / total).astype(jnp.bfloat16)
    weighted = (probs.astype(jnp.float32) * count).astype(jnp.bfloat16)
    latent_out = jnp.einsum("thp,pr->thr", weighted, keys_lat, preferred_element_type=jnp.float32)
    return latent_out.astype(jnp.bfloat16)


def _greet_all(me_e, me_r, groups, replicas):
    mesh_id = pl.DeviceIdType.MESH
    barrier = pltpu.get_barrier_semaphore()

    def greet(step, carry):
        pl.semaphore_signal(
            barrier, 1, device_id=(lax.rem(me_e + step, groups), me_r), device_id_type=mesh_id
        )
        return carry

    lax.fori_loop(1, groups, greet, 0)
    for step in range(1, replicas):
        pl.semaphore_signal(
            barrier, 1, device_id=(me_e, lax.rem(me_r + step, replicas)), device_id_type=mesh_id
        )
    pl.semaphore_wait(barrier, groups - 1 + replicas - 1)


def _dispatch_kernel(src_ref, out_ref, ep_send, ep_recv, local_sem, x_send, x_recv, f_send, f_recv):
    chunks, groups = src_ref.shape[:2]
    replicas = out_ref.shape[1]
    half = groups // 2
    me_e = lax.axis_index("ep")
    me_r = lax.axis_index("rep")
    right = lax.rem(me_r + 1, replicas)
    left = lax.rem(me_r + replicas - 1, replicas)
    across = lax.rem(me_r + 2, replicas)
    mesh_id = pl.DeviceIdType.MESH

    def ep_copy(c, peer, slot):
        return pltpu.make_async_remote_copy(
            src_ref.at[c, peer],
            out_ref.at[c, me_r, slot],
            ep_send.at[c, peer],
            ep_recv.at[c, slot],
            device_id=(peer, me_r),
            device_id_type=mesh_id,
        )

    def x_copy(c, side, slot):
        return pltpu.make_async_remote_copy(
            out_ref.at[c, slot],
            out_ref.at[c, slot],
            x_send.at[c, side],
            x_recv.at[c, side],
            device_id=(me_e, right if side == 0 else left),
            device_id_type=mesh_id,
        )

    def f_copy(c, side, slot, part):
        rows = pl.ds(part * half, half)
        return pltpu.make_async_remote_copy(
            out_ref.at[c, slot, rows],
            out_ref.at[c, slot, rows],
            f_send.at[c, side],
            f_recv.at[c, side],
            device_id=(me_e, right if side == 0 else left),
            device_id_type=mesh_id,
        )

    _greet_all(me_e, me_r, groups, replicas)

    locals_ = []
    for c in range(chunks):
        local = pltpu.make_async_copy(src_ref.at[c, me_e], out_ref.at[c, me_r, me_e], local_sem.at[c])
        local.start()
        locals_.append(local)

        def send(step, carry, c=c):
            ep_copy(c, lax.rem(me_e + step, groups), me_e).start()
            return carry

        lax.fori_loop(1, groups, send, 0)

    def forward(c):
        x_copy(c, 0, left).wait_recv()
        f_copy(c, 0, left, 1).start()
        x_copy(c, 1, right).wait_recv()
        f_copy(c, 1, right, 0).start()

    for c in range(chunks):
        locals_[c].wait()

        def arrive(step, carry, c=c):
            peer = lax.rem(me_e + step, groups)
            ep_copy(c, peer, peer).wait_recv()
            return carry

        lax.fori_loop(1, groups, arrive, 0)
        x_copy(c, 0, me_r).start()
        x_copy(c, 1, me_r).start()
        if c >= 1:
            forward(c - 1)
    forward(chunks - 1)

    for c in range(chunks):
        f_copy(c, 0, across, 1).wait_recv()
        f_copy(c, 1, across, 0).wait_recv()
        for side in range(2):
            x_copy(c, side, me_r).wait_send()
        f_copy(c, 0, left, 1).wait_send()
        f_copy(c, 1, right, 0).wait_send()

        def sent(step, carry, c=c):
            ep_copy(c, lax.rem(me_e + step, groups), me_e).wait_send()
            return carry

        lax.fori_loop(1, groups, sent, 0)


def dispatch(blocks, replicas):
    chunks, groups = blocks.shape[:2]
    out_shape = (chunks, replicas) + blocks.shape[1:]
    return pl.pallas_call(
        _dispatch_kernel,
        out_shape=jax.ShapeDtypeStruct(out_shape, blocks.dtype),
        in_specs=[pl.BlockSpec(memory_space=pl.ANY)],
        out_specs=pl.BlockSpec(memory_space=pl.ANY),
        scratch_shapes=[
            pltpu.SemaphoreType.DMA((chunks, groups)),
            pltpu.SemaphoreType.DMA((chunks, groups)),
            pltpu.SemaphoreType.DMA((chunks,)),
            pltpu.SemaphoreType.DMA((chunks, 2)),
            pltpu.SemaphoreType.DMA((chunks, 2)),
            pltpu.SemaphoreType.DMA((chunks, 2)),
            pltpu.SemaphoreType.DMA((chunks, 2)),
        ],
        compiler_params=pltpu.CompilerParams(collective_id=2, has_side_effects=True),
    )(blocks)


def _combine_kernel(terms_ref, out_ref, parts, sums, x_send, x_recv, x_local, ep_send, ep_recv, ep_local):
    replicas, chunks, groups = terms_ref.shape[:3]
    me_e = lax.axis_index("ep")
    me_r = lax.axis_index("rep")
    mesh_id = pl.DeviceIdType.MESH

    def x_copy(c, peer, slot):
        return pltpu.make_async_remote_copy(
            terms_ref.at[peer, c],
            parts.at[c, slot],
            x_send.at[c, peer],
            x_recv.at[c, slot],
            device_id=(me_e, peer),
            device_id_type=mesh_id,
        )

    def ep_copy(c, peer, slot):
        return pltpu.make_async_remote_copy(
            sums.at[c, peer],
            out_ref.at[c, slot],
            ep_send.at[c, peer],
            ep_recv.at[c, slot],
            device_id=(peer, me_r),
            device_id_type=mesh_id,
        )

    barrier = pltpu.get_barrier_semaphore()

    def greet(step, carry):
        pl.semaphore_signal(
            barrier, 1, device_id=(lax.rem(me_e + step, groups), me_r), device_id_type=mesh_id
        )
        return carry

    lax.fori_loop(1, groups, greet, 0)
    for step in range(1, replicas):
        pl.semaphore_signal(
            barrier, 1, device_id=(me_e, lax.rem(me_r + step, replicas)), device_id_type=mesh_id
        )
    pl.semaphore_wait(barrier, groups - 1 + replicas - 1)

    x_locals = []
    for c in range(chunks):
        local = pltpu.make_async_copy(terms_ref.at[me_r, c], parts.at[c, me_r], x_local.at[c])
        local.start()
        x_locals.append(local)
        for step in range(1, replicas):
            x_copy(c, lax.rem(me_r + step, replicas), me_r).start()

    ep_locals = []
    for c in range(chunks):
        x_locals[c].wait()
        for step in range(1, replicas):
            peer = lax.rem(me_r + step, replicas)
            x_copy(c, peer, peer).wait_recv()
        total = parts[c, 0].astype(jnp.float32)
        for source in range(1, replicas):
            total = total + parts[c, source].astype(jnp.float32)
        sums[c] = total.astype(sums.dtype)
        local = pltpu.make_async_copy(sums.at[c, me_e], out_ref.at[c, me_e], ep_local.at[c])
        local.start()
        ep_locals.append(local)

        def send(step, carry, c=c):
            ep_copy(c, lax.rem(me_e + step, groups), me_e).start()
            return carry

        lax.fori_loop(1, groups, send, 0)

    for c in range(chunks):
        for step in range(1, replicas):
            x_copy(c, lax.rem(me_r + step, replicas), me_r).wait_send()
        ep_locals[c].wait()

        def finish(step, carry, c=c):
            peer = lax.rem(me_e + step, groups)
            ep_copy(c, peer, me_e).wait_send()
            ep_copy(c, peer, peer).wait_recv()
            return carry

        lax.fori_loop(1, groups, finish, 0)


def combine_return(terms):
    replicas, chunks, groups = terms.shape[:3]
    tile = terms.shape[3:]
    return pl.pallas_call(
        _combine_kernel,
        out_shape=jax.ShapeDtypeStruct((chunks, groups) + tile, terms.dtype),
        in_specs=[pl.BlockSpec(memory_space=pl.ANY)],
        out_specs=pl.BlockSpec(memory_space=pl.ANY),
        scratch_shapes=[
            pltpu.VMEM((chunks, replicas, groups) + tile, terms.dtype),
            pltpu.VMEM((chunks, groups) + tile, terms.dtype),
            pltpu.SemaphoreType.DMA((chunks, replicas)),
            pltpu.SemaphoreType.DMA((chunks, replicas)),
            pltpu.SemaphoreType.DMA((chunks,)),
            pltpu.SemaphoreType.DMA((chunks, groups)),
            pltpu.SemaphoreType.DMA((chunks, groups)),
            pltpu.SemaphoreType.DMA((chunks,)),
        ],
        compiler_params=pltpu.CompilerParams(collective_id=3, has_side_effects=True),
    )(terms)


def _hidden_kernel(terms_ref, resid_ref, out_ref, parts, own, t_send, t_recv, t_local, h_send, h_recv, h_local):
    replicas = terms_ref.shape[0]
    me_e = lax.axis_index("ep")
    me_r = lax.axis_index("rep")
    mesh_id = pl.DeviceIdType.MESH

    def t_copy(peer, slot):
        return pltpu.make_async_remote_copy(
            terms_ref.at[peer],
            parts.at[slot],
            t_send.at[peer],
            t_recv.at[slot],
            device_id=(me_e, peer),
            device_id_type=mesh_id,
        )

    def h_copy(peer, slot):
        return pltpu.make_async_remote_copy(
            own,
            out_ref.at[slot],
            h_send.at[peer],
            h_recv.at[slot],
            device_id=(me_e, peer),
            device_id_type=mesh_id,
        )

    barrier = pltpu.get_barrier_semaphore()
    for step in range(1, replicas):
        pl.semaphore_signal(
            barrier, 1, device_id=(me_e, lax.rem(me_r + step, replicas)), device_id_type=mesh_id
        )
    pl.semaphore_wait(barrier, replicas - 1)
    local = pltpu.make_async_copy(terms_ref.at[me_r], parts.at[me_r], t_local)
    local.start()
    for step in range(1, replicas):
        t_copy(lax.rem(me_r + step, replicas), me_r).start()
    local.wait()
    for step in range(1, replicas):
        peer = lax.rem(me_r + step, replicas)
        t_copy(peer, peer).wait_recv()
    total = parts[0].astype(jnp.float32)
    for source in range(1, replicas):
        total = total + parts[source].astype(jnp.float32)
    attended = total.astype(own.dtype).astype(jnp.float32)
    own[...] = (resid_ref[...].astype(jnp.float32) + attended).astype(own.dtype)
    keep = pltpu.make_async_copy(own, out_ref.at[me_r], h_local)
    keep.start()
    for step in range(1, replicas):
        h_copy(lax.rem(me_r + step, replicas), me_r).start()
    for step in range(1, replicas):
        peer = lax.rem(me_r + step, replicas)
        t_copy(peer, me_r).wait_send()
        h_copy(peer, me_r).wait_send()
        h_copy(peer, peer).wait_recv()
    keep.wait()


def hidden_rows(terms, residual_block):
    replicas = terms.shape[0]
    block = terms.shape[1:]
    return pl.pallas_call(
        _hidden_kernel,
        out_shape=jax.ShapeDtypeStruct(terms.shape, terms.dtype),
        in_specs=[pl.BlockSpec(memory_space=pl.ANY), pl.BlockSpec(memory_space=pltpu.VMEM)],
        out_specs=pl.BlockSpec(memory_space=pl.ANY),
        scratch_shapes=[
            pltpu.VMEM(terms.shape, terms.dtype),
            pltpu.VMEM(block, terms.dtype),
            pltpu.SemaphoreType.DMA((replicas,)),
            pltpu.SemaphoreType.DMA((replicas,)),
            pltpu.SemaphoreType.DMA(()),
            pltpu.SemaphoreType.DMA((replicas,)),
            pltpu.SemaphoreType.DMA((replicas,)),
            pltpu.SemaphoreType.DMA(()),
        ],
        compiler_params=pltpu.CompilerParams(collective_id=4, has_side_effects=True),
    )(terms, residual_block)


def rep_exchange(blocks):
    return lax.all_to_all(blocks, "rep", split_axis=0, concat_axis=0, tiled=True)


def per_device(
    residual,
    query_latent,
    query_rope,
    cache_latent,
    cache_rope,
    page_table,
    lengths,
    value_up,
    out_proj,
    routes,
    route_weight,
    placement,
    expert_gate,
    expert_up,
    expert_down,
    shared_gate,
    shared_up,
    shared_down,
    norm_gain,
):
    replicas = lax.axis_size("rep")
    expert_groups = lax.axis_size("ep")
    rep_index = lax.axis_index("rep")
    latent_out = attend_rows(
        query_latent, query_rope, cache_latent, cache_rope, page_table, lengths
    )
    own_count = latent_out.shape[0]
    swapped = lax.all_to_all(latent_out, "rep", split_axis=1, concat_axis=0, tiled=True)
    group_rows = swapped.shape[0]
    head_out = jnp.einsum(
        "thr,hrv->thv", swapped, value_up, preferred_element_type=jnp.float32
    ).astype(jnp.bfloat16)
    attn_terms = jnp.dot(
        head_out.reshape(group_rows, -1), out_proj, preferred_element_type=jnp.float32
    )
    model_width = attn_terms.shape[1]
    own_residual = lax.dynamic_slice_in_dim(residual, rep_index * own_count, own_count, 0)
    hidden = hidden_rows(
        attn_terms.astype(jnp.bfloat16).reshape(replicas, own_count, model_width), own_residual
    ).reshape(group_rows, model_width)
    own_hidden = lax.dynamic_slice_in_dim(hidden, rep_index * own_count, own_count, 0)
    shared_act = (
        jax.nn.silu(jnp.dot(hidden, shared_gate, preferred_element_type=jnp.float32))
        * jnp.dot(hidden, shared_up, preferred_element_type=jnp.float32)
    ).astype(jnp.bfloat16)
    shared_terms = jnp.dot(shared_act, shared_down, preferred_element_type=jnp.float32)
    experts = placement.shape[0]
    route_count = routes.shape[1]
    assert experts == expert_groups and replicas == 4
    capacity = max(
        replicas, min(group_rows, 2 * group_rows * route_count // experts // replicas * replicas)
    )
    share = capacity // replicas
    expert_ids = jnp.arange(experts, dtype=jnp.int32)
    slot_index = jnp.sum(jnp.where(routes[:, :, None] == expert_ids, placement, 0), axis=2).reshape(
        -1
    )
    one_hot = (slot_index[:, None] == expert_ids[None, :]).astype(jnp.int32)
    earlier = jnp.cumsum(one_hot, axis=0) - one_hot
    position = jnp.sum(earlier * one_hot, axis=1)
    assignments = slot_index.shape[0]
    source_row = (
        jnp.full((experts * capacity,), group_rows, jnp.int32)
        .at[slot_index * capacity + position]
        .set(jnp.arange(assignments, dtype=jnp.int32) // route_count)
    ).reshape(experts, capacity)
    own_source = lax.dynamic_slice_in_dim(source_row, rep_index * share, share, 1).T.reshape(-1)
    padded = jnp.concatenate([hidden, jnp.zeros((1, model_width), jnp.bfloat16)], axis=0)
    lanes = 128
    outgoing = padded[own_source].reshape(share, experts, model_width // lanes, lanes)
    gathered = dispatch(outgoing, replicas).reshape(share, replicas, expert_groups, model_width)
    gate_values = jnp.einsum(
        "cqgd,df->cqgf", gathered, expert_gate[0], preferred_element_type=jnp.float32
    )
    up_values = jnp.einsum(
        "cqgd,df->cqgf", gathered, expert_up[0], preferred_element_type=jnp.float32
    )
    activated = (jax.nn.silu(gate_values) * up_values).astype(jnp.bfloat16)
    expert_terms = jnp.einsum(
        "cqgf,fd->qcgd", activated, expert_down[0], preferred_element_type=jnp.float32
    ).astype(jnp.bfloat16)
    returned = combine_return(
        expert_terms.reshape(expert_terms.shape[:3] + (model_width // lanes, lanes))
    ).reshape(share * experts, model_width)
    local_pos = position - rep_index * share
    mine = (local_pos >= 0) & (local_pos < share)
    column = jnp.clip(local_pos, 0, share - 1) * experts + slot_index
    weight_used = jnp.where(mine, route_weight.reshape(-1), 0.0)
    combine = jnp.sum(
        jnp.where(
            column[:, None] == jnp.arange(experts * share, dtype=jnp.int32)[None, :],
            weight_used[:, None],
            0.0,
        ).reshape(group_rows, route_count, experts * share),
        axis=1,
    )
    routed = jnp.dot(
        combine, returned.astype(jnp.float32), precision=lax.Precision.HIGHEST,
        preferred_element_type=jnp.float32,
    )
    row_sums = jnp.sum(
        rep_exchange(
            (routed + shared_terms).astype(jnp.bfloat16).reshape(replicas, own_count, model_width)
        ).astype(jnp.float32),
        axis=0,
    )
    mixed = row_sums + own_hidden.astype(jnp.float32)
    inverse = lax.rsqrt(jnp.mean(mixed * mixed, axis=1, keepdims=True) + EPSILON)
    return (mixed * inverse * norm_gain).astype(jnp.bfloat16)


def solution(mesh):
    in_specs = (
        P("ep", None),
        P(("ep", "rep"), None),
        P(("ep", "rep"), None),
        P(("ep", "rep"), None, None),
        P(("ep", "rep"), None),
        P(("ep", "rep"), None),
        P(("ep", "rep")),
        P("rep", None, None),
        P("rep", None),
        P("ep", None),
        P("ep", None),
        P(),
        P("ep", None, "rep"),
        P("ep", None, "rep"),
        P("ep", "rep", None),
        P(None, "rep"),
        P(None, "rep"),
        P("rep", None),
        P(),
    )
    out_specs = P(("ep", "rep"), None)
    return jax.shard_map(
        per_device, mesh=mesh, in_specs=in_specs, out_specs=out_specs, check_vma=False
    )
```

```python
import functools
import math

import jax
import jax.numpy as jnp
from jax import lax
from jax.experimental import pallas as pl
from jax.experimental.pallas import tpu as pltpu
from jax.sharding import PartitionSpec as P

ROPE = 64
VHEAD = 128


EPSILON = 1e-06


def attend_rows(query_latent, query_rope, cache_latent, cache_rope, page_table, lengths):
    row_count, table_len = page_table.shape
    page_count, page_len, latent_width = cache_latent.shape
    rope_width = cache_rope.shape[1] // page_len
    head_count = query_rope.shape[1] // rope_width
    positions = page_count * page_len
    keys_lat = cache_latent.reshape(positions, latent_width)
    keys_rope = cache_rope.reshape(positions, rope_width)
    query_lat = query_latent.reshape(row_count, head_count, latent_width)
    query_rot = query_rope.reshape(row_count, head_count, rope_width)
    score_scale = 1.0 / math.sqrt(VHEAD + ROPE)
    scores = (
        jnp.einsum("thr,pr->thp", query_lat, keys_lat, preferred_element_type=jnp.float32)
        + jnp.einsum("thr,pr->thp", query_rot, keys_rope, preferred_element_type=jnp.float32)
    ) * score_scale
    page_hit = (
        page_table[:, :, None] == jnp.arange(page_count, dtype=jnp.int32)[None, None, :]
    ).astype(jnp.float32)
    context_pos = (
        jnp.arange(table_len, dtype=jnp.int32)[:, None] * page_len
        + jnp.arange(page_len, dtype=jnp.int32)[None, :]
    )
    live = (context_pos[None, :, :] < lengths[:, None, None]).astype(jnp.float32)
    count = jnp.einsum("tkp,tks->tps", page_hit, live).reshape(row_count, 1, positions)
    present = count > 0
    masked = jnp.where(present, scores, -jnp.inf)
    row_peak = jnp.max(masked, axis=2, keepdims=True)
    expons = jnp.where(present, jnp.exp(scores - row_peak), 0.0)
    total = jnp.sum(expons * count, axis=2, keepdims=True)
    probs = (expons / total).astype(jnp.bfloat16)
    weighted = (probs.astype(jnp.float32) * count).astype(jnp.bfloat16)
    latent_out = jnp.einsum("thp,pr->thr", weighted, keys_lat, preferred_element_type=jnp.float32)
    return latent_out.astype(jnp.bfloat16)


def _greet_all(me_e, me_r, groups, replicas):
    mesh_id = pl.DeviceIdType.MESH
    barrier = pltpu.get_barrier_semaphore()

    def greet(step, carry):
        pl.semaphore_signal(
            barrier, 1, device_id=(lax.rem(me_e + step, groups), me_r), device_id_type=mesh_id
        )
        return carry

    lax.fori_loop(1, groups, greet, 0)
    for step in range(1, replicas):
        pl.semaphore_signal(
            barrier, 1, device_id=(me_e, lax.rem(me_r + step, replicas)), device_id_type=mesh_id
        )
    pl.semaphore_wait(barrier, groups - 1 + replicas - 1)


def _dispatch_kernel(src_ref, out_ref, ep_send, ep_recv, local_sem, x_send, x_recv, f_send, f_recv):
    chunks, groups = src_ref.shape[:2]
    replicas = out_ref.shape[1]
    half = groups // 2
    me_e = lax.axis_index("ep")
    me_r = lax.axis_index("rep")
    right = lax.rem(me_r + 1, replicas)
    left = lax.rem(me_r + replicas - 1, replicas)
    across = lax.rem(me_r + 2, replicas)
    mesh_id = pl.DeviceIdType.MESH

    def ep_copy(c, peer, slot):
        return pltpu.make_async_remote_copy(
            src_ref.at[c, peer],
            out_ref.at[c, me_r, slot],
            ep_send.at[c, peer],
            ep_recv.at[c, slot],
            device_id=(peer, me_r),
            device_id_type=mesh_id,
        )

    def x_copy(c, side, slot):
        return pltpu.make_async_remote_copy(
            out_ref.at[c, slot],
            out_ref.at[c, slot],
            x_send.at[c, side],
            x_recv.at[c, side],
            device_id=(me_e, right if side == 0 else left),
            device_id_type=mesh_id,
        )

    def f_copy(c, side, slot, part):
        rows = pl.ds(part * half, half)
        return pltpu.make_async_remote_copy(
            out_ref.at[c, slot, rows],
            out_ref.at[c, slot, rows],
            f_send.at[c, side],
            f_recv.at[c, side],
            device_id=(me_e, right if side == 0 else left),
            device_id_type=mesh_id,
        )

    _greet_all(me_e, me_r, groups, replicas)

    locals_ = []
    for c in range(chunks):
        local = pltpu.make_async_copy(src_ref.at[c, me_e], out_ref.at[c, me_r, me_e], local_sem.at[c])
        local.start()
        locals_.append(local)

        def send(step, carry, c=c):
            ep_copy(c, lax.rem(me_e + step, groups), me_e).start()
            return carry

        lax.fori_loop(1, groups, send, 0)

    def forward(c):
        x_copy(c, 0, left).wait_recv()
        f_copy(c, 0, left, 1).start()
        x_copy(c, 1, right).wait_recv()
        f_copy(c, 1, right, 0).start()

    for c in range(chunks):
        locals_[c].wait()

        def arrive(step, carry, c=c):
            peer = lax.rem(me_e + step, groups)
            ep_copy(c, peer, peer).wait_recv()
            return carry

        lax.fori_loop(1, groups, arrive, 0)
        x_copy(c, 0, me_r).start()
        x_copy(c, 1, me_r).start()
        if c >= 1:
            forward(c - 1)
    forward(chunks - 1)

    for c in range(chunks):
        f_copy(c, 0, across, 1).wait_recv()
        f_copy(c, 1, across, 0).wait_recv()
        for side in range(2):
            x_copy(c, side, me_r).wait_send()
        f_copy(c, 0, left, 1).wait_send()
        f_copy(c, 1, right, 0).wait_send()

        def sent(step, carry, c=c):
            ep_copy(c, lax.rem(me_e + step, groups), me_e).wait_send()
            return carry

        lax.fori_loop(1, groups, sent, 0)


def dispatch(blocks, replicas):
    chunks, groups = blocks.shape[:2]
    out_shape = (chunks, replicas) + blocks.shape[1:]
    return pl.pallas_call(
        _dispatch_kernel,
        out_shape=jax.ShapeDtypeStruct(out_shape, blocks.dtype),
        in_specs=[pl.BlockSpec(memory_space=pl.ANY)],
        out_specs=pl.BlockSpec(memory_space=pl.ANY),
        scratch_shapes=[
            pltpu.SemaphoreType.DMA((chunks, groups)),
            pltpu.SemaphoreType.DMA((chunks, groups)),
            pltpu.SemaphoreType.DMA((chunks,)),
            pltpu.SemaphoreType.DMA((chunks, 2)),
            pltpu.SemaphoreType.DMA((chunks, 2)),
            pltpu.SemaphoreType.DMA((chunks, 2)),
            pltpu.SemaphoreType.DMA((chunks, 2)),
        ],
        compiler_params=pltpu.CompilerParams(collective_id=2, has_side_effects=True),
    )(blocks)


def _combine_kernel(terms_ref, out_ref, parts, sums, x_send, x_recv, x_local, ep_send, ep_recv, ep_local):
    replicas, chunks, groups = terms_ref.shape[:3]
    me_e = lax.axis_index("ep")
    me_r = lax.axis_index("rep")
    mesh_id = pl.DeviceIdType.MESH

    def x_copy(c, peer, slot):
        return pltpu.make_async_remote_copy(
            terms_ref.at[peer, c],
            parts.at[c, slot],
            x_send.at[c, peer],
            x_recv.at[c, slot],
            device_id=(me_e, peer),
            device_id_type=mesh_id,
        )

    def ep_copy(c, peer, slot):
        return pltpu.make_async_remote_copy(
            sums.at[c, peer],
            out_ref.at[c, slot],
            ep_send.at[c, peer],
            ep_recv.at[c, slot],
            device_id=(peer, me_r),
            device_id_type=mesh_id,
        )

    barrier = pltpu.get_barrier_semaphore()

    def greet(step, carry):
        pl.semaphore_signal(
            barrier, 1, device_id=(lax.rem(me_e + step, groups), me_r), device_id_type=mesh_id
        )
        return carry

    lax.fori_loop(1, groups, greet, 0)
    for step in range(1, replicas):
        pl.semaphore_signal(
            barrier, 1, device_id=(me_e, lax.rem(me_r + step, replicas)), device_id_type=mesh_id
        )
    pl.semaphore_wait(barrier, groups - 1 + replicas - 1)

    x_locals = []
    for c in range(chunks):
        local = pltpu.make_async_copy(terms_ref.at[me_r, c], parts.at[c, me_r], x_local.at[c])
        local.start()
        x_locals.append(local)
        for step in range(1, replicas):
            x_copy(c, lax.rem(me_r + step, replicas), me_r).start()

    ep_locals = []
    for c in range(chunks):
        x_locals[c].wait()
        for step in range(1, replicas):
            peer = lax.rem(me_r + step, replicas)
            x_copy(c, peer, peer).wait_recv()
        total = parts[c, 0].astype(jnp.float32)
        for source in range(1, replicas):
            total = total + parts[c, source].astype(jnp.float32)
        sums[c] = total.astype(sums.dtype)
        local = pltpu.make_async_copy(sums.at[c, me_e], out_ref.at[c, me_e], ep_local.at[c])
        local.start()
        ep_locals.append(local)

        def send(step, carry, c=c):
            ep_copy(c, lax.rem(me_e + step, groups), me_e).start()
            return carry

        lax.fori_loop(1, groups, send, 0)

    for c in range(chunks):
        for step in range(1, replicas):
            x_copy(c, lax.rem(me_r + step, replicas), me_r).wait_send()
        ep_locals[c].wait()

        def finish(step, carry, c=c):
            peer = lax.rem(me_e + step, groups)
            ep_copy(c, peer, me_e).wait_send()
            ep_copy(c, peer, peer).wait_recv()
            return carry

        lax.fori_loop(1, groups, finish, 0)


def combine_return(terms):
    replicas, chunks, groups = terms.shape[:3]
    tile = terms.shape[3:]
    return pl.pallas_call(
        _combine_kernel,
        out_shape=jax.ShapeDtypeStruct((chunks, groups) + tile, terms.dtype),
        in_specs=[pl.BlockSpec(memory_space=pl.ANY)],
        out_specs=pl.BlockSpec(memory_space=pl.ANY),
        scratch_shapes=[
            pltpu.VMEM((chunks, replicas, groups) + tile, terms.dtype),
            pltpu.VMEM((chunks, groups) + tile, terms.dtype),
            pltpu.SemaphoreType.DMA((chunks, replicas)),
            pltpu.SemaphoreType.DMA((chunks, replicas)),
            pltpu.SemaphoreType.DMA((chunks,)),
            pltpu.SemaphoreType.DMA((chunks, groups)),
            pltpu.SemaphoreType.DMA((chunks, groups)),
            pltpu.SemaphoreType.DMA((chunks,)),
        ],
        compiler_params=pltpu.CompilerParams(collective_id=3, has_side_effects=True),
    )(terms)


def _hidden_kernel(terms_ref, resid_ref, out_ref, parts, own, t_send, t_recv, t_local, h_send, h_recv, h_local):
    replicas = terms_ref.shape[0]
    me_e = lax.axis_index("ep")
    me_r = lax.axis_index("rep")
    mesh_id = pl.DeviceIdType.MESH

    def t_copy(peer, slot):
        return pltpu.make_async_remote_copy(
            terms_ref.at[peer],
            parts.at[slot],
            t_send.at[peer],
            t_recv.at[slot],
            device_id=(me_e, peer),
            device_id_type=mesh_id,
        )

    def h_copy(peer, slot):
        return pltpu.make_async_remote_copy(
            own,
            out_ref.at[slot],
            h_send.at[peer],
            h_recv.at[slot],
            device_id=(me_e, peer),
            device_id_type=mesh_id,
        )

    barrier = pltpu.get_barrier_semaphore()
    for step in range(1, replicas):
        pl.semaphore_signal(
            barrier, 1, device_id=(me_e, lax.rem(me_r + step, replicas)), device_id_type=mesh_id
        )
    pl.semaphore_wait(barrier, replicas - 1)
    local = pltpu.make_async_copy(terms_ref.at[me_r], parts.at[me_r], t_local)
    local.start()
    for step in range(1, replicas):
        t_copy(lax.rem(me_r + step, replicas), me_r).start()
    local.wait()
    for step in range(1, replicas):
        peer = lax.rem(me_r + step, replicas)
        t_copy(peer, peer).wait_recv()
    total = parts[0].astype(jnp.float32)
    for source in range(1, replicas):
        total = total + parts[source].astype(jnp.float32)
    attended = total.astype(own.dtype).astype(jnp.float32)
    own[...] = (resid_ref[...].astype(jnp.float32) + attended).astype(own.dtype)
    keep = pltpu.make_async_copy(own, out_ref.at[me_r], h_local)
    keep.start()
    for step in range(1, replicas):
        h_copy(lax.rem(me_r + step, replicas), me_r).start()
    for step in range(1, replicas):
        peer = lax.rem(me_r + step, replicas)
        t_copy(peer, me_r).wait_send()
        h_copy(peer, me_r).wait_send()
        h_copy(peer, peer).wait_recv()
    keep.wait()


def hidden_rows(terms, residual_block):
    replicas = terms.shape[0]
    block = terms.shape[1:]
    return pl.pallas_call(
        _hidden_kernel,
        out_shape=jax.ShapeDtypeStruct(terms.shape, terms.dtype),
        in_specs=[pl.BlockSpec(memory_space=pl.ANY), pl.BlockSpec(memory_space=pltpu.VMEM)],
        out_specs=pl.BlockSpec(memory_space=pl.ANY),
        scratch_shapes=[
            pltpu.VMEM(terms.shape, terms.dtype),
            pltpu.VMEM(block, terms.dtype),
            pltpu.SemaphoreType.DMA((replicas,)),
            pltpu.SemaphoreType.DMA((replicas,)),
            pltpu.SemaphoreType.DMA(()),
            pltpu.SemaphoreType.DMA((replicas,)),
            pltpu.SemaphoreType.DMA((replicas,)),
            pltpu.SemaphoreType.DMA(()),
        ],
        compiler_params=pltpu.CompilerParams(collective_id=4, has_side_effects=True),
    )(terms, residual_block)


def _finish_kernel(terms_ref, hidden_ref, gain_ref, out_ref, parts, t_send, t_recv, t_local):
    replicas = terms_ref.shape[0]
    me_e = lax.axis_index("ep")
    me_r = lax.axis_index("rep")
    mesh_id = pl.DeviceIdType.MESH

    def t_copy(peer, slot):
        return pltpu.make_async_remote_copy(
            terms_ref.at[peer],
            parts.at[slot],
            t_send.at[peer],
            t_recv.at[slot],
            device_id=(me_e, peer),
            device_id_type=mesh_id,
        )

    barrier = pltpu.get_barrier_semaphore()
    for step in range(1, replicas):
        pl.semaphore_signal(
            barrier, 1, device_id=(me_e, lax.rem(me_r + step, replicas)), device_id_type=mesh_id
        )
    pl.semaphore_wait(barrier, replicas - 1)
    local = pltpu.make_async_copy(terms_ref.at[me_r], parts.at[me_r], t_local)
    local.start()
    for step in range(1, replicas):
        t_copy(lax.rem(me_r + step, replicas), me_r).start()
    local.wait()
    for step in range(1, replicas):
        peer = lax.rem(me_r + step, replicas)
        t_copy(peer, peer).wait_recv()
    total = parts[0].astype(jnp.float32)
    for source in range(1, replicas):
        total = total + parts[source].astype(jnp.float32)
    mixed = total + hidden_ref[...].astype(jnp.float32)
    inverse = lax.rsqrt(jnp.mean(mixed * mixed, axis=1, keepdims=True) + EPSILON)
    out_ref[...] = (mixed * inverse * gain_ref[...]).astype(out_ref.dtype)
    for step in range(1, replicas):
        t_copy(lax.rem(me_r + step, replicas), me_r).wait_send()


def finish_rows(terms, hidden_block, gain):
    replicas = terms.shape[0]
    block = terms.shape[1:]
    return pl.pallas_call(
        _finish_kernel,
        out_shape=jax.ShapeDtypeStruct(block, hidden_block.dtype),
        in_specs=[
            pl.BlockSpec(memory_space=pl.ANY),
            pl.BlockSpec(memory_space=pltpu.VMEM),
            pl.BlockSpec(memory_space=pltpu.VMEM),
        ],
        out_specs=pl.BlockSpec(memory_space=pltpu.VMEM),
        scratch_shapes=[
            pltpu.VMEM(terms.shape, terms.dtype),
            pltpu.SemaphoreType.DMA((replicas,)),
            pltpu.SemaphoreType.DMA((replicas,)),
            pltpu.SemaphoreType.DMA(()),
        ],
        compiler_params=pltpu.CompilerParams(collective_id=5, has_side_effects=True),
    )(terms, hidden_block, gain.reshape(1, -1))


def rep_exchange(blocks):
    return lax.all_to_all(blocks, "rep", split_axis=0, concat_axis=0, tiled=True)


def per_device(
    residual,
    query_latent,
    query_rope,
    cache_latent,
    cache_rope,
    page_table,
    lengths,
    value_up,
    out_proj,
    routes,
    route_weight,
    placement,
    expert_gate,
    expert_up,
    expert_down,
    shared_gate,
    shared_up,
    shared_down,
    norm_gain,
):
    replicas = lax.axis_size("rep")
    expert_groups = lax.axis_size("ep")
    rep_index = lax.axis_index("rep")
    latent_out = attend_rows(
        query_latent, query_rope, cache_latent, cache_rope, page_table, lengths
    )
    own_count = latent_out.shape[0]
    swapped = lax.all_to_all(latent_out, "rep", split_axis=1, concat_axis=0, tiled=True)
    group_rows = swapped.shape[0]
    head_out = jnp.einsum(
        "thr,hrv->thv", swapped, value_up, preferred_element_type=jnp.float32
    ).astype(jnp.bfloat16)
    attn_terms = jnp.dot(
        head_out.reshape(group_rows, -1), out_proj, preferred_element_type=jnp.float32
    )
    model_width = attn_terms.shape[1]
    own_residual = lax.dynamic_slice_in_dim(residual, rep_index * own_count, own_count, 0)
    hidden = hidden_rows(
        attn_terms.astype(jnp.bfloat16).reshape(replicas, own_count, model_width), own_residual
    ).reshape(group_rows, model_width)
    own_hidden = lax.dynamic_slice_in_dim(hidden, rep_index * own_count, own_count, 0)
    shared_act = (
        jax.nn.silu(jnp.dot(hidden, shared_gate, preferred_element_type=jnp.float32))
        * jnp.dot(hidden, shared_up, preferred_element_type=jnp.float32)
    ).astype(jnp.bfloat16)
    shared_terms = jnp.dot(shared_act, shared_down, preferred_element_type=jnp.float32)
    experts = placement.shape[0]
    route_count = routes.shape[1]
    assert experts == expert_groups and replicas == 4
    capacity = max(
        replicas, min(group_rows, 2 * group_rows * route_count // experts // replicas * replicas)
    )
    share = capacity // replicas
    expert_ids = jnp.arange(experts, dtype=jnp.int32)
    slot_index = jnp.sum(jnp.where(routes[:, :, None] == expert_ids, placement, 0), axis=2).reshape(
        -1
    )
    one_hot = (slot_index[:, None] == expert_ids[None, :]).astype(jnp.int32)
    earlier = jnp.cumsum(one_hot, axis=0) - one_hot
    position = jnp.sum(earlier * one_hot, axis=1)
    assignments = slot_index.shape[0]
    source_row = (
        jnp.full((experts * capacity,), group_rows, jnp.int32)
        .at[slot_index * capacity + position]
        .set(jnp.arange(assignments, dtype=jnp.int32) // route_count)
    ).reshape(experts, capacity)
    own_source = lax.dynamic_slice_in_dim(source_row, rep_index * share, share, 1).T.reshape(-1)
    padded = jnp.concatenate([hidden, jnp.zeros((1, model_width), jnp.bfloat16)], axis=0)
    lanes = 128
    outgoing = padded[own_source].reshape(share, experts, model_width // lanes, lanes)
    gathered = dispatch(outgoing, replicas).reshape(share, replicas, expert_groups, model_width)
    gate_values = jnp.einsum(
        "cqgd,df->cqgf", gathered, expert_gate[0], preferred_element_type=jnp.float32
    )
    up_values = jnp.einsum(
        "cqgd,df->cqgf", gathered, expert_up[0], preferred_element_type=jnp.float32
    )
    activated = (jax.nn.silu(gate_values) * up_values).astype(jnp.bfloat16)
    expert_terms = jnp.einsum(
        "cqgf,fd->qcgd", activated, expert_down[0], preferred_element_type=jnp.float32
    ).astype(jnp.bfloat16)
    returned = combine_return(
        expert_terms.reshape(expert_terms.shape[:3] + (model_width // lanes, lanes))
    ).reshape(share * experts, model_width)
    local_pos = position - rep_index * share
    mine = (local_pos >= 0) & (local_pos < share)
    column = jnp.clip(local_pos, 0, share - 1) * experts + slot_index
    weight_used = jnp.where(mine, route_weight.reshape(-1), 0.0)
    combine = jnp.sum(
        jnp.where(
            column[:, None] == jnp.arange(experts * share, dtype=jnp.int32)[None, :],
            weight_used[:, None],
            0.0,
        ).reshape(group_rows, route_count, experts * share),
        axis=1,
    )
    routed = jnp.dot(
        combine, returned.astype(jnp.float32), precision=lax.Precision.HIGHEST,
        preferred_element_type=jnp.float32,
    )
    return finish_rows(
        (routed + shared_terms).astype(jnp.bfloat16).reshape(replicas, own_count, model_width),
        own_hidden,
        norm_gain,
    )


def solution(mesh):
    in_specs = (
        P("ep", None),
        P(("ep", "rep"), None),
        P(("ep", "rep"), None),
        P(("ep", "rep"), None, None),
        P(("ep", "rep"), None),
        P(("ep", "rep"), None),
        P(("ep", "rep")),
        P("rep", None, None),
        P("rep", None),
        P("ep", None),
        P("ep", None),
        P(),
        P("ep", None, "rep"),
        P("ep", None, "rep"),
        P("ep", "rep", None),
        P(None, "rep"),
        P(None, "rep"),
        P("rep", None),
        P(),
    )
    out_specs = P(("ep", "rep"), None)
    return jax.shard_map(
        per_device, mesh=mesh, in_specs=in_specs, out_specs=out_specs, check_vma=False
    )
```

```python
import functools
import math

import jax
import jax.numpy as jnp
from jax import lax
from jax.experimental import pallas as pl
from jax.experimental.pallas import tpu as pltpu
from jax.sharding import PartitionSpec as P

ROPE = 64
VHEAD = 128


EPSILON = 1e-06


def attend_rows(query_latent, query_rope, cache_latent, cache_rope, page_table, lengths):
    row_count, table_len = page_table.shape
    page_count, page_len, latent_width = cache_latent.shape
    rope_width = cache_rope.shape[1] // page_len
    head_count = query_rope.shape[1] // rope_width
    positions = page_count * page_len
    keys_lat = cache_latent.reshape(positions, latent_width)
    keys_rope = cache_rope.reshape(positions, rope_width)
    query_lat = query_latent.reshape(row_count, head_count, latent_width)
    query_rot = query_rope.reshape(row_count, head_count, rope_width)
    score_scale = 1.0 / math.sqrt(VHEAD + ROPE)
    scores = (
        jnp.einsum("thr,pr->thp", query_lat, keys_lat, preferred_element_type=jnp.float32)
        + jnp.einsum("thr,pr->thp", query_rot, keys_rope, preferred_element_type=jnp.float32)
    ) * score_scale
    page_hit = (
        page_table[:, :, None] == jnp.arange(page_count, dtype=jnp.int32)[None, None, :]
    ).astype(jnp.float32)
    context_pos = (
        jnp.arange(table_len, dtype=jnp.int32)[:, None] * page_len
        + jnp.arange(page_len, dtype=jnp.int32)[None, :]
    )
    live = (context_pos[None, :, :] < lengths[:, None, None]).astype(jnp.float32)
    count = jnp.einsum("tkp,tks->tps", page_hit, live).reshape(row_count, 1, positions)
    present = count > 0
    masked = jnp.where(present, scores, -jnp.inf)
    row_peak = jnp.max(masked, axis=2, keepdims=True)
    expons = jnp.where(present, jnp.exp(scores - row_peak), 0.0)
    total = jnp.sum(expons * count, axis=2, keepdims=True)
    probs = (expons / total).astype(jnp.bfloat16)
    weighted = (probs.astype(jnp.float32) * count).astype(jnp.bfloat16)
    latent_out = jnp.einsum("thp,pr->thr", weighted, keys_lat, preferred_element_type=jnp.float32)
    return latent_out.astype(jnp.bfloat16)


def _greet_all(me_e, me_r, groups, replicas):
    mesh_id = pl.DeviceIdType.MESH
    barrier = pltpu.get_barrier_semaphore()

    def greet(step, carry):
        pl.semaphore_signal(
            barrier, 1, device_id=(lax.rem(me_e + step, groups), me_r), device_id_type=mesh_id
        )
        return carry

    lax.fori_loop(1, groups, greet, 0)
    for step in range(1, replicas):
        pl.semaphore_signal(
            barrier, 1, device_id=(me_e, lax.rem(me_r + step, replicas)), device_id_type=mesh_id
        )
    pl.semaphore_wait(barrier, groups - 1 + replicas - 1)


def _dispatch_kernel(src_ref, out_ref, ep_send, ep_recv, local_sem, x_send, x_recv, f_send, f_recv):
    chunks, groups = src_ref.shape[:2]
    replicas = out_ref.shape[1]
    half = groups // 2
    me_e = lax.axis_index("ep")
    me_r = lax.axis_index("rep")
    right = lax.rem(me_r + 1, replicas)
    left = lax.rem(me_r + replicas - 1, replicas)
    across = lax.rem(me_r + 2, replicas)
    mesh_id = pl.DeviceIdType.MESH

    def ep_copy(c, peer, slot):
        return pltpu.make_async_remote_copy(
            src_ref.at[c, peer],
            out_ref.at[c, me_r, slot],
            ep_send.at[c, peer],
            ep_recv.at[c, slot],
            device_id=(peer, me_r),
            device_id_type=mesh_id,
        )

    def x_copy(c, side, slot):
        return pltpu.make_async_remote_copy(
            out_ref.at[c, slot],
            out_ref.at[c, slot],
            x_send.at[c, side],
            x_recv.at[c, side],
            device_id=(me_e, right if side == 0 else left),
            device_id_type=mesh_id,
        )

    def f_copy(c, side, slot, part):
        rows = pl.ds(part * half, half)
        return pltpu.make_async_remote_copy(
            out_ref.at[c, slot, rows],
            out_ref.at[c, slot, rows],
            f_send.at[c, side],
            f_recv.at[c, side],
            device_id=(me_e, right if side == 0 else left),
            device_id_type=mesh_id,
        )

    _greet_all(me_e, me_r, groups, replicas)

    locals_ = []
    for c in range(chunks):
        local = pltpu.make_async_copy(src_ref.at[c, me_e], out_ref.at[c, me_r, me_e], local_sem.at[c])
        local.start()
        locals_.append(local)

        def send(step, carry, c=c):
            ep_copy(c, lax.rem(me_e + step, groups), me_e).start()
            return carry

        lax.fori_loop(1, groups, send, 0)

    def forward(c):
        x_copy(c, 0, left).wait_recv()
        f_copy(c, 0, left, 1).start()
        x_copy(c, 1, right).wait_recv()
        f_copy(c, 1, right, 0).start()

    for c in range(chunks):
        locals_[c].wait()

        def arrive(step, carry, c=c):
            peer = lax.rem(me_e + step, groups)
            ep_copy(c, peer, peer).wait_recv()
            return carry

        lax.fori_loop(1, groups, arrive, 0)
        x_copy(c, 0, me_r).start()
        x_copy(c, 1, me_r).start()
        if c >= 1:
            forward(c - 1)
    forward(chunks - 1)

    for c in range(chunks):
        f_copy(c, 0, across, 1).wait_recv()
        f_copy(c, 1, across, 0).wait_recv()
        for side in range(2):
            x_copy(c, side, me_r).wait_send()
        f_copy(c, 0, left, 1).wait_send()
        f_copy(c, 1, right, 0).wait_send()

        def sent(step, carry, c=c):
            ep_copy(c, lax.rem(me_e + step, groups), me_e).wait_send()
            return carry

        lax.fori_loop(1, groups, sent, 0)


def dispatch(blocks, replicas):
    chunks, groups = blocks.shape[:2]
    out_shape = (chunks, replicas) + blocks.shape[1:]
    return pl.pallas_call(
        _dispatch_kernel,
        out_shape=jax.ShapeDtypeStruct(out_shape, blocks.dtype),
        in_specs=[pl.BlockSpec(memory_space=pl.ANY)],
        out_specs=pl.BlockSpec(memory_space=pl.ANY),
        scratch_shapes=[
            pltpu.SemaphoreType.DMA((chunks, groups)),
            pltpu.SemaphoreType.DMA((chunks, groups)),
            pltpu.SemaphoreType.DMA((chunks,)),
            pltpu.SemaphoreType.DMA((chunks, 2)),
            pltpu.SemaphoreType.DMA((chunks, 2)),
            pltpu.SemaphoreType.DMA((chunks, 2)),
            pltpu.SemaphoreType.DMA((chunks, 2)),
        ],
        compiler_params=pltpu.CompilerParams(collective_id=2, has_side_effects=True),
    )(blocks)


def _combine_kernel(terms_ref, out_ref, parts, sums, x_send, x_recv, x_local, ep_send, ep_recv, ep_local):
    replicas, chunks, groups = terms_ref.shape[:3]
    me_e = lax.axis_index("ep")
    me_r = lax.axis_index("rep")
    mesh_id = pl.DeviceIdType.MESH

    def x_copy(c, peer, slot):
        return pltpu.make_async_remote_copy(
            terms_ref.at[peer, c],
            parts.at[c, slot],
            x_send.at[c, peer],
            x_recv.at[c, slot],
            device_id=(me_e, peer),
            device_id_type=mesh_id,
        )

    def ep_copy(c, peer, slot):
        return pltpu.make_async_remote_copy(
            sums.at[c, peer],
            out_ref.at[c, slot],
            ep_send.at[c, peer],
            ep_recv.at[c, slot],
            device_id=(peer, me_r),
            device_id_type=mesh_id,
        )

    barrier = pltpu.get_barrier_semaphore()

    def greet(step, carry):
        pl.semaphore_signal(
            barrier, 1, device_id=(lax.rem(me_e + step, groups), me_r), device_id_type=mesh_id
        )
        return carry

    lax.fori_loop(1, groups, greet, 0)
    for step in range(1, replicas):
        pl.semaphore_signal(
            barrier, 1, device_id=(me_e, lax.rem(me_r + step, replicas)), device_id_type=mesh_id
        )
    pl.semaphore_wait(barrier, groups - 1 + replicas - 1)

    x_locals = []

    def issue(c):
        local = pltpu.make_async_copy(terms_ref.at[me_r, c], parts.at[c, me_r], x_local.at[c])
        local.start()
        x_locals.append(local)
        for step in range(1, replicas):
            x_copy(c, lax.rem(me_r + step, replicas), me_r).start()

    ahead = 2
    for c in range(min(ahead, chunks)):
        issue(c)

    ep_locals = []
    for c in range(chunks):
        x_locals[c].wait()
        for step in range(1, replicas):
            peer = lax.rem(me_r + step, replicas)
            x_copy(c, peer, peer).wait_recv()
        total = parts[c, 0].astype(jnp.float32)
        for source in range(1, replicas):
            total = total + parts[c, source].astype(jnp.float32)
        sums[c] = total.astype(sums.dtype)
        local = pltpu.make_async_copy(sums.at[c, me_e], out_ref.at[c, me_e], ep_local.at[c])
        local.start()
        ep_locals.append(local)

        def send(step, carry, c=c):
            ep_copy(c, lax.rem(me_e + step, groups), me_e).start()
            return carry

        lax.fori_loop(1, groups, send, 0)
        if c + ahead < chunks:
            issue(c + ahead)

    for c in range(chunks):
        for step in range(1, replicas):
            x_copy(c, lax.rem(me_r + step, replicas), me_r).wait_send()
        ep_locals[c].wait()

        def finish(step, carry, c=c):
            peer = lax.rem(me_e + step, groups)
            ep_copy(c, peer, me_e).wait_send()
            ep_copy(c, peer, peer).wait_recv()
            return carry

        lax.fori_loop(1, groups, finish, 0)


def combine_return(terms):
    replicas, chunks, groups = terms.shape[:3]
    tile = terms.shape[3:]
    return pl.pallas_call(
        _combine_kernel,
        out_shape=jax.ShapeDtypeStruct((chunks, groups) + tile, terms.dtype),
        in_specs=[pl.BlockSpec(memory_space=pl.ANY)],
        out_specs=pl.BlockSpec(memory_space=pl.ANY),
        scratch_shapes=[
            pltpu.VMEM((chunks, replicas, groups) + tile, terms.dtype),
            pltpu.VMEM((chunks, groups) + tile, terms.dtype),
            pltpu.SemaphoreType.DMA((chunks, replicas)),
            pltpu.SemaphoreType.DMA((chunks, replicas)),
            pltpu.SemaphoreType.DMA((chunks,)),
            pltpu.SemaphoreType.DMA((chunks, groups)),
            pltpu.SemaphoreType.DMA((chunks, groups)),
            pltpu.SemaphoreType.DMA((chunks,)),
        ],
        compiler_params=pltpu.CompilerParams(collective_id=3, has_side_effects=True),
    )(terms)


def _hidden_kernel(terms_ref, resid_ref, out_ref, parts, own, t_send, t_recv, t_local, h_send, h_recv, h_local):
    replicas = terms_ref.shape[0]
    me_e = lax.axis_index("ep")
    me_r = lax.axis_index("rep")
    mesh_id = pl.DeviceIdType.MESH

    def t_copy(peer, slot):
        return pltpu.make_async_remote_copy(
            terms_ref.at[peer],
            parts.at[slot],
            t_send.at[peer],
            t_recv.at[slot],
            device_id=(me_e, peer),
            device_id_type=mesh_id,
        )

    def h_copy(peer, slot):
        return pltpu.make_async_remote_copy(
            own,
            out_ref.at[slot],
            h_send.at[peer],
            h_recv.at[slot],
            device_id=(me_e, peer),
            device_id_type=mesh_id,
        )

    barrier = pltpu.get_barrier_semaphore()
    for step in range(1, replicas):
        pl.semaphore_signal(
            barrier, 1, device_id=(me_e, lax.rem(me_r + step, replicas)), device_id_type=mesh_id
        )
    pl.semaphore_wait(barrier, replicas - 1)
    local = pltpu.make_async_copy(terms_ref.at[me_r], parts.at[me_r], t_local)
    local.start()
    for step in range(1, replicas):
        t_copy(lax.rem(me_r + step, replicas), me_r).start()
    local.wait()
    for step in range(1, replicas):
        peer = lax.rem(me_r + step, replicas)
        t_copy(peer, peer).wait_recv()
    total = parts[0].astype(jnp.float32)
    for source in range(1, replicas):
        total = total + parts[source].astype(jnp.float32)
    attended = total.astype(own.dtype).astype(jnp.float32)
    own[...] = (resid_ref[...].astype(jnp.float32) + attended).astype(own.dtype)
    keep = pltpu.make_async_copy(own, out_ref.at[me_r], h_local)
    keep.start()
    for step in range(1, replicas):
        h_copy(lax.rem(me_r + step, replicas), me_r).start()
    for step in range(1, replicas):
        peer = lax.rem(me_r + step, replicas)
        t_copy(peer, me_r).wait_send()
        h_copy(peer, me_r).wait_send()
        h_copy(peer, peer).wait_recv()
    keep.wait()


def hidden_rows(terms, residual_block):
    replicas = terms.shape[0]
    block = terms.shape[1:]
    return pl.pallas_call(
        _hidden_kernel,
        out_shape=jax.ShapeDtypeStruct(terms.shape, terms.dtype),
        in_specs=[pl.BlockSpec(memory_space=pl.ANY), pl.BlockSpec(memory_space=pltpu.VMEM)],
        out_specs=pl.BlockSpec(memory_space=pl.ANY),
        scratch_shapes=[
            pltpu.VMEM(terms.shape, terms.dtype),
            pltpu.VMEM(block, terms.dtype),
            pltpu.SemaphoreType.DMA((replicas,)),
            pltpu.SemaphoreType.DMA((replicas,)),
            pltpu.SemaphoreType.DMA(()),
            pltpu.SemaphoreType.DMA((replicas,)),
            pltpu.SemaphoreType.DMA((replicas,)),
            pltpu.SemaphoreType.DMA(()),
        ],
        compiler_params=pltpu.CompilerParams(collective_id=4, has_side_effects=True),
    )(terms, residual_block)


def rep_exchange(blocks):
    return lax.all_to_all(blocks, "rep", split_axis=0, concat_axis=0, tiled=True)


def per_device(
    residual,
    query_latent,
    query_rope,
    cache_latent,
    cache_rope,
    page_table,
    lengths,
    value_up,
    out_proj,
    routes,
    route_weight,
    placement,
    expert_gate,
    expert_up,
    expert_down,
    shared_gate,
    shared_up,
    shared_down,
    norm_gain,
):
    replicas = lax.axis_size("rep")
    expert_groups = lax.axis_size("ep")
    rep_index = lax.axis_index("rep")
    latent_out = attend_rows(
        query_latent, query_rope, cache_latent, cache_rope, page_table, lengths
    )
    own_count = latent_out.shape[0]
    swapped = lax.all_to_all(latent_out, "rep", split_axis=1, concat_axis=0, tiled=True)
    group_rows = swapped.shape[0]
    head_out = jnp.einsum(
        "thr,hrv->thv", swapped, value_up, preferred_element_type=jnp.float32
    ).astype(jnp.bfloat16)
    attn_terms = jnp.dot(
        head_out.reshape(group_rows, -1), out_proj, preferred_element_type=jnp.float32
    )
    model_width = attn_terms.shape[1]
    own_residual = lax.dynamic_slice_in_dim(residual, rep_index * own_count, own_count, 0)
    hidden = hidden_rows(
        attn_terms.astype(jnp.bfloat16).reshape(replicas, own_count, model_width), own_residual
    ).reshape(group_rows, model_width)
    own_hidden = lax.dynamic_slice_in_dim(hidden, rep_index * own_count, own_count, 0)
    shared_act = (
        jax.nn.silu(jnp.dot(hidden, shared_gate, preferred_element_type=jnp.float32))
        * jnp.dot(hidden, shared_up, preferred_element_type=jnp.float32)
    ).astype(jnp.bfloat16)
    shared_terms = jnp.dot(shared_act, shared_down, preferred_element_type=jnp.float32)
    experts = placement.shape[0]
    route_count = routes.shape[1]
    assert experts == expert_groups and replicas == 4
    capacity = max(
        replicas, min(group_rows, 2 * group_rows * route_count // experts // replicas * replicas)
    )
    share = capacity // replicas
    expert_ids = jnp.arange(experts, dtype=jnp.int32)
    slot_index = jnp.sum(jnp.where(routes[:, :, None] == expert_ids, placement, 0), axis=2).reshape(
        -1
    )
    one_hot = (slot_index[:, None] == expert_ids[None, :]).astype(jnp.int32)
    earlier = jnp.cumsum(one_hot, axis=0) - one_hot
    position = jnp.sum(earlier * one_hot, axis=1)
    assignments = slot_index.shape[0]
    source_row = (
        jnp.full((experts * capacity,), group_rows, jnp.int32)
        .at[slot_index * capacity + position]
        .set(jnp.arange(assignments, dtype=jnp.int32) // route_count)
    ).reshape(experts, capacity)
    own_source = lax.dynamic_slice_in_dim(source_row, rep_index * share, share, 1).T.reshape(-1)
    padded = jnp.concatenate([hidden, jnp.zeros((1, model_width), jnp.bfloat16)], axis=0)
    lanes = 128
    outgoing = padded[own_source].reshape(share, experts, model_width // lanes, lanes)
    gathered = dispatch(outgoing, replicas).reshape(share, replicas, expert_groups, model_width)
    gate_values = jnp.einsum(
        "cqgd,df->cqgf", gathered, expert_gate[0], preferred_element_type=jnp.float32
    )
    up_values = jnp.einsum(
        "cqgd,df->cqgf", gathered, expert_up[0], preferred_element_type=jnp.float32
    )
    activated = (jax.nn.silu(gate_values) * up_values).astype(jnp.bfloat16)
    expert_terms = jnp.einsum(
        "cqgf,fd->qcgd", activated, expert_down[0], preferred_element_type=jnp.float32
    ).astype(jnp.bfloat16)
    returned = combine_return(
        expert_terms.reshape(expert_terms.shape[:3] + (model_width // lanes, lanes))
    ).reshape(share * experts, model_width)
    local_pos = position - rep_index * share
    mine = (local_pos >= 0) & (local_pos < share)
    column = jnp.clip(local_pos, 0, share - 1) * experts + slot_index
    weight_used = jnp.where(mine, route_weight.reshape(-1), 0.0)
    combine = jnp.sum(
        jnp.where(
            column[:, None] == jnp.arange(experts * share, dtype=jnp.int32)[None, :],
            weight_used[:, None],
            0.0,
        ).reshape(group_rows, route_count, experts * share),
        axis=1,
    )
    routed = jnp.dot(
        combine, returned.astype(jnp.float32), precision=lax.Precision.HIGHEST,
        preferred_element_type=jnp.float32,
    )
    row_sums = jnp.sum(
        rep_exchange(
            (routed + shared_terms).astype(jnp.bfloat16).reshape(replicas, own_count, model_width)
        ).astype(jnp.float32),
        axis=0,
    )
    mixed = row_sums + own_hidden.astype(jnp.float32)
    inverse = lax.rsqrt(jnp.mean(mixed * mixed, axis=1, keepdims=True) + EPSILON)
    return (mixed * inverse * norm_gain).astype(jnp.bfloat16)


def solution(mesh):
    in_specs = (
        P("ep", None),
        P(("ep", "rep"), None),
        P(("ep", "rep"), None),
        P(("ep", "rep"), None, None),
        P(("ep", "rep"), None),
        P(("ep", "rep"), None),
        P(("ep", "rep")),
        P("rep", None, None),
        P("rep", None),
        P("ep", None),
        P("ep", None),
        P(),
        P("ep", None, "rep"),
        P("ep", None, "rep"),
        P("ep", "rep", None),
        P(None, "rep"),
        P(None, "rep"),
        P("rep", None),
        P(),
    )
    out_specs = P(("ep", "rep"), None)
    return jax.shard_map(
        per_device, mesh=mesh, in_specs=in_specs, out_specs=out_specs, check_vma=False
    )
```

```python
import functools
import math

import jax
import jax.numpy as jnp
from jax import lax
from jax.experimental import pallas as pl
from jax.experimental.pallas import tpu as pltpu
from jax.sharding import PartitionSpec as P

ROPE = 64
VHEAD = 128


EPSILON = 1e-06


def attend_rows(query_latent, query_rope, cache_latent, cache_rope, page_table, lengths):
    row_count, table_len = page_table.shape
    page_count, page_len, latent_width = cache_latent.shape
    rope_width = cache_rope.shape[1] // page_len
    head_count = query_rope.shape[1] // rope_width
    positions = page_count * page_len
    keys_lat = cache_latent.reshape(positions, latent_width)
    keys_rope = cache_rope.reshape(positions, rope_width)
    query_lat = query_latent.reshape(row_count, head_count, latent_width)
    query_rot = query_rope.reshape(row_count, head_count, rope_width)
    score_scale = 1.0 / math.sqrt(VHEAD + ROPE)
    scores = (
        jnp.einsum("thr,pr->thp", query_lat, keys_lat, preferred_element_type=jnp.float32)
        + jnp.einsum("thr,pr->thp", query_rot, keys_rope, preferred_element_type=jnp.float32)
    ) * score_scale
    page_hit = (
        page_table[:, :, None] == jnp.arange(page_count, dtype=jnp.int32)[None, None, :]
    ).astype(jnp.float32)
    context_pos = (
        jnp.arange(table_len, dtype=jnp.int32)[:, None] * page_len
        + jnp.arange(page_len, dtype=jnp.int32)[None, :]
    )
    live = (context_pos[None, :, :] < lengths[:, None, None]).astype(jnp.float32)
    count = jnp.einsum("tkp,tks->tps", page_hit, live).reshape(row_count, 1, positions)
    present = count > 0
    masked = jnp.where(present, scores, -jnp.inf)
    row_peak = jnp.max(masked, axis=2, keepdims=True)
    expons = jnp.where(present, jnp.exp(scores - row_peak), 0.0)
    total = jnp.sum(expons * count, axis=2, keepdims=True)
    probs = (expons / total).astype(jnp.bfloat16)
    weighted = (probs.astype(jnp.float32) * count).astype(jnp.bfloat16)
    latent_out = jnp.einsum("thp,pr->thr", weighted, keys_lat, preferred_element_type=jnp.float32)
    return latent_out.astype(jnp.bfloat16)


def _greet_all(me_e, me_r, groups, replicas):
    mesh_id = pl.DeviceIdType.MESH
    barrier = pltpu.get_barrier_semaphore()

    def greet(step, carry):
        pl.semaphore_signal(
            barrier, 1, device_id=(lax.rem(me_e + step, groups), me_r), device_id_type=mesh_id
        )
        return carry

    lax.fori_loop(1, groups, greet, 0)
    for step in range(1, replicas):
        pl.semaphore_signal(
            barrier, 1, device_id=(me_e, lax.rem(me_r + step, replicas)), device_id_type=mesh_id
        )
    pl.semaphore_wait(barrier, groups - 1 + replicas - 1)


def _dispatch_kernel(src_ref, out_ref, ep_send, ep_recv, local_sem, x_send, x_recv, f_send, f_recv):
    chunks, groups = src_ref.shape[:2]
    replicas = out_ref.shape[1]
    half = groups // 2
    me_e = lax.axis_index("ep")
    me_r = lax.axis_index("rep")
    right = lax.rem(me_r + 1, replicas)
    left = lax.rem(me_r + replicas - 1, replicas)
    across = lax.rem(me_r + 2, replicas)
    mesh_id = pl.DeviceIdType.MESH

    def ep_copy(c, peer, slot):
        return pltpu.make_async_remote_copy(
            src_ref.at[c, peer],
            out_ref.at[c, me_r, slot],
            ep_send.at[c, peer],
            ep_recv.at[c, slot],
            device_id=(peer, me_r),
            device_id_type=mesh_id,
        )

    def x_copy(c, side, slot):
        return pltpu.make_async_remote_copy(
            out_ref.at[c, slot],
            out_ref.at[c, slot],
            x_send.at[c, side],
            x_recv.at[c, side],
            device_id=(me_e, right if side == 0 else left),
            device_id_type=mesh_id,
        )

    def f_copy(c, side, slot, part):
        rows = pl.ds(part * half, half)
        return pltpu.make_async_remote_copy(
            out_ref.at[c, slot, rows],
            out_ref.at[c, slot, rows],
            f_send.at[c, side],
            f_recv.at[c, side],
            device_id=(me_e, right if side == 0 else left),
            device_id_type=mesh_id,
        )

    _greet_all(me_e, me_r, groups, replicas)

    locals_ = []
    for c in range(chunks):
        local = pltpu.make_async_copy(src_ref.at[c, me_e], out_ref.at[c, me_r, me_e], local_sem.at[c])
        local.start()
        locals_.append(local)

        def send(step, carry, c=c):
            ep_copy(c, lax.rem(me_e + step, groups), me_e).start()
            return carry

        lax.fori_loop(1, groups, send, 0)

    def forward(c):
        x_copy(c, 0, left).wait_recv()
        f_copy(c, 0, left, 1).start()
        x_copy(c, 1, right).wait_recv()
        f_copy(c, 1, right, 0).start()

    for c in range(chunks):
        locals_[c].wait()

        def arrive(step, carry, c=c):
            peer = lax.rem(me_e + step, groups)
            ep_copy(c, peer, peer).wait_recv()
            return carry

        lax.fori_loop(1, groups, arrive, 0)
        x_copy(c, 0, me_r).start()
        x_copy(c, 1, me_r).start()
        if c >= 1:
            forward(c - 1)
    forward(chunks - 1)

    for c in range(chunks):
        f_copy(c, 0, across, 1).wait_recv()
        f_copy(c, 1, across, 0).wait_recv()
        for side in range(2):
            x_copy(c, side, me_r).wait_send()
        f_copy(c, 0, left, 1).wait_send()
        f_copy(c, 1, right, 0).wait_send()

        def sent(step, carry, c=c):
            ep_copy(c, lax.rem(me_e + step, groups), me_e).wait_send()
            return carry

        lax.fori_loop(1, groups, sent, 0)


def dispatch(blocks, replicas):
    chunks, groups = blocks.shape[:2]
    out_shape = (chunks, replicas) + blocks.shape[1:]
    return pl.pallas_call(
        _dispatch_kernel,
        out_shape=jax.ShapeDtypeStruct(out_shape, blocks.dtype),
        in_specs=[pl.BlockSpec(memory_space=pl.ANY)],
        out_specs=pl.BlockSpec(memory_space=pl.ANY),
        scratch_shapes=[
            pltpu.SemaphoreType.DMA((chunks, groups)),
            pltpu.SemaphoreType.DMA((chunks, groups)),
            pltpu.SemaphoreType.DMA((chunks,)),
            pltpu.SemaphoreType.DMA((chunks, 2)),
            pltpu.SemaphoreType.DMA((chunks, 2)),
            pltpu.SemaphoreType.DMA((chunks, 2)),
            pltpu.SemaphoreType.DMA((chunks, 2)),
        ],
        compiler_params=pltpu.CompilerParams(collective_id=2, has_side_effects=True),
    )(blocks)


def _combine_kernel(terms_ref, out_ref, parts, sums, x_send, x_recv, x_local, ep_send, ep_recv, ep_local):
    chunks, replicas, groups = terms_ref.shape[:3]
    me_e = lax.axis_index("ep")
    me_r = lax.axis_index("rep")
    mesh_id = pl.DeviceIdType.MESH

    def x_copy(c, peer, slot):
        return pltpu.make_async_remote_copy(
            terms_ref.at[c, peer],
            parts.at[c, slot],
            x_send.at[c, peer],
            x_recv.at[c, slot],
            device_id=(me_e, peer),
            device_id_type=mesh_id,
        )

    def ep_copy(c, peer, slot):
        return pltpu.make_async_remote_copy(
            sums.at[c, peer],
            out_ref.at[c, slot],
            ep_send.at[c, peer],
            ep_recv.at[c, slot],
            device_id=(peer, me_r),
            device_id_type=mesh_id,
        )

    barrier = pltpu.get_barrier_semaphore()

    def greet(step, carry):
        pl.semaphore_signal(
            barrier, 1, device_id=(lax.rem(me_e + step, groups), me_r), device_id_type=mesh_id
        )
        return carry

    lax.fori_loop(1, groups, greet, 0)
    for step in range(1, replicas):
        pl.semaphore_signal(
            barrier, 1, device_id=(me_e, lax.rem(me_r + step, replicas)), device_id_type=mesh_id
        )
    pl.semaphore_wait(barrier, groups - 1 + replicas - 1)

    x_locals = []

    def issue(c):
        local = pltpu.make_async_copy(terms_ref.at[c, me_r], parts.at[c, me_r], x_local.at[c])
        local.start()
        x_locals.append(local)
        for step in range(1, replicas):
            x_copy(c, lax.rem(me_r + step, replicas), me_r).start()

    ahead = 2
    for c in range(min(ahead, chunks)):
        issue(c)

    ep_locals = []
    for c in range(chunks):
        x_locals[c].wait()
        for step in range(1, replicas):
            peer = lax.rem(me_r + step, replicas)
            x_copy(c, peer, peer).wait_recv()
        total = parts[c, 0].astype(jnp.float32)
        for source in range(1, replicas):
            total = total + parts[c, source].astype(jnp.float32)
        sums[c] = total.astype(sums.dtype)
        local = pltpu.make_async_copy(sums.at[c, me_e], out_ref.at[c, me_e], ep_local.at[c])
        local.start()
        ep_locals.append(local)

        def send(step, carry, c=c):
            ep_copy(c, lax.rem(me_e + step, groups), me_e).start()
            return carry

        lax.fori_loop(1, groups, send, 0)
        if c + ahead < chunks:
            issue(c + ahead)

    for c in range(chunks):
        for step in range(1, replicas):
            x_copy(c, lax.rem(me_r + step, replicas), me_r).wait_send()
        ep_locals[c].wait()

        def finish(step, carry, c=c):
            peer = lax.rem(me_e + step, groups)
            ep_copy(c, peer, me_e).wait_send()
            ep_copy(c, peer, peer).wait_recv()
            return carry

        lax.fori_loop(1, groups, finish, 0)


def combine_return(terms):
    chunks, replicas, groups = terms.shape[:3]
    tile = terms.shape[3:]
    return pl.pallas_call(
        _combine_kernel,
        out_shape=jax.ShapeDtypeStruct((chunks, groups) + tile, terms.dtype),
        in_specs=[pl.BlockSpec(memory_space=pl.ANY)],
        out_specs=pl.BlockSpec(memory_space=pl.ANY),
        scratch_shapes=[
            pltpu.VMEM((chunks, replicas, groups) + tile, terms.dtype),
            pltpu.VMEM((chunks, groups) + tile, terms.dtype),
            pltpu.SemaphoreType.DMA((chunks, replicas)),
            pltpu.SemaphoreType.DMA((chunks, replicas)),
            pltpu.SemaphoreType.DMA((chunks,)),
            pltpu.SemaphoreType.DMA((chunks, groups)),
            pltpu.SemaphoreType.DMA((chunks, groups)),
            pltpu.SemaphoreType.DMA((chunks,)),
        ],
        compiler_params=pltpu.CompilerParams(collective_id=3, has_side_effects=True),
    )(terms)


def _hidden_kernel(terms_ref, resid_ref, out_ref, parts, own, t_send, t_recv, t_local, h_send, h_recv, h_local):
    replicas = terms_ref.shape[0]
    me_e = lax.axis_index("ep")
    me_r = lax.axis_index("rep")
    mesh_id = pl.DeviceIdType.MESH

    def t_copy(peer, slot):
        return pltpu.make_async_remote_copy(
            terms_ref.at[peer],
            parts.at[slot],
            t_send.at[peer],
            t_recv.at[slot],
            device_id=(me_e, peer),
            device_id_type=mesh_id,
        )

    def h_copy(peer, slot):
        return pltpu.make_async_remote_copy(
            own,
            out_ref.at[slot],
            h_send.at[peer],
            h_recv.at[slot],
            device_id=(me_e, peer),
            device_id_type=mesh_id,
        )

    barrier = pltpu.get_barrier_semaphore()
    for step in range(1, replicas):
        pl.semaphore_signal(
            barrier, 1, device_id=(me_e, lax.rem(me_r + step, replicas)), device_id_type=mesh_id
        )
    pl.semaphore_wait(barrier, replicas - 1)
    local = pltpu.make_async_copy(terms_ref.at[me_r], parts.at[me_r], t_local)
    local.start()
    for step in range(1, replicas):
        t_copy(lax.rem(me_r + step, replicas), me_r).start()
    local.wait()
    for step in range(1, replicas):
        peer = lax.rem(me_r + step, replicas)
        t_copy(peer, peer).wait_recv()
    total = parts[0].astype(jnp.float32)
    for source in range(1, replicas):
        total = total + parts[source].astype(jnp.float32)
    attended = total.astype(own.dtype).astype(jnp.float32)
    own[...] = (resid_ref[...].astype(jnp.float32) + attended).astype(own.dtype)
    keep = pltpu.make_async_copy(own, out_ref.at[me_r], h_local)
    keep.start()
    for step in range(1, replicas):
        h_copy(lax.rem(me_r + step, replicas), me_r).start()
    for step in range(1, replicas):
        peer = lax.rem(me_r + step, replicas)
        t_copy(peer, me_r).wait_send()
        h_copy(peer, me_r).wait_send()
        h_copy(peer, peer).wait_recv()
    keep.wait()


def hidden_rows(terms, residual_block):
    replicas = terms.shape[0]
    block = terms.shape[1:]
    return pl.pallas_call(
        _hidden_kernel,
        out_shape=jax.ShapeDtypeStruct(terms.shape, terms.dtype),
        in_specs=[pl.BlockSpec(memory_space=pl.ANY), pl.BlockSpec(memory_space=pltpu.VMEM)],
        out_specs=pl.BlockSpec(memory_space=pl.ANY),
        scratch_shapes=[
            pltpu.VMEM(terms.shape, terms.dtype),
            pltpu.VMEM(block, terms.dtype),
            pltpu.SemaphoreType.DMA((replicas,)),
            pltpu.SemaphoreType.DMA((replicas,)),
            pltpu.SemaphoreType.DMA(()),
            pltpu.SemaphoreType.DMA((replicas,)),
            pltpu.SemaphoreType.DMA((replicas,)),
            pltpu.SemaphoreType.DMA(()),
        ],
        compiler_params=pltpu.CompilerParams(collective_id=4, has_side_effects=True),
    )(terms, residual_block)


def rep_exchange(blocks):
    return lax.all_to_all(blocks, "rep", split_axis=0, concat_axis=0, tiled=True)


def per_device(
    residual,
    query_latent,
    query_rope,
    cache_latent,
    cache_rope,
    page_table,
    lengths,
    value_up,
    out_proj,
    routes,
    route_weight,
    placement,
    expert_gate,
    expert_up,
    expert_down,
    shared_gate,
    shared_up,
    shared_down,
    norm_gain,
):
    replicas = lax.axis_size("rep")
    expert_groups = lax.axis_size("ep")
    rep_index = lax.axis_index("rep")
    latent_out = attend_rows(
        query_latent, query_rope, cache_latent, cache_rope, page_table, lengths
    )
    own_count = latent_out.shape[0]
    swapped = lax.all_to_all(latent_out, "rep", split_axis=1, concat_axis=0, tiled=True)
    group_rows = swapped.shape[0]
    head_out = jnp.einsum(
        "thr,hrv->thv", swapped, value_up, preferred_element_type=jnp.float32
    ).astype(jnp.bfloat16)
    attn_terms = jnp.dot(
        head_out.reshape(group_rows, -1), out_proj, preferred_element_type=jnp.float32
    )
    model_width = attn_terms.shape[1]
    own_residual = lax.dynamic_slice_in_dim(residual, rep_index * own_count, own_count, 0)
    hidden = hidden_rows(
        attn_terms.astype(jnp.bfloat16).reshape(replicas, own_count, model_width), own_residual
    ).reshape(group_rows, model_width)
    own_hidden = lax.dynamic_slice_in_dim(hidden, rep_index * own_count, own_count, 0)
    shared_act = (
        jax.nn.silu(jnp.dot(hidden, shared_gate, preferred_element_type=jnp.float32))
        * jnp.dot(hidden, shared_up, preferred_element_type=jnp.float32)
    ).astype(jnp.bfloat16)
    shared_terms = jnp.dot(shared_act, shared_down, preferred_element_type=jnp.float32)
    experts = placement.shape[0]
    route_count = routes.shape[1]
    assert experts == expert_groups and replicas == 4
    capacity = max(
        replicas, min(group_rows, 2 * group_rows * route_count // experts // replicas * replicas)
    )
    share = capacity // replicas
    expert_ids = jnp.arange(experts, dtype=jnp.int32)
    slot_index = jnp.sum(jnp.where(routes[:, :, None] == expert_ids, placement, 0), axis=2).reshape(
        -1
    )
    one_hot = (slot_index[:, None] == expert_ids[None, :]).astype(jnp.int32)
    earlier = jnp.cumsum(one_hot, axis=0) - one_hot
    position = jnp.sum(earlier * one_hot, axis=1)
    assignments = slot_index.shape[0]
    source_row = (
        jnp.full((experts * capacity,), group_rows, jnp.int32)
        .at[slot_index * capacity + position]
        .set(jnp.arange(assignments, dtype=jnp.int32) // route_count)
    ).reshape(experts, capacity)
    own_source = lax.dynamic_slice_in_dim(source_row, rep_index * share, share, 1).T.reshape(-1)
    padded = jnp.concatenate([hidden, jnp.zeros((1, model_width), jnp.bfloat16)], axis=0)
    lanes = 128
    outgoing = padded[own_source].reshape(share, experts, model_width // lanes, lanes)
    gathered = dispatch(outgoing, replicas)
    tiles = (model_width // lanes, lanes)
    gate_values = jnp.einsum(
        "cqgxy,xyf->cqgf", gathered, expert_gate[0].reshape(tiles + (-1,)),
        preferred_element_type=jnp.float32,
    )
    up_values = jnp.einsum(
        "cqgxy,xyf->cqgf", gathered, expert_up[0].reshape(tiles + (-1,)),
        preferred_element_type=jnp.float32,
    )
    activated = (jax.nn.silu(gate_values) * up_values).astype(jnp.bfloat16)
    expert_terms = jnp.einsum(
        "cqgf,fxy->cqgxy", activated, expert_down[0].reshape((-1,) + tiles),
        preferred_element_type=jnp.float32,
    ).astype(jnp.bfloat16)
    returned = combine_return(expert_terms).reshape(share * experts, model_width)
    local_pos = position - rep_index * share
    mine = (local_pos >= 0) & (local_pos < share)
    column = jnp.clip(local_pos, 0, share - 1) * experts + slot_index
    weight_used = jnp.where(mine, route_weight.reshape(-1), 0.0)
    combine = jnp.sum(
        jnp.where(
            column[:, None] == jnp.arange(experts * share, dtype=jnp.int32)[None, :],
            weight_used[:, None],
            0.0,
        ).reshape(group_rows, route_count, experts * share),
        axis=1,
    )
    routed = jnp.dot(
        combine, returned.astype(jnp.float32), precision=lax.Precision.HIGHEST,
        preferred_element_type=jnp.float32,
    )
    row_sums = jnp.sum(
        rep_exchange(
            (routed + shared_terms).astype(jnp.bfloat16).reshape(replicas, own_count, model_width)
        ).astype(jnp.float32),
        axis=0,
    )
    mixed = row_sums + own_hidden.astype(jnp.float32)
    inverse = lax.rsqrt(jnp.mean(mixed * mixed, axis=1, keepdims=True) + EPSILON)
    return (mixed * inverse * norm_gain).astype(jnp.bfloat16)


def solution(mesh):
    in_specs = (
        P("ep", None),
        P(("ep", "rep"), None),
        P(("ep", "rep"), None),
        P(("ep", "rep"), None, None),
        P(("ep", "rep"), None),
        P(("ep", "rep"), None),
        P(("ep", "rep")),
        P("rep", None, None),
        P("rep", None),
        P("ep", None),
        P("ep", None),
        P(),
        P("ep", None, "rep"),
        P("ep", None, "rep"),
        P("ep", "rep", None),
        P(None, "rep"),
        P(None, "rep"),
        P("rep", None),
        P(),
    )
    out_specs = P(("ep", "rep"), None)
    return jax.shard_map(
        per_device, mesh=mesh, in_specs=in_specs, out_specs=out_specs, check_vma=False
    )
```

```python
import functools
import math

import jax
import jax.numpy as jnp
from jax import lax
from jax.experimental import pallas as pl
from jax.experimental.pallas import tpu as pltpu
from jax.sharding import PartitionSpec as P

ROPE = 64
VHEAD = 128


EPSILON = 1e-06


def attend_rows(query_latent, query_rope, cache_latent, cache_rope, page_table, lengths):
    row_count, table_len = page_table.shape
    page_count, page_len, latent_width = cache_latent.shape
    rope_width = cache_rope.shape[1] // page_len
    head_count = query_rope.shape[1] // rope_width
    positions = page_count * page_len
    keys_lat = cache_latent.reshape(positions, latent_width)
    keys_rope = cache_rope.reshape(positions, rope_width)
    query_lat = query_latent.reshape(row_count, head_count, latent_width)
    query_rot = query_rope.reshape(row_count, head_count, rope_width)
    score_scale = 1.0 / math.sqrt(VHEAD + ROPE)
    scores = (
        jnp.einsum("thr,pr->thp", query_lat, keys_lat, preferred_element_type=jnp.float32)
        + jnp.einsum("thr,pr->thp", query_rot, keys_rope, preferred_element_type=jnp.float32)
    ) * score_scale
    page_hit = (
        page_table[:, :, None] == jnp.arange(page_count, dtype=jnp.int32)[None, None, :]
    ).astype(jnp.float32)
    context_pos = (
        jnp.arange(table_len, dtype=jnp.int32)[:, None] * page_len
        + jnp.arange(page_len, dtype=jnp.int32)[None, :]
    )
    live = (context_pos[None, :, :] < lengths[:, None, None]).astype(jnp.float32)
    count = jnp.einsum("tkp,tks->tps", page_hit, live).reshape(row_count, 1, positions)
    present = count > 0
    masked = jnp.where(present, scores, -jnp.inf)
    row_peak = jnp.max(masked, axis=2, keepdims=True)
    expons = jnp.where(present, jnp.exp(scores - row_peak), 0.0)
    total = jnp.sum(expons * count, axis=2, keepdims=True)
    probs = (expons / total).astype(jnp.bfloat16)
    weighted = (probs.astype(jnp.float32) * count).astype(jnp.bfloat16)
    latent_out = jnp.einsum("thp,pr->thr", weighted, keys_lat, preferred_element_type=jnp.float32)
    return latent_out.astype(jnp.bfloat16)


def _greet_all(me_e, me_r, groups, replicas):
    mesh_id = pl.DeviceIdType.MESH
    barrier = pltpu.get_barrier_semaphore()

    def greet(step, carry):
        pl.semaphore_signal(
            barrier, 1, device_id=(lax.rem(me_e + step, groups), me_r), device_id_type=mesh_id
        )
        return carry

    lax.fori_loop(1, groups, greet, 0)
    for step in range(1, replicas):
        pl.semaphore_signal(
            barrier, 1, device_id=(me_e, lax.rem(me_r + step, replicas)), device_id_type=mesh_id
        )
    pl.semaphore_wait(barrier, groups - 1 + replicas - 1)


def _dispatch_kernel(src_ref, out_ref, ep_send, ep_recv, local_sem, x_send, x_recv, f_send, f_recv):
    chunks, groups = src_ref.shape[:2]
    replicas = out_ref.shape[1]
    half = groups // 2
    me_e = lax.axis_index("ep")
    me_r = lax.axis_index("rep")
    right = lax.rem(me_r + 1, replicas)
    left = lax.rem(me_r + replicas - 1, replicas)
    across = lax.rem(me_r + 2, replicas)
    mesh_id = pl.DeviceIdType.MESH

    def ep_copy(c, peer, slot):
        return pltpu.make_async_remote_copy(
            src_ref.at[c, peer],
            out_ref.at[c, me_r, slot],
            ep_send.at[c, peer],
            ep_recv.at[c, slot],
            device_id=(peer, me_r),
            device_id_type=mesh_id,
        )

    def x_copy(c, side, slot):
        return pltpu.make_async_remote_copy(
            out_ref.at[c, slot],
            out_ref.at[c, slot],
            x_send.at[c, side],
            x_recv.at[c, side],
            device_id=(me_e, right if side == 0 else left),
            device_id_type=mesh_id,
        )

    def f_copy(c, side, slot, part):
        rows = pl.ds(part * half, half)
        return pltpu.make_async_remote_copy(
            out_ref.at[c, slot, rows],
            out_ref.at[c, slot, rows],
            f_send.at[c, side],
            f_recv.at[c, side],
            device_id=(me_e, right if side == 0 else left),
            device_id_type=mesh_id,
        )

    _greet_all(me_e, me_r, groups, replicas)

    locals_ = []
    for c in range(chunks):
        local = pltpu.make_async_copy(src_ref.at[c, me_e], out_ref.at[c, me_r, me_e], local_sem.at[c])
        local.start()
        locals_.append(local)

        def send(step, carry, c=c):
            ep_copy(c, lax.rem(me_e + step, groups), me_e).start()
            return carry

        lax.fori_loop(1, groups, send, 0)

    def forward(c):
        x_copy(c, 0, left).wait_recv()
        f_copy(c, 0, left, 1).start()
        x_copy(c, 1, right).wait_recv()
        f_copy(c, 1, right, 0).start()

    for c in range(chunks):
        locals_[c].wait()

        def arrive(step, carry, c=c):
            peer = lax.rem(me_e + step, groups)
            ep_copy(c, peer, peer).wait_recv()
            return carry

        lax.fori_loop(1, groups, arrive, 0)
        x_copy(c, 0, me_r).start()
        x_copy(c, 1, me_r).start()
        if c >= 1:
            forward(c - 1)
    forward(chunks - 1)

    for c in range(chunks):
        f_copy(c, 0, across, 1).wait_recv()
        f_copy(c, 1, across, 0).wait_recv()
        for side in range(2):
            x_copy(c, side, me_r).wait_send()
        f_copy(c, 0, left, 1).wait_send()
        f_copy(c, 1, right, 0).wait_send()

        def sent(step, carry, c=c):
            ep_copy(c, lax.rem(me_e + step, groups), me_e).wait_send()
            return carry

        lax.fori_loop(1, groups, sent, 0)


def dispatch(blocks, replicas):
    chunks, groups = blocks.shape[:2]
    out_shape = (chunks, replicas) + blocks.shape[1:]
    return pl.pallas_call(
        _dispatch_kernel,
        out_shape=jax.ShapeDtypeStruct(out_shape, blocks.dtype),
        in_specs=[pl.BlockSpec(memory_space=pl.ANY)],
        out_specs=pl.BlockSpec(memory_space=pl.ANY),
        scratch_shapes=[
            pltpu.SemaphoreType.DMA((chunks, groups)),
            pltpu.SemaphoreType.DMA((chunks, groups)),
            pltpu.SemaphoreType.DMA((chunks,)),
            pltpu.SemaphoreType.DMA((chunks, 2)),
            pltpu.SemaphoreType.DMA((chunks, 2)),
            pltpu.SemaphoreType.DMA((chunks, 2)),
            pltpu.SemaphoreType.DMA((chunks, 2)),
        ],
        compiler_params=pltpu.CompilerParams(collective_id=2, has_side_effects=True),
    )(blocks)


def _combine_kernel(terms_ref, out_ref, parts, sums, x_send, x_recv, x_local, ep_send, ep_recv, ep_local):
    chunks, replicas, groups = terms_ref.shape[:3]
    me_e = lax.axis_index("ep")
    me_r = lax.axis_index("rep")
    mesh_id = pl.DeviceIdType.MESH

    def x_copy(c, peer, slot):
        return pltpu.make_async_remote_copy(
            terms_ref.at[c, peer],
            parts.at[c, slot],
            x_send.at[c, peer],
            x_recv.at[c, slot],
            device_id=(me_e, peer),
            device_id_type=mesh_id,
        )

    def ep_copy(c, peer, slot):
        return pltpu.make_async_remote_copy(
            sums.at[c, peer],
            out_ref.at[c, slot],
            ep_send.at[c, peer],
            ep_recv.at[c, slot],
            device_id=(peer, me_r),
            device_id_type=mesh_id,
        )

    barrier = pltpu.get_barrier_semaphore()

    def greet(step, carry):
        pl.semaphore_signal(
            barrier, 1, device_id=(lax.rem(me_e + step, groups), me_r), device_id_type=mesh_id
        )
        return carry

    lax.fori_loop(1, groups, greet, 0)
    for step in range(1, replicas):
        pl.semaphore_signal(
            barrier, 1, device_id=(me_e, lax.rem(me_r + step, replicas)), device_id_type=mesh_id
        )
    pl.semaphore_wait(barrier, groups - 1 + replicas - 1)

    x_locals = []
    for c in range(chunks):
        local = pltpu.make_async_copy(terms_ref.at[c, me_r], parts.at[c, me_r], x_local.at[c])
        local.start()
        x_locals.append(local)
        for step in range(1, replicas):
            x_copy(c, lax.rem(me_r + step, replicas), me_r).start()

    ep_locals = []
    for c in range(chunks):
        x_locals[c].wait()
        for step in range(1, replicas):
            peer = lax.rem(me_r + step, replicas)
            x_copy(c, peer, peer).wait_recv()
        total = parts[c, 0].astype(jnp.float32)
        for source in range(1, replicas):
            total = total + parts[c, source].astype(jnp.float32)
        sums[c] = total.astype(sums.dtype)
        local = pltpu.make_async_copy(sums.at[c, me_e], out_ref.at[c, me_e], ep_local.at[c])
        local.start()
        ep_locals.append(local)

        def send(step, carry, c=c):
            ep_copy(c, lax.rem(me_e + step, groups), me_e).start()
            return carry

        lax.fori_loop(1, groups, send, 0)

    for c in range(chunks):
        for step in range(1, replicas):
            x_copy(c, lax.rem(me_r + step, replicas), me_r).wait_send()
        ep_locals[c].wait()

        def finish(step, carry, c=c):
            peer = lax.rem(me_e + step, groups)
            ep_copy(c, peer, me_e).wait_send()
            ep_copy(c, peer, peer).wait_recv()
            return carry

        lax.fori_loop(1, groups, finish, 0)


def combine_return(terms):
    chunks, replicas, groups = terms.shape[:3]
    tile = terms.shape[3:]
    return pl.pallas_call(
        _combine_kernel,
        out_shape=jax.ShapeDtypeStruct((chunks, groups) + tile, terms.dtype),
        in_specs=[pl.BlockSpec(memory_space=pl.ANY)],
        out_specs=pl.BlockSpec(memory_space=pl.ANY),
        scratch_shapes=[
            pltpu.VMEM((chunks, replicas, groups) + tile, terms.dtype),
            pltpu.VMEM((chunks, groups) + tile, terms.dtype),
            pltpu.SemaphoreType.DMA((chunks, replicas)),
            pltpu.SemaphoreType.DMA((chunks, replicas)),
            pltpu.SemaphoreType.DMA((chunks,)),
            pltpu.SemaphoreType.DMA((chunks, groups)),
            pltpu.SemaphoreType.DMA((chunks, groups)),
            pltpu.SemaphoreType.DMA((chunks,)),
        ],
        compiler_params=pltpu.CompilerParams(collective_id=3, has_side_effects=True),
    )(terms)


def _hidden_kernel(terms_ref, resid_ref, out_ref, parts, own, t_send, t_recv, t_local, h_send, h_recv, h_local):
    replicas = terms_ref.shape[0]
    me_e = lax.axis_index("ep")
    me_r = lax.axis_index("rep")
    mesh_id = pl.DeviceIdType.MESH

    def t_copy(peer, slot):
        return pltpu.make_async_remote_copy(
            terms_ref.at[peer],
            parts.at[slot],
            t_send.at[peer],
            t_recv.at[slot],
            device_id=(me_e, peer),
            device_id_type=mesh_id,
        )

    def h_copy(peer, slot):
        return pltpu.make_async_remote_copy(
            own,
            out_ref.at[slot],
            h_send.at[peer],
            h_recv.at[slot],
            device_id=(me_e, peer),
            device_id_type=mesh_id,
        )

    barrier = pltpu.get_barrier_semaphore()
    for step in range(1, replicas):
        pl.semaphore_signal(
            barrier, 1, device_id=(me_e, lax.rem(me_r + step, replicas)), device_id_type=mesh_id
        )
    pl.semaphore_wait(barrier, replicas - 1)
    local = pltpu.make_async_copy(terms_ref.at[me_r], parts.at[me_r], t_local)
    local.start()
    for step in range(1, replicas):
        t_copy(lax.rem(me_r + step, replicas), me_r).start()
    local.wait()
    for step in range(1, replicas):
        peer = lax.rem(me_r + step, replicas)
        t_copy(peer, peer).wait_recv()
    total = parts[0].astype(jnp.float32)
    for source in range(1, replicas):
        total = total + parts[source].astype(jnp.float32)
    attended = total.astype(own.dtype).astype(jnp.float32)
    own[...] = (resid_ref[...].astype(jnp.float32) + attended).astype(own.dtype)
    keep = pltpu.make_async_copy(own, out_ref.at[me_r], h_local)
    keep.start()
    for step in range(1, replicas):
        h_copy(lax.rem(me_r + step, replicas), me_r).start()
    for step in range(1, replicas):
        peer = lax.rem(me_r + step, replicas)
        t_copy(peer, me_r).wait_send()
        h_copy(peer, me_r).wait_send()
        h_copy(peer, peer).wait_recv()
    keep.wait()


def hidden_rows(terms, residual_block):
    replicas = terms.shape[0]
    block = terms.shape[1:]
    return pl.pallas_call(
        _hidden_kernel,
        out_shape=jax.ShapeDtypeStruct(terms.shape, terms.dtype),
        in_specs=[pl.BlockSpec(memory_space=pl.ANY), pl.BlockSpec(memory_space=pltpu.VMEM)],
        out_specs=pl.BlockSpec(memory_space=pl.ANY),
        scratch_shapes=[
            pltpu.VMEM(terms.shape, terms.dtype),
            pltpu.VMEM(block, terms.dtype),
            pltpu.SemaphoreType.DMA((replicas,)),
            pltpu.SemaphoreType.DMA((replicas,)),
            pltpu.SemaphoreType.DMA(()),
            pltpu.SemaphoreType.DMA((replicas,)),
            pltpu.SemaphoreType.DMA((replicas,)),
            pltpu.SemaphoreType.DMA(()),
        ],
        compiler_params=pltpu.CompilerParams(collective_id=4, has_side_effects=True),
    )(terms, residual_block)


def rep_exchange(blocks):
    return lax.all_to_all(blocks, "rep", split_axis=0, concat_axis=0, tiled=True)


def per_device(
    residual,
    query_latent,
    query_rope,
    cache_latent,
    cache_rope,
    page_table,
    lengths,
    value_up,
    out_proj,
    routes,
    route_weight,
    placement,
    expert_gate,
    expert_up,
    expert_down,
    shared_gate,
    shared_up,
    shared_down,
    norm_gain,
):
    replicas = lax.axis_size("rep")
    expert_groups = lax.axis_size("ep")
    rep_index = lax.axis_index("rep")
    latent_out = attend_rows(
        query_latent, query_rope, cache_latent, cache_rope, page_table, lengths
    )
    own_count = latent_out.shape[0]
    swapped = lax.all_to_all(latent_out, "rep", split_axis=1, concat_axis=0, tiled=True)
    group_rows = swapped.shape[0]
    head_out = jnp.einsum(
        "thr,hrv->thv", swapped, value_up, preferred_element_type=jnp.float32
    ).astype(jnp.bfloat16)
    attn_terms = jnp.dot(
        head_out.reshape(group_rows, -1), out_proj, preferred_element_type=jnp.float32
    )
    model_width = attn_terms.shape[1]
    own_residual = lax.dynamic_slice_in_dim(residual, rep_index * own_count, own_count, 0)
    hidden = hidden_rows(
        attn_terms.astype(jnp.bfloat16).reshape(replicas, own_count, model_width), own_residual
    ).reshape(group_rows, model_width)
    own_hidden = lax.dynamic_slice_in_dim(hidden, rep_index * own_count, own_count, 0)
    shared_act = (
        jax.nn.silu(jnp.dot(hidden, shared_gate, preferred_element_type=jnp.float32))
        * jnp.dot(hidden, shared_up, preferred_element_type=jnp.float32)
    ).astype(jnp.bfloat16)
    shared_terms = jnp.dot(shared_act, shared_down, preferred_element_type=jnp.float32)
    experts = placement.shape[0]
    route_count = routes.shape[1]
    assert experts == expert_groups and replicas == 4
    capacity = max(
        replicas, min(group_rows, 2 * group_rows * route_count // experts // replicas * replicas)
    )
    share = capacity // replicas
    expert_ids = jnp.arange(experts, dtype=jnp.int32)
    slot_index = jnp.sum(jnp.where(routes[:, :, None] == expert_ids, placement, 0), axis=2).reshape(
        -1
    )
    one_hot = (slot_index[:, None] == expert_ids[None, :]).astype(jnp.int32)
    earlier = jnp.cumsum(one_hot, axis=0) - one_hot
    position = jnp.sum(earlier * one_hot, axis=1)
    assignments = slot_index.shape[0]
    row_tag = (jnp.arange(assignments, dtype=jnp.int32) // route_count + 1).astype(jnp.float32)
    own_pos = rep_index * share + jnp.arange(share, dtype=jnp.int32)
    filled = jnp.einsum(
        "ae,ac->ce",
        one_hot.astype(jnp.float32) * row_tag[:, None],
        (position[:, None] == own_pos[None, :]).astype(jnp.float32),
        precision=lax.Precision.HIGHEST,
        preferred_element_type=jnp.float32,
    )
    own_source = jnp.where(filled > 0, filled.astype(jnp.int32) - 1, group_rows).reshape(-1)
    padded = jnp.concatenate([hidden, jnp.zeros((1, model_width), jnp.bfloat16)], axis=0)
    lanes = 128
    outgoing = padded[own_source].reshape(share, experts, model_width // lanes, lanes)
    gathered = dispatch(outgoing, replicas).reshape(share, replicas, expert_groups, model_width)
    gate_values = jnp.einsum(
        "cqgd,df->cqgf", gathered, expert_gate[0], preferred_element_type=jnp.float32
    )
    up_values = jnp.einsum(
        "cqgd,df->cqgf", gathered, expert_up[0], preferred_element_type=jnp.float32
    )
    activated = (jax.nn.silu(gate_values) * up_values).astype(jnp.bfloat16)
    expert_terms = jnp.einsum(
        "cqgf,fd->cqgd", activated, expert_down[0], preferred_element_type=jnp.float32
    ).astype(jnp.bfloat16)
    returned = combine_return(
        expert_terms.reshape(expert_terms.shape[:3] + (model_width // lanes, lanes))
    ).reshape(share * experts, model_width)
    local_pos = position - rep_index * share
    mine = (local_pos >= 0) & (local_pos < share)
    column = jnp.clip(local_pos, 0, share - 1) * experts + slot_index
    weight_used = jnp.where(mine, route_weight.reshape(-1), 0.0)
    combine = jnp.sum(
        jnp.where(
            column[:, None] == jnp.arange(experts * share, dtype=jnp.int32)[None, :],
            weight_used[:, None],
            0.0,
        ).reshape(group_rows, route_count, experts * share),
        axis=1,
    )
    routed = jnp.dot(
        combine, returned.astype(jnp.float32), precision=lax.Precision.HIGHEST,
        preferred_element_type=jnp.float32,
    )
    row_sums = jnp.sum(
        rep_exchange(
            (routed + shared_terms).astype(jnp.bfloat16).reshape(replicas, own_count, model_width)
        ).astype(jnp.float32),
        axis=0,
    )
    mixed = row_sums + own_hidden.astype(jnp.float32)
    inverse = lax.rsqrt(jnp.mean(mixed * mixed, axis=1, keepdims=True) + EPSILON)
    return (mixed * inverse * norm_gain).astype(jnp.bfloat16)


def solution(mesh):
    in_specs = (
        P("ep", None),
        P(("ep", "rep"), None),
        P(("ep", "rep"), None),
        P(("ep", "rep"), None, None),
        P(("ep", "rep"), None),
        P(("ep", "rep"), None),
        P(("ep", "rep")),
        P("rep", None, None),
        P("rep", None),
        P("ep", None),
        P("ep", None),
        P(),
        P("ep", None, "rep"),
        P("ep", None, "rep"),
        P("ep", "rep", None),
        P(None, "rep"),
        P(None, "rep"),
        P("rep", None),
        P(),
    )
    out_specs = P(("ep", "rep"), None)
    return jax.shard_map(
        per_device, mesh=mesh, in_specs=in_specs, out_specs=out_specs, check_vma=False
    )
```

```python
import functools
import math

import jax
import jax.numpy as jnp
from jax import lax
from jax.experimental import pallas as pl
from jax.experimental.pallas import tpu as pltpu
from jax.sharding import PartitionSpec as P

ROPE = 64
VHEAD = 128


EPSILON = 1e-06


def attend_rows(query_latent, query_rope, cache_latent, cache_rope, page_table, lengths):
    row_count, table_len = page_table.shape
    page_count, page_len, latent_width = cache_latent.shape
    rope_width = cache_rope.shape[1] // page_len
    head_count = query_rope.shape[1] // rope_width
    positions = page_count * page_len
    keys_lat = cache_latent.reshape(positions, latent_width)
    keys_rope = cache_rope.reshape(positions, rope_width)
    query_lat = query_latent.reshape(row_count, head_count, latent_width)
    query_rot = query_rope.reshape(row_count, head_count, rope_width)
    score_scale = 1.0 / math.sqrt(VHEAD + ROPE)
    scores = (
        jnp.einsum("thr,pr->thp", query_lat, keys_lat, preferred_element_type=jnp.float32)
        + jnp.einsum("thr,pr->thp", query_rot, keys_rope, preferred_element_type=jnp.float32)
    ) * score_scale
    page_hit = (
        page_table[:, :, None] == jnp.arange(page_count, dtype=jnp.int32)[None, None, :]
    ).astype(jnp.float32)
    context_pos = (
        jnp.arange(table_len, dtype=jnp.int32)[:, None] * page_len
        + jnp.arange(page_len, dtype=jnp.int32)[None, :]
    )
    live = (context_pos[None, :, :] < lengths[:, None, None]).astype(jnp.float32)
    count = jnp.einsum("tkp,tks->tps", page_hit, live).reshape(row_count, 1, positions)
    present = count > 0
    masked = jnp.where(present, scores, -jnp.inf)
    row_peak = jnp.max(masked, axis=2, keepdims=True)
    expons = jnp.where(present, jnp.exp(scores - row_peak), 0.0)
    total = jnp.sum(expons * count, axis=2, keepdims=True)
    probs = (expons / total).astype(jnp.bfloat16)
    weighted = (probs.astype(jnp.float32) * count).astype(jnp.bfloat16)
    latent_out = jnp.einsum("thp,pr->thr", weighted, keys_lat, preferred_element_type=jnp.float32)
    return latent_out.astype(jnp.bfloat16)


def _greet_all(me_e, me_r, groups, replicas):
    mesh_id = pl.DeviceIdType.MESH
    barrier = pltpu.get_barrier_semaphore()

    def greet(step, carry):
        pl.semaphore_signal(
            barrier, 1, device_id=(lax.rem(me_e + step, groups), me_r), device_id_type=mesh_id
        )
        return carry

    lax.fori_loop(1, groups, greet, 0)
    for step in range(1, replicas):
        pl.semaphore_signal(
            barrier, 1, device_id=(me_e, lax.rem(me_r + step, replicas)), device_id_type=mesh_id
        )
    pl.semaphore_wait(barrier, groups - 1 + replicas - 1)


def _dispatch_kernel(src_ref, out_ref, ep_send, ep_recv, local_sem, x_send, x_recv, f_send, f_recv):
    chunks, groups = src_ref.shape[:2]
    replicas = out_ref.shape[1]
    half = groups // 2
    me_e = lax.axis_index("ep")
    me_r = lax.axis_index("rep")
    right = lax.rem(me_r + 1, replicas)
    left = lax.rem(me_r + replicas - 1, replicas)
    across = lax.rem(me_r + 2, replicas)
    mesh_id = pl.DeviceIdType.MESH

    def ep_copy(c, peer, slot):
        return pltpu.make_async_remote_copy(
            src_ref.at[c, peer],
            out_ref.at[c, me_r, slot],
            ep_send.at[c, peer],
            ep_recv.at[c, slot],
            device_id=(peer, me_r),
            device_id_type=mesh_id,
        )

    def x_copy(c, side, slot):
        return pltpu.make_async_remote_copy(
            out_ref.at[c, slot],
            out_ref.at[c, slot],
            x_send.at[c, side],
            x_recv.at[c, side],
            device_id=(me_e, right if side == 0 else left),
            device_id_type=mesh_id,
        )

    def f_copy(c, side, slot, part):
        rows = pl.ds(part * half, half)
        return pltpu.make_async_remote_copy(
            out_ref.at[c, slot, rows],
            out_ref.at[c, slot, rows],
            f_send.at[c, side],
            f_recv.at[c, side],
            device_id=(me_e, right if side == 0 else left),
            device_id_type=mesh_id,
        )

    _greet_all(me_e, me_r, groups, replicas)

    locals_ = []
    for c in range(chunks):
        local = pltpu.make_async_copy(src_ref.at[c, me_e], out_ref.at[c, me_r, me_e], local_sem.at[c])
        local.start()
        locals_.append(local)

        def send(step, carry, c=c):
            ep_copy(c, lax.rem(me_e + step, groups), me_e).start()
            return carry

        lax.fori_loop(1, groups, send, 0)

    def forward(c):
        x_copy(c, 0, left).wait_recv()
        f_copy(c, 0, left, 1).start()
        x_copy(c, 1, right).wait_recv()
        f_copy(c, 1, right, 0).start()

    for c in range(chunks):
        locals_[c].wait()

        def arrive(step, carry, c=c):
            peer = lax.rem(me_e + step, groups)
            ep_copy(c, peer, peer).wait_recv()
            return carry

        lax.fori_loop(1, groups, arrive, 0)
        x_copy(c, 0, me_r).start()
        x_copy(c, 1, me_r).start()
        if c >= 1:
            forward(c - 1)
    forward(chunks - 1)

    for c in range(chunks):
        f_copy(c, 0, across, 1).wait_recv()
        f_copy(c, 1, across, 0).wait_recv()
        for side in range(2):
            x_copy(c, side, me_r).wait_send()
        f_copy(c, 0, left, 1).wait_send()
        f_copy(c, 1, right, 0).wait_send()

        def sent(step, carry, c=c):
            ep_copy(c, lax.rem(me_e + step, groups), me_e).wait_send()
            return carry

        lax.fori_loop(1, groups, sent, 0)


def dispatch(blocks, replicas):
    chunks, groups = blocks.shape[:2]
    out_shape = (chunks, replicas) + blocks.shape[1:]
    return pl.pallas_call(
        _dispatch_kernel,
        out_shape=jax.ShapeDtypeStruct(out_shape, blocks.dtype),
        in_specs=[pl.BlockSpec(memory_space=pl.ANY)],
        out_specs=pl.BlockSpec(memory_space=pl.ANY),
        scratch_shapes=[
            pltpu.SemaphoreType.DMA((chunks, groups)),
            pltpu.SemaphoreType.DMA((chunks, groups)),
            pltpu.SemaphoreType.DMA((chunks,)),
            pltpu.SemaphoreType.DMA((chunks, 2)),
            pltpu.SemaphoreType.DMA((chunks, 2)),
            pltpu.SemaphoreType.DMA((chunks, 2)),
            pltpu.SemaphoreType.DMA((chunks, 2)),
        ],
        compiler_params=pltpu.CompilerParams(collective_id=2, has_side_effects=True),
    )(blocks)


def _combine_kernel(terms_ref, out_ref, parts, sums, x_send, x_recv, x_local, ep_send, ep_recv, ep_local):
    chunks, replicas, groups = terms_ref.shape[:3]
    me_e = lax.axis_index("ep")
    me_r = lax.axis_index("rep")
    mesh_id = pl.DeviceIdType.MESH

    def x_copy(c, peer, slot):
        return pltpu.make_async_remote_copy(
            terms_ref.at[c, peer],
            parts.at[c, slot],
            x_send.at[c, peer],
            x_recv.at[c, slot],
            device_id=(me_e, peer),
            device_id_type=mesh_id,
        )

    def ep_copy(c, peer, slot):
        return pltpu.make_async_remote_copy(
            sums.at[c, peer],
            out_ref.at[c, slot],
            ep_send.at[c, peer],
            ep_recv.at[c, slot],
            device_id=(peer, me_r),
            device_id_type=mesh_id,
        )

    barrier = pltpu.get_barrier_semaphore()

    def greet(step, carry):
        pl.semaphore_signal(
            barrier, 1, device_id=(lax.rem(me_e + step, groups), me_r), device_id_type=mesh_id
        )
        return carry

    lax.fori_loop(1, groups, greet, 0)
    for step in range(1, replicas):
        pl.semaphore_signal(
            barrier, 1, device_id=(me_e, lax.rem(me_r + step, replicas)), device_id_type=mesh_id
        )
    pl.semaphore_wait(barrier, groups - 1 + replicas - 1)

    x_locals = []
    for c in range(chunks):
        local = pltpu.make_async_copy(terms_ref.at[c, me_r], parts.at[c, me_r], x_local.at[c])
        local.start()
        x_locals.append(local)
        for step in range(1, replicas):
            x_copy(c, lax.rem(me_r + step, replicas), me_r).start()

    ep_locals = []
    for c in range(chunks):
        x_locals[c].wait()
        for step in range(1, replicas):
            peer = lax.rem(me_r + step, replicas)
            x_copy(c, peer, peer).wait_recv()
        total = parts[c, 0].astype(jnp.float32)
        for source in range(1, replicas):
            total = total + parts[c, source].astype(jnp.float32)
        sums[c] = total.astype(sums.dtype)
        local = pltpu.make_async_copy(sums.at[c, me_e], out_ref.at[c, me_e], ep_local.at[c])
        local.start()
        ep_locals.append(local)

        def send(step, carry, c=c):
            ep_copy(c, lax.rem(me_e + step, groups), me_e).start()
            return carry

        lax.fori_loop(1, groups, send, 0)

    for c in range(chunks):
        for step in range(1, replicas):
            x_copy(c, lax.rem(me_r + step, replicas), me_r).wait_send()
        ep_locals[c].wait()

        def finish(step, carry, c=c):
            peer = lax.rem(me_e + step, groups)
            ep_copy(c, peer, me_e).wait_send()
            ep_copy(c, peer, peer).wait_recv()
            return carry

        lax.fori_loop(1, groups, finish, 0)


def combine_return(terms):
    chunks, replicas, groups = terms.shape[:3]
    tile = terms.shape[3:]
    return pl.pallas_call(
        _combine_kernel,
        out_shape=jax.ShapeDtypeStruct((chunks, groups) + tile, terms.dtype),
        in_specs=[pl.BlockSpec(memory_space=pl.ANY)],
        out_specs=pl.BlockSpec(memory_space=pl.ANY),
        scratch_shapes=[
            pltpu.VMEM((chunks, replicas, groups) + tile, terms.dtype),
            pltpu.VMEM((chunks, groups) + tile, terms.dtype),
            pltpu.SemaphoreType.DMA((chunks, replicas)),
            pltpu.SemaphoreType.DMA((chunks, replicas)),
            pltpu.SemaphoreType.DMA((chunks,)),
            pltpu.SemaphoreType.DMA((chunks, groups)),
            pltpu.SemaphoreType.DMA((chunks, groups)),
            pltpu.SemaphoreType.DMA((chunks,)),
        ],
        compiler_params=pltpu.CompilerParams(collective_id=3, has_side_effects=True),
    )(terms)


def _hidden_kernel(terms_ref, resid_ref, out_ref, parts, own, t_send, t_recv, t_local, h_send, h_recv, h_local):
    replicas = terms_ref.shape[0]
    me_e = lax.axis_index("ep")
    me_r = lax.axis_index("rep")
    mesh_id = pl.DeviceIdType.MESH

    def t_copy(peer, slot):
        return pltpu.make_async_remote_copy(
            terms_ref.at[peer],
            parts.at[slot],
            t_send.at[peer],
            t_recv.at[slot],
            device_id=(me_e, peer),
            device_id_type=mesh_id,
        )

    def h_copy(peer, slot):
        return pltpu.make_async_remote_copy(
            own,
            out_ref.at[slot],
            h_send.at[peer],
            h_recv.at[slot],
            device_id=(me_e, peer),
            device_id_type=mesh_id,
        )

    barrier = pltpu.get_barrier_semaphore()
    for step in range(1, replicas):
        pl.semaphore_signal(
            barrier, 1, device_id=(me_e, lax.rem(me_r + step, replicas)), device_id_type=mesh_id
        )
    pl.semaphore_wait(barrier, replicas - 1)
    local = pltpu.make_async_copy(terms_ref.at[me_r], parts.at[me_r], t_local)
    local.start()
    for step in range(1, replicas):
        t_copy(lax.rem(me_r + step, replicas), me_r).start()
    local.wait()
    for step in range(1, replicas):
        peer = lax.rem(me_r + step, replicas)
        t_copy(peer, peer).wait_recv()
    total = parts[0].astype(jnp.float32)
    for source in range(1, replicas):
        total = total + parts[source].astype(jnp.float32)
    attended = total.astype(own.dtype).astype(jnp.float32)
    rows = own.shape[0]
    block = resid_ref[pl.ds(pl.multiple_of(me_r * rows, rows), rows), :]
    own[...] = (block.astype(jnp.float32) + attended).astype(own.dtype)
    keep = pltpu.make_async_copy(own, out_ref.at[me_r], h_local)
    keep.start()
    for step in range(1, replicas):
        h_copy(lax.rem(me_r + step, replicas), me_r).start()
    for step in range(1, replicas):
        peer = lax.rem(me_r + step, replicas)
        t_copy(peer, me_r).wait_send()
        h_copy(peer, me_r).wait_send()
        h_copy(peer, peer).wait_recv()
    keep.wait()


def hidden_rows(terms, residual):
    replicas = terms.shape[0]
    block = terms.shape[1:]
    return pl.pallas_call(
        _hidden_kernel,
        out_shape=jax.ShapeDtypeStruct(terms.shape, terms.dtype),
        in_specs=[pl.BlockSpec(memory_space=pl.ANY), pl.BlockSpec(memory_space=pltpu.VMEM)],
        out_specs=pl.BlockSpec(memory_space=pl.ANY),
        scratch_shapes=[
            pltpu.VMEM(terms.shape, terms.dtype),
            pltpu.VMEM(block, terms.dtype),
            pltpu.SemaphoreType.DMA((replicas,)),
            pltpu.SemaphoreType.DMA((replicas,)),
            pltpu.SemaphoreType.DMA(()),
            pltpu.SemaphoreType.DMA((replicas,)),
            pltpu.SemaphoreType.DMA((replicas,)),
            pltpu.SemaphoreType.DMA(()),
        ],
        compiler_params=pltpu.CompilerParams(collective_id=4, has_side_effects=True),
    )(terms, residual)


def rep_exchange(blocks):
    return lax.all_to_all(blocks, "rep", split_axis=0, concat_axis=0, tiled=True)


def per_device(
    residual,
    query_latent,
    query_rope,
    cache_latent,
    cache_rope,
    page_table,
    lengths,
    value_up,
    out_proj,
    routes,
    route_weight,
    placement,
    expert_gate,
    expert_up,
    expert_down,
    shared_gate,
    shared_up,
    shared_down,
    norm_gain,
):
    replicas = lax.axis_size("rep")
    expert_groups = lax.axis_size("ep")
    rep_index = lax.axis_index("rep")
    latent_out = attend_rows(
        query_latent, query_rope, cache_latent, cache_rope, page_table, lengths
    )
    own_count = latent_out.shape[0]
    swapped = lax.all_to_all(latent_out, "rep", split_axis=1, concat_axis=0, tiled=True)
    group_rows = swapped.shape[0]
    head_out = jnp.einsum(
        "thr,hrv->thv", swapped, value_up, preferred_element_type=jnp.float32
    ).astype(jnp.bfloat16)
    attn_terms = jnp.dot(
        head_out.reshape(group_rows, -1), out_proj, preferred_element_type=jnp.float32
    )
    model_width = attn_terms.shape[1]
    hidden = hidden_rows(
        attn_terms.astype(jnp.bfloat16).reshape(replicas, own_count, model_width), residual
    ).reshape(group_rows, model_width)
    own_hidden = lax.dynamic_slice_in_dim(hidden, rep_index * own_count, own_count, 0)
    shared_act = (
        jax.nn.silu(jnp.dot(hidden, shared_gate, preferred_element_type=jnp.float32))
        * jnp.dot(hidden, shared_up, preferred_element_type=jnp.float32)
    ).astype(jnp.bfloat16)
    shared_terms = jnp.dot(shared_act, shared_down, preferred_element_type=jnp.float32)
    experts = placement.shape[0]
    route_count = routes.shape[1]
    assert experts == expert_groups and replicas == 4
    capacity = max(
        replicas, min(group_rows, 2 * group_rows * route_count // experts // replicas * replicas)
    )
    share = capacity // replicas
    expert_ids = jnp.arange(experts, dtype=jnp.int32)
    slot_index = jnp.sum(jnp.where(routes[:, :, None] == expert_ids, placement, 0), axis=2).reshape(
        -1
    )
    one_hot = (slot_index[:, None] == expert_ids[None, :]).astype(jnp.int32)
    earlier = jnp.cumsum(one_hot, axis=0) - one_hot
    position = jnp.sum(earlier * one_hot, axis=1)
    assignments = slot_index.shape[0]
    row_tag = (jnp.arange(assignments, dtype=jnp.int32) // route_count + 1).astype(jnp.float32)
    own_pos = rep_index * share + jnp.arange(share, dtype=jnp.int32)
    filled = jnp.einsum(
        "ae,ac->ce",
        one_hot.astype(jnp.float32) * row_tag[:, None],
        (position[:, None] == own_pos[None, :]).astype(jnp.float32),
        precision=lax.Precision.HIGHEST,
        preferred_element_type=jnp.float32,
    )
    own_source = jnp.where(filled > 0, filled.astype(jnp.int32) - 1, group_rows).reshape(-1)
    padded = jnp.concatenate([hidden, jnp.zeros((1, model_width), jnp.bfloat16)], axis=0)
    lanes = 128
    outgoing = padded[own_source].reshape(share, experts, model_width // lanes, lanes)
    gathered = dispatch(outgoing, replicas).reshape(share, replicas, expert_groups, model_width)
    gate_values = jnp.einsum(
        "cqgd,df->cqgf", gathered, expert_gate[0], preferred_element_type=jnp.float32
    )
    up_values = jnp.einsum(
        "cqgd,df->cqgf", gathered, expert_up[0], preferred_element_type=jnp.float32
    )
    activated = (jax.nn.silu(gate_values) * up_values).astype(jnp.bfloat16)
    expert_terms = jnp.einsum(
        "cqgf,fd->cqgd", activated, expert_down[0], preferred_element_type=jnp.float32
    ).astype(jnp.bfloat16)
    returned = combine_return(
        expert_terms.reshape(expert_terms.shape[:3] + (model_width // lanes, lanes))
    ).reshape(share * experts, model_width)
    local_pos = position - rep_index * share
    mine = (local_pos >= 0) & (local_pos < share)
    column = jnp.clip(local_pos, 0, share - 1) * experts + slot_index
    weight_used = jnp.where(mine, route_weight.reshape(-1), 0.0)
    combine = jnp.sum(
        jnp.where(
            column[:, None] == jnp.arange(experts * share, dtype=jnp.int32)[None, :],
            weight_used[:, None],
            0.0,
        ).reshape(group_rows, route_count, experts * share),
        axis=1,
    )
    routed = jnp.dot(
        combine, returned.astype(jnp.float32), precision=lax.Precision.HIGHEST,
        preferred_element_type=jnp.float32,
    )
    row_sums = jnp.sum(
        rep_exchange(
            (routed + shared_terms).astype(jnp.bfloat16).reshape(replicas, own_count, model_width)
        ).astype(jnp.float32),
        axis=0,
    )
    mixed = row_sums + own_hidden.astype(jnp.float32)
    inverse = lax.rsqrt(jnp.mean(mixed * mixed, axis=1, keepdims=True) + EPSILON)
    return (mixed * inverse * norm_gain).astype(jnp.bfloat16)


def solution(mesh):
    in_specs = (
        P("ep", None),
        P(("ep", "rep"), None),
        P(("ep", "rep"), None),
        P(("ep", "rep"), None, None),
        P(("ep", "rep"), None),
        P(("ep", "rep"), None),
        P(("ep", "rep")),
        P("rep", None, None),
        P("rep", None),
        P("ep", None),
        P("ep", None),
        P(),
        P("ep", None, "rep"),
        P("ep", None, "rep"),
        P("ep", "rep", None),
        P(None, "rep"),
        P(None, "rep"),
        P("rep", None),
        P(),
    )
    out_specs = P(("ep", "rep"), None)
    return jax.shard_map(
        per_device, mesh=mesh, in_specs=in_specs, out_specs=out_specs, check_vma=False
    )
```

```python
import functools
import math

import jax
import jax.numpy as jnp
from jax import lax
from jax.experimental import pallas as pl
from jax.experimental.pallas import tpu as pltpu
from jax.sharding import PartitionSpec as P

ROPE = 64
VHEAD = 128


EPSILON = 1e-06


def attend_rows(query_latent, query_rope, cache_latent, cache_rope, page_table, lengths):
    row_count, table_len = page_table.shape
    page_count, page_len, latent_width = cache_latent.shape
    rope_width = cache_rope.shape[1] // page_len
    head_count = query_rope.shape[1] // rope_width
    positions = page_count * page_len
    keys_lat = cache_latent.reshape(positions, latent_width)
    keys_rope = cache_rope.reshape(positions, rope_width)
    query_lat = query_latent.reshape(row_count, head_count, latent_width)
    query_rot = query_rope.reshape(row_count, head_count, rope_width)
    score_scale = 1.0 / math.sqrt(VHEAD + ROPE)
    scores = (
        jnp.einsum("thr,pr->thp", query_lat, keys_lat, preferred_element_type=jnp.float32)
        + jnp.einsum("thr,pr->thp", query_rot, keys_rope, preferred_element_type=jnp.float32)
    ) * score_scale
    page_hit = (
        page_table[:, :, None] == jnp.arange(page_count, dtype=jnp.int32)[None, None, :]
    ).astype(jnp.float32)
    context_pos = (
        jnp.arange(table_len, dtype=jnp.int32)[:, None] * page_len
        + jnp.arange(page_len, dtype=jnp.int32)[None, :]
    )
    live = (context_pos[None, :, :] < lengths[:, None, None]).astype(jnp.float32)
    count = jnp.einsum("tkp,tks->tps", page_hit, live).reshape(row_count, 1, positions)
    present = count > 0
    masked = jnp.where(present, scores, -jnp.inf)
    row_peak = jnp.max(masked, axis=2, keepdims=True)
    expons = jnp.where(present, jnp.exp(scores - row_peak), 0.0)
    total = jnp.sum(expons * count, axis=2, keepdims=True)
    probs = (expons / total).astype(jnp.bfloat16)
    weighted = (probs.astype(jnp.float32) * count).astype(jnp.bfloat16)
    latent_out = jnp.einsum("thp,pr->thr", weighted, keys_lat, preferred_element_type=jnp.float32)
    return latent_out.astype(jnp.bfloat16)


def _greet_all(me_e, me_r, groups, replicas):
    mesh_id = pl.DeviceIdType.MESH
    barrier = pltpu.get_barrier_semaphore()

    def greet(step, carry):
        pl.semaphore_signal(
            barrier, 1, device_id=(lax.rem(me_e + step, groups), me_r), device_id_type=mesh_id
        )
        return carry

    lax.fori_loop(1, groups, greet, 0)
    for step in range(1, replicas):
        pl.semaphore_signal(
            barrier, 1, device_id=(me_e, lax.rem(me_r + step, replicas)), device_id_type=mesh_id
        )
    pl.semaphore_wait(barrier, groups - 1 + replicas - 1)


def _dispatch_kernel(src_ref, out_ref, ep_send, ep_recv, local_sem, x_send, x_recv, f_send, f_recv):
    chunks, groups = src_ref.shape[:2]
    replicas = out_ref.shape[1]
    half = groups // 2
    me_e = lax.axis_index("ep")
    me_r = lax.axis_index("rep")
    right = lax.rem(me_r + 1, replicas)
    left = lax.rem(me_r + replicas - 1, replicas)
    across = lax.rem(me_r + 2, replicas)
    mesh_id = pl.DeviceIdType.MESH

    def ep_copy(c, peer, slot):
        return pltpu.make_async_remote_copy(
            src_ref.at[c, peer],
            out_ref.at[c, me_r, slot],
            ep_send.at[c, peer],
            ep_recv.at[c, slot],
            device_id=(peer, me_r),
            device_id_type=mesh_id,
        )

    def x_copy(c, side, slot):
        return pltpu.make_async_remote_copy(
            out_ref.at[c, slot],
            out_ref.at[c, slot],
            x_send.at[c, side],
            x_recv.at[c, side],
            device_id=(me_e, right if side == 0 else left),
            device_id_type=mesh_id,
        )

    def f_copy(c, side, slot, part):
        rows = pl.ds(part * half, half)
        return pltpu.make_async_remote_copy(
            out_ref.at[c, slot, rows],
            out_ref.at[c, slot, rows],
            f_send.at[c, side],
            f_recv.at[c, side],
            device_id=(me_e, right if side == 0 else left),
            device_id_type=mesh_id,
        )

    _greet_all(me_e, me_r, groups, replicas)

    locals_ = []
    for c in range(chunks):
        local = pltpu.make_async_copy(src_ref.at[c, me_e], out_ref.at[c, me_r, me_e], local_sem.at[c])
        local.start()
        locals_.append(local)

        def send(step, carry, c=c):
            ep_copy(c, lax.rem(me_e + step, groups), me_e).start()
            return carry

        lax.fori_loop(1, groups, send, 0)

    def forward(c):
        x_copy(c, 0, left).wait_recv()
        f_copy(c, 0, left, 1).start()
        x_copy(c, 1, right).wait_recv()
        f_copy(c, 1, right, 0).start()

    for c in range(chunks):
        locals_[c].wait()

        def arrive(step, carry, c=c):
            peer = lax.rem(me_e + step, groups)
            ep_copy(c, peer, peer).wait_recv()
            return carry

        lax.fori_loop(1, groups, arrive, 0)
        x_copy(c, 0, me_r).start()
        x_copy(c, 1, me_r).start()
        if c >= 1:
            forward(c - 1)
    forward(chunks - 1)

    for c in range(chunks):
        f_copy(c, 0, across, 1).wait_recv()
        f_copy(c, 1, across, 0).wait_recv()
        for side in range(2):
            x_copy(c, side, me_r).wait_send()
        f_copy(c, 0, left, 1).wait_send()
        f_copy(c, 1, right, 0).wait_send()

        def sent(step, carry, c=c):
            ep_copy(c, lax.rem(me_e + step, groups), me_e).wait_send()
            return carry

        lax.fori_loop(1, groups, sent, 0)


def dispatch(blocks, replicas):
    chunks, groups = blocks.shape[:2]
    out_shape = (chunks, replicas) + blocks.shape[1:]
    return pl.pallas_call(
        _dispatch_kernel,
        out_shape=jax.ShapeDtypeStruct(out_shape, blocks.dtype),
        in_specs=[pl.BlockSpec(memory_space=pl.ANY)],
        out_specs=pl.BlockSpec(memory_space=pl.ANY),
        scratch_shapes=[
            pltpu.SemaphoreType.DMA((chunks, groups)),
            pltpu.SemaphoreType.DMA((chunks, groups)),
            pltpu.SemaphoreType.DMA((chunks,)),
            pltpu.SemaphoreType.DMA((chunks, 2)),
            pltpu.SemaphoreType.DMA((chunks, 2)),
            pltpu.SemaphoreType.DMA((chunks, 2)),
            pltpu.SemaphoreType.DMA((chunks, 2)),
        ],
        compiler_params=pltpu.CompilerParams(collective_id=2, has_side_effects=True),
    )(blocks)


def _combine_kernel(terms_ref, out_ref, parts, sums, x_send, x_recv, x_local, ep_send, ep_recv, ep_local):
    chunks, replicas, groups = terms_ref.shape[:3]
    me_e = lax.axis_index("ep")
    me_r = lax.axis_index("rep")
    mesh_id = pl.DeviceIdType.MESH

    def x_copy(c, peer, slot):
        return pltpu.make_async_remote_copy(
            terms_ref.at[c, peer],
            parts.at[c, slot],
            x_send.at[c, peer],
            x_recv.at[c, slot],
            device_id=(me_e, peer),
            device_id_type=mesh_id,
        )

    def ep_copy(c, peer, slot):
        return pltpu.make_async_remote_copy(
            sums.at[c, peer],
            out_ref.at[c, slot],
            ep_send.at[c, peer],
            ep_recv.at[c, slot],
            device_id=(peer, me_r),
            device_id_type=mesh_id,
        )

    barrier = pltpu.get_barrier_semaphore()

    def greet(step, carry):
        pl.semaphore_signal(
            barrier, 1, device_id=(lax.rem(me_e + step, groups), me_r), device_id_type=mesh_id
        )
        return carry

    lax.fori_loop(1, groups, greet, 0)
    for step in range(1, replicas):
        pl.semaphore_signal(
            barrier, 1, device_id=(me_e, lax.rem(me_r + step, replicas)), device_id_type=mesh_id
        )
    pl.semaphore_wait(barrier, groups - 1 + replicas - 1)

    x_locals = []
    for c in range(chunks):
        local = pltpu.make_async_copy(terms_ref.at[c, me_r], parts.at[c, me_r], x_local.at[c])
        local.start()
        x_locals.append(local)
        for step in range(1, replicas):
            x_copy(c, lax.rem(me_r + step, replicas), me_r).start()

    ep_locals = []
    for c in range(chunks):
        x_locals[c].wait()
        for step in range(1, replicas):
            peer = lax.rem(me_r + step, replicas)
            x_copy(c, peer, peer).wait_recv()
        total = parts[c, 0].astype(jnp.float32)
        for source in range(1, replicas):
            total = total + parts[c, source].astype(jnp.float32)
        sums[c] = total.reshape(sums.shape[1:]).astype(sums.dtype)
        local = pltpu.make_async_copy(sums.at[c, me_e], out_ref.at[c, me_e], ep_local.at[c])
        local.start()
        ep_locals.append(local)

        def send(step, carry, c=c):
            ep_copy(c, lax.rem(me_e + step, groups), me_e).start()
            return carry

        lax.fori_loop(1, groups, send, 0)

    for c in range(chunks):
        for step in range(1, replicas):
            x_copy(c, lax.rem(me_r + step, replicas), me_r).wait_send()
        ep_locals[c].wait()

        def finish(step, carry, c=c):
            peer = lax.rem(me_e + step, groups)
            ep_copy(c, peer, me_e).wait_send()
            ep_copy(c, peer, peer).wait_recv()
            return carry

        lax.fori_loop(1, groups, finish, 0)


def combine_return(terms):
    chunks, replicas, groups, width = terms.shape
    lanes = 128
    tile = (width // lanes, lanes)
    return pl.pallas_call(
        _combine_kernel,
        out_shape=jax.ShapeDtypeStruct((chunks, groups) + tile, terms.dtype),
        in_specs=[pl.BlockSpec(memory_space=pl.ANY)],
        out_specs=pl.BlockSpec(memory_space=pl.ANY),
        scratch_shapes=[
            pltpu.VMEM(terms.shape, terms.dtype),
            pltpu.VMEM((chunks, groups) + tile, terms.dtype),
            pltpu.SemaphoreType.DMA((chunks, replicas)),
            pltpu.SemaphoreType.DMA((chunks, replicas)),
            pltpu.SemaphoreType.DMA((chunks,)),
            pltpu.SemaphoreType.DMA((chunks, groups)),
            pltpu.SemaphoreType.DMA((chunks, groups)),
            pltpu.SemaphoreType.DMA((chunks,)),
        ],
        compiler_params=pltpu.CompilerParams(collective_id=3, has_side_effects=True),
    )(terms)


def _hidden_kernel(terms_ref, resid_ref, out_ref, parts, own, t_send, t_recv, t_local, h_send, h_recv, h_local):
    replicas = terms_ref.shape[0]
    me_e = lax.axis_index("ep")
    me_r = lax.axis_index("rep")
    mesh_id = pl.DeviceIdType.MESH

    def t_copy(peer, slot):
        return pltpu.make_async_remote_copy(
            terms_ref.at[peer],
            parts.at[slot],
            t_send.at[peer],
            t_recv.at[slot],
            device_id=(me_e, peer),
            device_id_type=mesh_id,
        )

    def h_copy(peer, slot):
        return pltpu.make_async_remote_copy(
            own,
            out_ref.at[slot],
            h_send.at[peer],
            h_recv.at[slot],
            device_id=(me_e, peer),
            device_id_type=mesh_id,
        )

    barrier = pltpu.get_barrier_semaphore()
    for step in range(1, replicas):
        pl.semaphore_signal(
            barrier, 1, device_id=(me_e, lax.rem(me_r + step, replicas)), device_id_type=mesh_id
        )
    pl.semaphore_wait(barrier, replicas - 1)
    local = pltpu.make_async_copy(terms_ref.at[me_r], parts.at[me_r], t_local)
    local.start()
    for step in range(1, replicas):
        t_copy(lax.rem(me_r + step, replicas), me_r).start()
    local.wait()
    for step in range(1, replicas):
        peer = lax.rem(me_r + step, replicas)
        t_copy(peer, peer).wait_recv()
    total = parts[0].astype(jnp.float32)
    for source in range(1, replicas):
        total = total + parts[source].astype(jnp.float32)
    attended = total.astype(own.dtype).astype(jnp.float32)
    own[...] = (resid_ref[...].astype(jnp.float32) + attended).astype(own.dtype)
    keep = pltpu.make_async_copy(own, out_ref.at[me_r], h_local)
    keep.start()
    for step in range(1, replicas):
        h_copy(lax.rem(me_r + step, replicas), me_r).start()
    for step in range(1, replicas):
        peer = lax.rem(me_r + step, replicas)
        t_copy(peer, me_r).wait_send()
        h_copy(peer, me_r).wait_send()
        h_copy(peer, peer).wait_recv()
    keep.wait()


def hidden_rows(terms, residual_block):
    replicas = terms.shape[0]
    block = terms.shape[1:]
    return pl.pallas_call(
        _hidden_kernel,
        out_shape=jax.ShapeDtypeStruct(terms.shape, terms.dtype),
        in_specs=[pl.BlockSpec(memory_space=pl.ANY), pl.BlockSpec(memory_space=pltpu.VMEM)],
        out_specs=pl.BlockSpec(memory_space=pl.ANY),
        scratch_shapes=[
            pltpu.VMEM(terms.shape, terms.dtype),
            pltpu.VMEM(block, terms.dtype),
            pltpu.SemaphoreType.DMA((replicas,)),
            pltpu.SemaphoreType.DMA((replicas,)),
            pltpu.SemaphoreType.DMA(()),
            pltpu.SemaphoreType.DMA((replicas,)),
            pltpu.SemaphoreType.DMA((replicas,)),
            pltpu.SemaphoreType.DMA(()),
        ],
        compiler_params=pltpu.CompilerParams(collective_id=4, has_side_effects=True),
    )(terms, residual_block)


def rep_exchange(blocks):
    return lax.all_to_all(blocks, "rep", split_axis=0, concat_axis=0, tiled=True)


def per_device(
    residual,
    query_latent,
    query_rope,
    cache_latent,
    cache_rope,
    page_table,
    lengths,
    value_up,
    out_proj,
    routes,
    route_weight,
    placement,
    expert_gate,
    expert_up,
    expert_down,
    shared_gate,
    shared_up,
    shared_down,
    norm_gain,
):
    replicas = lax.axis_size("rep")
    expert_groups = lax.axis_size("ep")
    rep_index = lax.axis_index("rep")
    latent_out = attend_rows(
        query_latent, query_rope, cache_latent, cache_rope, page_table, lengths
    )
    own_count = latent_out.shape[0]
    swapped = lax.all_to_all(latent_out, "rep", split_axis=1, concat_axis=0, tiled=True)
    group_rows = swapped.shape[0]
    head_out = jnp.einsum(
        "thr,hrv->thv", swapped, value_up, preferred_element_type=jnp.float32
    ).astype(jnp.bfloat16)
    attn_terms = jnp.dot(
        head_out.reshape(group_rows, -1), out_proj, preferred_element_type=jnp.float32
    )
    model_width = attn_terms.shape[1]
    own_residual = lax.dynamic_slice_in_dim(residual, rep_index * own_count, own_count, 0)
    hidden = hidden_rows(
        attn_terms.astype(jnp.bfloat16).reshape(replicas, own_count, model_width), own_residual
    ).reshape(group_rows, model_width)
    own_hidden = lax.dynamic_slice_in_dim(hidden, rep_index * own_count, own_count, 0)
    shared_act = (
        jax.nn.silu(jnp.dot(hidden, shared_gate, preferred_element_type=jnp.float32))
        * jnp.dot(hidden, shared_up, preferred_element_type=jnp.float32)
    ).astype(jnp.bfloat16)
    shared_terms = jnp.dot(shared_act, shared_down, preferred_element_type=jnp.float32)
    experts = placement.shape[0]
    route_count = routes.shape[1]
    assert experts == expert_groups and replicas == 4
    capacity = max(
        replicas, min(group_rows, 2 * group_rows * route_count // experts // replicas * replicas)
    )
    share = capacity // replicas
    expert_ids = jnp.arange(experts, dtype=jnp.int32)
    slot_index = jnp.sum(jnp.where(routes[:, :, None] == expert_ids, placement, 0), axis=2).reshape(
        -1
    )
    one_hot = (slot_index[:, None] == expert_ids[None, :]).astype(jnp.int32)
    earlier = jnp.cumsum(one_hot, axis=0) - one_hot
    position = jnp.sum(earlier * one_hot, axis=1)
    assignments = slot_index.shape[0]
    row_tag = (jnp.arange(assignments, dtype=jnp.int32) // route_count + 1).astype(jnp.float32)
    own_pos = rep_index * share + jnp.arange(share, dtype=jnp.int32)
    filled = jnp.einsum(
        "ae,ac->ce",
        one_hot.astype(jnp.float32) * row_tag[:, None],
        (position[:, None] == own_pos[None, :]).astype(jnp.float32),
        precision=lax.Precision.HIGHEST,
        preferred_element_type=jnp.float32,
    )
    own_source = jnp.where(filled > 0, filled.astype(jnp.int32) - 1, group_rows).reshape(-1)
    padded = jnp.concatenate([hidden, jnp.zeros((1, model_width), jnp.bfloat16)], axis=0)
    lanes = 128
    outgoing = padded[own_source].reshape(share, experts, model_width // lanes, lanes)
    gathered = dispatch(outgoing, replicas).reshape(share, replicas, expert_groups, model_width)
    gate_values = jnp.einsum(
        "cqgd,df->cqgf", gathered, expert_gate[0], preferred_element_type=jnp.float32
    )
    up_values = jnp.einsum(
        "cqgd,df->cqgf", gathered, expert_up[0], preferred_element_type=jnp.float32
    )
    activated = (jax.nn.silu(gate_values) * up_values).astype(jnp.bfloat16)
    expert_terms = jnp.einsum(
        "cqgf,fd->cqgd", activated, expert_down[0], preferred_element_type=jnp.float32
    ).astype(jnp.bfloat16)
    returned = combine_return(expert_terms).reshape(share * experts, model_width)
    local_pos = position - rep_index * share
    mine = (local_pos >= 0) & (local_pos < share)
    column = jnp.clip(local_pos, 0, share - 1) * experts + slot_index
    weight_used = jnp.where(mine, route_weight.reshape(-1), 0.0)
    combine = jnp.sum(
        jnp.where(
            column[:, None] == jnp.arange(experts * share, dtype=jnp.int32)[None, :],
            weight_used[:, None],
            0.0,
        ).reshape(group_rows, route_count, experts * share),
        axis=1,
    )
    routed = jnp.dot(
        combine, returned.astype(jnp.float32), precision=lax.Precision.HIGHEST,
        preferred_element_type=jnp.float32,
    )
    row_sums = jnp.sum(
        rep_exchange(
            (routed + shared_terms).astype(jnp.bfloat16).reshape(replicas, own_count, model_width)
        ).astype(jnp.float32),
        axis=0,
    )
    mixed = row_sums + own_hidden.astype(jnp.float32)
    inverse = lax.rsqrt(jnp.mean(mixed * mixed, axis=1, keepdims=True) + EPSILON)
    return (mixed * inverse * norm_gain).astype(jnp.bfloat16)


def solution(mesh):
    in_specs = (
        P("ep", None),
        P(("ep", "rep"), None),
        P(("ep", "rep"), None),
        P(("ep", "rep"), None, None),
        P(("ep", "rep"), None),
        P(("ep", "rep"), None),
        P(("ep", "rep")),
        P("rep", None, None),
        P("rep", None),
        P("ep", None),
        P("ep", None),
        P(),
        P("ep", None, "rep"),
        P("ep", None, "rep"),
        P("ep", "rep", None),
        P(None, "rep"),
        P(None, "rep"),
        P("rep", None),
        P(),
    )
    out_specs = P(("ep", "rep"), None)
    return jax.shard_map(
        per_device, mesh=mesh, in_specs=in_specs, out_specs=out_specs, check_vma=False
    )
```

```python
import functools
import math

import jax
import jax.numpy as jnp
from jax import lax
from jax.experimental import pallas as pl
from jax.experimental.pallas import tpu as pltpu
from jax.sharding import PartitionSpec as P

ROPE = 64
VHEAD = 128


EPSILON = 1e-06


def attend_rows(query_latent, query_rope, cache_latent, cache_rope, page_table, lengths):
    row_count, table_len = page_table.shape
    page_count, page_len, latent_width = cache_latent.shape
    rope_width = cache_rope.shape[1] // page_len
    head_count = query_rope.shape[1] // rope_width
    positions = page_count * page_len
    keys_lat = cache_latent.reshape(positions, latent_width)
    keys_rope = cache_rope.reshape(positions, rope_width)
    query_lat = query_latent.reshape(row_count, head_count, latent_width)
    query_rot = query_rope.reshape(row_count, head_count, rope_width)
    score_scale = 1.0 / math.sqrt(VHEAD + ROPE)
    scores = (
        jnp.einsum("thr,pr->thp", query_lat, keys_lat, preferred_element_type=jnp.float32)
        + jnp.einsum("thr,pr->thp", query_rot, keys_rope, preferred_element_type=jnp.float32)
    ) * score_scale
    page_hit = (
        page_table[:, :, None] == jnp.arange(page_count, dtype=jnp.int32)[None, None, :]
    ).astype(jnp.float32)
    context_pos = (
        jnp.arange(table_len, dtype=jnp.int32)[:, None] * page_len
        + jnp.arange(page_len, dtype=jnp.int32)[None, :]
    )
    live = (context_pos[None, :, :] < lengths[:, None, None]).astype(jnp.float32)
    count = jnp.einsum("tkp,tks->tps", page_hit, live).reshape(row_count, 1, positions)
    present = count > 0
    masked = jnp.where(present, scores, -jnp.inf)
    row_peak = jnp.max(masked, axis=2, keepdims=True)
    expons = jnp.where(present, jnp.exp(scores - row_peak), 0.0)
    total = jnp.sum(expons * count, axis=2, keepdims=True)
    probs = (expons / total).astype(jnp.bfloat16)
    weighted = (probs.astype(jnp.float32) * count).astype(jnp.bfloat16)
    latent_out = jnp.einsum("thp,pr->thr", weighted, keys_lat, preferred_element_type=jnp.float32)
    return latent_out.astype(jnp.bfloat16)


def _greet_all(me_e, me_r, groups, replicas):
    mesh_id = pl.DeviceIdType.MESH
    barrier = pltpu.get_barrier_semaphore()

    def greet(step, carry):
        pl.semaphore_signal(
            barrier, 1, device_id=(lax.rem(me_e + step, groups), me_r), device_id_type=mesh_id
        )
        return carry

    lax.fori_loop(1, groups, greet, 0)
    for step in range(1, replicas):
        pl.semaphore_signal(
            barrier, 1, device_id=(me_e, lax.rem(me_r + step, replicas)), device_id_type=mesh_id
        )
    pl.semaphore_wait(barrier, groups - 1 + replicas - 1)


def _dispatch_kernel(src_ref, out_ref, land, ep_send, ep_recv, local_sem, x_send, x_recv, f_send, f_recv):
    chunks, groups = src_ref.shape[:2]
    replicas = land.shape[1]
    half = groups // 2
    me_e = lax.axis_index("ep")
    me_r = lax.axis_index("rep")
    right = lax.rem(me_r + 1, replicas)
    left = lax.rem(me_r + replicas - 1, replicas)
    across = lax.rem(me_r + 2, replicas)
    mesh_id = pl.DeviceIdType.MESH

    def ep_copy(c, peer, slot):
        return pltpu.make_async_remote_copy(
            src_ref.at[c, peer],
            land.at[c, me_r, slot],
            ep_send.at[c, peer],
            ep_recv.at[c, slot],
            device_id=(peer, me_r),
            device_id_type=mesh_id,
        )

    def x_copy(c, side, slot):
        return pltpu.make_async_remote_copy(
            land.at[c, slot],
            land.at[c, slot],
            x_send.at[c, side],
            x_recv.at[c, side],
            device_id=(me_e, right if side == 0 else left),
            device_id_type=mesh_id,
        )

    def f_copy(c, side, slot, part):
        rows = pl.ds(part * half, half)
        return pltpu.make_async_remote_copy(
            land.at[c, slot, rows],
            land.at[c, slot, rows],
            f_send.at[c, side],
            f_recv.at[c, side],
            device_id=(me_e, right if side == 0 else left),
            device_id_type=mesh_id,
        )

    _greet_all(me_e, me_r, groups, replicas)

    locals_ = []
    for c in range(chunks):
        local = pltpu.make_async_copy(src_ref.at[c, me_e], land.at[c, me_r, me_e], local_sem.at[c])
        local.start()
        locals_.append(local)

        def send(step, carry, c=c):
            ep_copy(c, lax.rem(me_e + step, groups), me_e).start()
            return carry

        lax.fori_loop(1, groups, send, 0)

    def forward(c):
        x_copy(c, 0, left).wait_recv()
        f_copy(c, 0, left, 1).start()
        x_copy(c, 1, right).wait_recv()
        f_copy(c, 1, right, 0).start()

    for c in range(chunks):
        locals_[c].wait()

        def arrive(step, carry, c=c):
            peer = lax.rem(me_e + step, groups)
            ep_copy(c, peer, peer).wait_recv()
            return carry

        lax.fori_loop(1, groups, arrive, 0)
        x_copy(c, 0, me_r).start()
        x_copy(c, 1, me_r).start()
        if c >= 1:
            forward(c - 1)
    forward(chunks - 1)

    for c in range(chunks):
        f_copy(c, 0, across, 1).wait_recv()
        f_copy(c, 1, across, 0).wait_recv()
        for slot in range(replicas):
            out_ref[c, slot] = land[c, slot].reshape(out_ref.shape[2:])
        for side in range(2):
            x_copy(c, side, me_r).wait_send()
        f_copy(c, 0, left, 1).wait_send()
        f_copy(c, 1, right, 0).wait_send()

        def sent(step, carry, c=c):
            ep_copy(c, lax.rem(me_e + step, groups), me_e).wait_send()
            return carry

        lax.fori_loop(1, groups, sent, 0)


def dispatch(blocks, replicas):
    chunks, groups = blocks.shape[:2]
    tile = blocks.shape[2:]
    out_shape = (chunks, replicas, groups, tile[0] * tile[1])
    return pl.pallas_call(
        _dispatch_kernel,
        out_shape=jax.ShapeDtypeStruct(out_shape, blocks.dtype),
        in_specs=[pl.BlockSpec(memory_space=pl.ANY)],
        out_specs=pl.BlockSpec(memory_space=pltpu.VMEM),
        scratch_shapes=[
            pltpu.VMEM((chunks, replicas) + blocks.shape[1:], blocks.dtype),
            pltpu.SemaphoreType.DMA((chunks, groups)),
            pltpu.SemaphoreType.DMA((chunks, groups)),
            pltpu.SemaphoreType.DMA((chunks,)),
            pltpu.SemaphoreType.DMA((chunks, 2)),
            pltpu.SemaphoreType.DMA((chunks, 2)),
            pltpu.SemaphoreType.DMA((chunks, 2)),
            pltpu.SemaphoreType.DMA((chunks, 2)),
        ],
        compiler_params=pltpu.CompilerParams(collective_id=2, has_side_effects=True),
    )(blocks)


def _combine_kernel(terms_ref, out_ref, parts, sums, x_send, x_recv, x_local, ep_send, ep_recv, ep_local):
    chunks, replicas, groups = terms_ref.shape[:3]
    me_e = lax.axis_index("ep")
    me_r = lax.axis_index("rep")
    mesh_id = pl.DeviceIdType.MESH

    def x_copy(c, peer, slot):
        return pltpu.make_async_remote_copy(
            terms_ref.at[c, peer],
            parts.at[c, slot],
            x_send.at[c, peer],
            x_recv.at[c, slot],
            device_id=(me_e, peer),
            device_id_type=mesh_id,
        )

    def ep_copy(c, peer, slot):
        return pltpu.make_async_remote_copy(
            sums.at[c, peer],
            out_ref.at[c, slot],
            ep_send.at[c, peer],
            ep_recv.at[c, slot],
            device_id=(peer, me_r),
            device_id_type=mesh_id,
        )

    barrier = pltpu.get_barrier_semaphore()

    def greet(step, carry):
        pl.semaphore_signal(
            barrier, 1, device_id=(lax.rem(me_e + step, groups), me_r), device_id_type=mesh_id
        )
        return carry

    lax.fori_loop(1, groups, greet, 0)
    for step in range(1, replicas):
        pl.semaphore_signal(
            barrier, 1, device_id=(me_e, lax.rem(me_r + step, replicas)), device_id_type=mesh_id
        )
    pl.semaphore_wait(barrier, groups - 1 + replicas - 1)

    x_locals = []
    for c in range(chunks):
        local = pltpu.make_async_copy(terms_ref.at[c, me_r], parts.at[c, me_r], x_local.at[c])
        local.start()
        x_locals.append(local)
        for step in range(1, replicas):
            x_copy(c, lax.rem(me_r + step, replicas), me_r).start()

    ep_locals = []
    for c in range(chunks):
        x_locals[c].wait()
        for step in range(1, replicas):
            peer = lax.rem(me_r + step, replicas)
            x_copy(c, peer, peer).wait_recv()
        total = parts[c, 0].astype(jnp.float32)
        for source in range(1, replicas):
            total = total + parts[c, source].astype(jnp.float32)
        sums[c] = total.reshape(sums.shape[1:]).astype(sums.dtype)
        local = pltpu.make_async_copy(sums.at[c, me_e], out_ref.at[c, me_e], ep_local.at[c])
        local.start()
        ep_locals.append(local)

        def send(step, carry, c=c):
            ep_copy(c, lax.rem(me_e + step, groups), me_e).start()
            return carry

        lax.fori_loop(1, groups, send, 0)

    for c in range(chunks):
        for step in range(1, replicas):
            x_copy(c, lax.rem(me_r + step, replicas), me_r).wait_send()
        ep_locals[c].wait()

        def finish(step, carry, c=c):
            peer = lax.rem(me_e + step, groups)
            ep_copy(c, peer, me_e).wait_send()
            ep_copy(c, peer, peer).wait_recv()
            return carry

        lax.fori_loop(1, groups, finish, 0)


def combine_return(terms):
    chunks, replicas, groups, width = terms.shape
    lanes = 128
    tile = (width // lanes, lanes)
    return pl.pallas_call(
        _combine_kernel,
        out_shape=jax.ShapeDtypeStruct((chunks, groups) + tile, terms.dtype),
        in_specs=[pl.BlockSpec(memory_space=pl.ANY)],
        out_specs=pl.BlockSpec(memory_space=pl.ANY),
        scratch_shapes=[
            pltpu.VMEM(terms.shape, terms.dtype),
            pltpu.VMEM((chunks, groups) + tile, terms.dtype),
            pltpu.SemaphoreType.DMA((chunks, replicas)),
            pltpu.SemaphoreType.DMA((chunks, replicas)),
            pltpu.SemaphoreType.DMA((chunks,)),
            pltpu.SemaphoreType.DMA((chunks, groups)),
            pltpu.SemaphoreType.DMA((chunks, groups)),
            pltpu.SemaphoreType.DMA((chunks,)),
        ],
        compiler_params=pltpu.CompilerParams(collective_id=3, has_side_effects=True),
    )(terms)


def _hidden_kernel(terms_ref, resid_ref, out_ref, parts, own, t_send, t_recv, t_local, h_send, h_recv, h_local):
    replicas = terms_ref.shape[0]
    me_e = lax.axis_index("ep")
    me_r = lax.axis_index("rep")
    mesh_id = pl.DeviceIdType.MESH

    def t_copy(peer, slot):
        return pltpu.make_async_remote_copy(
            terms_ref.at[peer],
            parts.at[slot],
            t_send.at[peer],
            t_recv.at[slot],
            device_id=(me_e, peer),
            device_id_type=mesh_id,
        )

    def h_copy(peer, slot):
        return pltpu.make_async_remote_copy(
            own,
            out_ref.at[slot],
            h_send.at[peer],
            h_recv.at[slot],
            device_id=(me_e, peer),
            device_id_type=mesh_id,
        )

    barrier = pltpu.get_barrier_semaphore()
    for step in range(1, replicas):
        pl.semaphore_signal(
            barrier, 1, device_id=(me_e, lax.rem(me_r + step, replicas)), device_id_type=mesh_id
        )
    pl.semaphore_wait(barrier, replicas - 1)
    local = pltpu.make_async_copy(terms_ref.at[me_r], parts.at[me_r], t_local)
    local.start()
    for step in range(1, replicas):
        t_copy(lax.rem(me_r + step, replicas), me_r).start()
    local.wait()
    for step in range(1, replicas):
        peer = lax.rem(me_r + step, replicas)
        t_copy(peer, peer).wait_recv()
    total = parts[0].astype(jnp.float32)
    for source in range(1, replicas):
        total = total + parts[source].astype(jnp.float32)
    attended = total.astype(own.dtype).astype(jnp.float32)
    own[...] = (resid_ref[...].astype(jnp.float32) + attended).astype(own.dtype)
    keep = pltpu.make_async_copy(own, out_ref.at[me_r], h_local)
    keep.start()
    for step in range(1, replicas):
        h_copy(lax.rem(me_r + step, replicas), me_r).start()
    for step in range(1, replicas):
        peer = lax.rem(me_r + step, replicas)
        t_copy(peer, me_r).wait_send()
        h_copy(peer, me_r).wait_send()
        h_copy(peer, peer).wait_recv()
    keep.wait()


def hidden_rows(terms, residual_block):
    replicas = terms.shape[0]
    block = terms.shape[1:]
    return pl.pallas_call(
        _hidden_kernel,
        out_shape=jax.ShapeDtypeStruct(terms.shape, terms.dtype),
        in_specs=[pl.BlockSpec(memory_space=pl.ANY), pl.BlockSpec(memory_space=pltpu.VMEM)],
        out_specs=pl.BlockSpec(memory_space=pl.ANY),
        scratch_shapes=[
            pltpu.VMEM(terms.shape, terms.dtype),
            pltpu.VMEM(block, terms.dtype),
            pltpu.SemaphoreType.DMA((replicas,)),
            pltpu.SemaphoreType.DMA((replicas,)),
            pltpu.SemaphoreType.DMA(()),
            pltpu.SemaphoreType.DMA((replicas,)),
            pltpu.SemaphoreType.DMA((replicas,)),
            pltpu.SemaphoreType.DMA(()),
        ],
        compiler_params=pltpu.CompilerParams(collective_id=4, has_side_effects=True),
    )(terms, residual_block)


def rep_exchange(blocks):
    return lax.all_to_all(blocks, "rep", split_axis=0, concat_axis=0, tiled=True)


def per_device(
    residual,
    query_latent,
    query_rope,
    cache_latent,
    cache_rope,
    page_table,
    lengths,
    value_up,
    out_proj,
    routes,
    route_weight,
    placement,
    expert_gate,
    expert_up,
    expert_down,
    shared_gate,
    shared_up,
    shared_down,
    norm_gain,
):
    replicas = lax.axis_size("rep")
    expert_groups = lax.axis_size("ep")
    rep_index = lax.axis_index("rep")
    latent_out = attend_rows(
        query_latent, query_rope, cache_latent, cache_rope, page_table, lengths
    )
    own_count = latent_out.shape[0]
    swapped = lax.all_to_all(latent_out, "rep", split_axis=1, concat_axis=0, tiled=True)
    group_rows = swapped.shape[0]
    head_out = jnp.einsum(
        "thr,hrv->thv", swapped, value_up, preferred_element_type=jnp.float32
    ).astype(jnp.bfloat16)
    attn_terms = jnp.dot(
        head_out.reshape(group_rows, -1), out_proj, preferred_element_type=jnp.float32
    )
    model_width = attn_terms.shape[1]
    own_residual = lax.dynamic_slice_in_dim(residual, rep_index * own_count, own_count, 0)
    hidden = hidden_rows(
        attn_terms.astype(jnp.bfloat16).reshape(replicas, own_count, model_width), own_residual
    ).reshape(group_rows, model_width)
    own_hidden = lax.dynamic_slice_in_dim(hidden, rep_index * own_count, own_count, 0)
    shared_act = (
        jax.nn.silu(jnp.dot(hidden, shared_gate, preferred_element_type=jnp.float32))
        * jnp.dot(hidden, shared_up, preferred_element_type=jnp.float32)
    ).astype(jnp.bfloat16)
    shared_terms = jnp.dot(shared_act, shared_down, preferred_element_type=jnp.float32)
    experts = placement.shape[0]
    route_count = routes.shape[1]
    assert experts == expert_groups and replicas == 4
    capacity = max(
        replicas, min(group_rows, 2 * group_rows * route_count // experts // replicas * replicas)
    )
    share = capacity // replicas
    expert_ids = jnp.arange(experts, dtype=jnp.int32)
    slot_index = jnp.sum(jnp.where(routes[:, :, None] == expert_ids, placement, 0), axis=2).reshape(
        -1
    )
    one_hot = (slot_index[:, None] == expert_ids[None, :]).astype(jnp.int32)
    earlier = jnp.cumsum(one_hot, axis=0) - one_hot
    position = jnp.sum(earlier * one_hot, axis=1)
    assignments = slot_index.shape[0]
    row_tag = (jnp.arange(assignments, dtype=jnp.int32) // route_count + 1).astype(jnp.float32)
    own_pos = rep_index * share + jnp.arange(share, dtype=jnp.int32)
    filled = jnp.einsum(
        "ae,ac->ce",
        one_hot.astype(jnp.float32) * row_tag[:, None],
        (position[:, None] == own_pos[None, :]).astype(jnp.float32),
        precision=lax.Precision.HIGHEST,
        preferred_element_type=jnp.float32,
    )
    own_source = jnp.where(filled > 0, filled.astype(jnp.int32) - 1, group_rows).reshape(-1)
    padded = jnp.concatenate([hidden, jnp.zeros((1, model_width), jnp.bfloat16)], axis=0)
    lanes = 128
    outgoing = padded[own_source].reshape(share, experts, model_width // lanes, lanes)
    gathered = dispatch(outgoing, replicas)
    gate_values = jnp.einsum(
        "cqgd,df->cqgf", gathered, expert_gate[0], preferred_element_type=jnp.float32
    )
    up_values = jnp.einsum(
        "cqgd,df->cqgf", gathered, expert_up[0], preferred_element_type=jnp.float32
    )
    activated = (jax.nn.silu(gate_values) * up_values).astype(jnp.bfloat16)
    expert_terms = jnp.einsum(
        "cqgf,fd->cqgd", activated, expert_down[0], preferred_element_type=jnp.float32
    ).astype(jnp.bfloat16)
    returned = combine_return(expert_terms).reshape(share * experts, model_width)
    local_pos = position - rep_index * share
    mine = (local_pos >= 0) & (local_pos < share)
    column = jnp.clip(local_pos, 0, share - 1) * experts + slot_index
    weight_used = jnp.where(mine, route_weight.reshape(-1), 0.0)
    combine = jnp.sum(
        jnp.where(
            column[:, None] == jnp.arange(experts * share, dtype=jnp.int32)[None, :],
            weight_used[:, None],
            0.0,
        ).reshape(group_rows, route_count, experts * share),
        axis=1,
    )
    routed = jnp.dot(
        combine, returned.astype(jnp.float32), precision=lax.Precision.HIGHEST,
        preferred_element_type=jnp.float32,
    )
    row_sums = jnp.sum(
        rep_exchange(
            (routed + shared_terms).astype(jnp.bfloat16).reshape(replicas, own_count, model_width)
        ).astype(jnp.float32),
        axis=0,
    )
    mixed = row_sums + own_hidden.astype(jnp.float32)
    inverse = lax.rsqrt(jnp.mean(mixed * mixed, axis=1, keepdims=True) + EPSILON)
    return (mixed * inverse * norm_gain).astype(jnp.bfloat16)


def solution(mesh):
    in_specs = (
        P("ep", None),
        P(("ep", "rep"), None),
        P(("ep", "rep"), None),
        P(("ep", "rep"), None, None),
        P(("ep", "rep"), None),
        P(("ep", "rep"), None),
        P(("ep", "rep")),
        P("rep", None, None),
        P("rep", None),
        P("ep", None),
        P("ep", None),
        P(),
        P("ep", None, "rep"),
        P("ep", None, "rep"),
        P("ep", "rep", None),
        P(None, "rep"),
        P(None, "rep"),
        P("rep", None),
        P(),
    )
    out_specs = P(("ep", "rep"), None)
    return jax.shard_map(
        per_device, mesh=mesh, in_specs=in_specs, out_specs=out_specs, check_vma=False
    )
```

```python
import functools
import math

import jax
import jax.numpy as jnp
from jax import lax
from jax.experimental import pallas as pl
from jax.experimental.pallas import tpu as pltpu
from jax.sharding import PartitionSpec as P

ROPE = 64
VHEAD = 128


EPSILON = 1e-06


def attend_rows(query_latent, query_rope, cache_latent, cache_rope, page_table, lengths):
    row_count, table_len = page_table.shape
    page_count, page_len, latent_width = cache_latent.shape
    rope_width = cache_rope.shape[1] // page_len
    head_count = query_rope.shape[1] // rope_width
    positions = page_count * page_len
    keys_lat = cache_latent.reshape(positions, latent_width)
    keys_rope = cache_rope.reshape(positions, rope_width)
    query_lat = query_latent.reshape(row_count, head_count, latent_width)
    query_rot = query_rope.reshape(row_count, head_count, rope_width)
    score_scale = 1.0 / math.sqrt(VHEAD + ROPE)
    scores = (
        jnp.einsum("thr,pr->thp", query_lat, keys_lat, preferred_element_type=jnp.float32)
        + jnp.einsum("thr,pr->thp", query_rot, keys_rope, preferred_element_type=jnp.float32)
    ) * score_scale
    page_hit = (
        page_table[:, :, None] == jnp.arange(page_count, dtype=jnp.int32)[None, None, :]
    ).astype(jnp.float32)
    context_pos = (
        jnp.arange(table_len, dtype=jnp.int32)[:, None] * page_len
        + jnp.arange(page_len, dtype=jnp.int32)[None, :]
    )
    live = (context_pos[None, :, :] < lengths[:, None, None]).astype(jnp.float32)
    count = jnp.einsum("tkp,tks->tps", page_hit, live).reshape(row_count, 1, positions)
    present = count > 0
    masked = jnp.where(present, scores, -jnp.inf)
    row_peak = jnp.max(masked, axis=2, keepdims=True)
    expons = jnp.where(present, jnp.exp(scores - row_peak), 0.0)
    total = jnp.sum(expons * count, axis=2, keepdims=True)
    probs = (expons / total).astype(jnp.bfloat16)
    weighted = (probs.astype(jnp.float32) * count).astype(jnp.bfloat16)
    latent_out = jnp.einsum("thp,pr->thr", weighted, keys_lat, preferred_element_type=jnp.float32)
    return latent_out.astype(jnp.bfloat16)


def _greet_all(me_e, me_r, groups, replicas):
    mesh_id = pl.DeviceIdType.MESH
    barrier = pltpu.get_barrier_semaphore()

    def greet(step, carry):
        pl.semaphore_signal(
            barrier, 1, device_id=(lax.rem(me_e + step, groups), me_r), device_id_type=mesh_id
        )
        return carry

    lax.fori_loop(1, groups, greet, 0)
    for step in range(1, replicas):
        pl.semaphore_signal(
            barrier, 1, device_id=(me_e, lax.rem(me_r + step, replicas)), device_id_type=mesh_id
        )
    pl.semaphore_wait(barrier, groups - 1 + replicas - 1)


def _dispatch_kernel(src_ref, out_ref, land, ep_send, ep_recv, local_sem, x_send, x_recv, f_send, f_recv):
    chunks, groups = src_ref.shape[:2]
    replicas = land.shape[1]
    half = groups // 2
    me_e = lax.axis_index("ep")
    me_r = lax.axis_index("rep")
    right = lax.rem(me_r + 1, replicas)
    left = lax.rem(me_r + replicas - 1, replicas)
    across = lax.rem(me_r + 2, replicas)
    mesh_id = pl.DeviceIdType.MESH

    def ep_copy(c, peer, slot):
        return pltpu.make_async_remote_copy(
            src_ref.at[c, peer],
            land.at[c, me_r, slot],
            ep_send.at[c, peer],
            ep_recv.at[c, slot],
            device_id=(peer, me_r),
            device_id_type=mesh_id,
        )

    def x_copy(c, side, slot):
        return pltpu.make_async_remote_copy(
            land.at[c, slot],
            land.at[c, slot],
            x_send.at[c, side],
            x_recv.at[c, side],
            device_id=(me_e, right if side == 0 else left),
            device_id_type=mesh_id,
        )

    def f_copy(c, side, slot, part):
        rows = pl.ds(part * half, half)
        return pltpu.make_async_remote_copy(
            land.at[c, slot, rows],
            land.at[c, slot, rows],
            f_send.at[c, side],
            f_recv.at[c, side],
            device_id=(me_e, right if side == 0 else left),
            device_id_type=mesh_id,
        )

    _greet_all(me_e, me_r, groups, replicas)

    locals_ = []
    for c in range(chunks):
        local = pltpu.make_async_copy(src_ref.at[c, me_e], land.at[c, me_r, me_e], local_sem.at[c])
        local.start()
        locals_.append(local)

        def send(step, carry, c=c):
            ep_copy(c, lax.rem(me_e + step, groups), me_e).start()
            return carry

        lax.fori_loop(1, groups, send, 0)

    def forward(c):
        x_copy(c, 0, left).wait_recv()
        f_copy(c, 0, left, 1).start()
        x_copy(c, 1, right).wait_recv()
        f_copy(c, 1, right, 0).start()

    for c in range(chunks):
        locals_[c].wait()

        def arrive(step, carry, c=c):
            peer = lax.rem(me_e + step, groups)
            ep_copy(c, peer, peer).wait_recv()
            return carry

        lax.fori_loop(1, groups, arrive, 0)
        x_copy(c, 0, me_r).start()
        x_copy(c, 1, me_r).start()
        if c >= 1:
            forward(c - 1)
    forward(chunks - 1)

    for c in range(chunks):
        f_copy(c, 0, across, 1).wait_recv()
        f_copy(c, 1, across, 0).wait_recv()
        for slot in range(replicas):
            out_ref[c, slot] = land[c, slot].reshape(out_ref.shape[2:])
        for side in range(2):
            x_copy(c, side, me_r).wait_send()
        f_copy(c, 0, left, 1).wait_send()
        f_copy(c, 1, right, 0).wait_send()

        def sent(step, carry, c=c):
            ep_copy(c, lax.rem(me_e + step, groups), me_e).wait_send()
            return carry

        lax.fori_loop(1, groups, sent, 0)


def dispatch(blocks, replicas):
    chunks, groups = blocks.shape[:2]
    tile = blocks.shape[2:]
    out_shape = (chunks, replicas, groups, tile[0] * tile[1])
    return pl.pallas_call(
        _dispatch_kernel,
        out_shape=jax.ShapeDtypeStruct(out_shape, blocks.dtype),
        in_specs=[pl.BlockSpec(memory_space=pl.ANY)],
        out_specs=pl.BlockSpec(memory_space=pltpu.VMEM),
        scratch_shapes=[
            pltpu.VMEM((chunks, replicas) + blocks.shape[1:], blocks.dtype),
            pltpu.SemaphoreType.DMA((chunks, groups)),
            pltpu.SemaphoreType.DMA((chunks, groups)),
            pltpu.SemaphoreType.DMA((chunks,)),
            pltpu.SemaphoreType.DMA((chunks, 2)),
            pltpu.SemaphoreType.DMA((chunks, 2)),
            pltpu.SemaphoreType.DMA((chunks, 2)),
            pltpu.SemaphoreType.DMA((chunks, 2)),
        ],
        compiler_params=pltpu.CompilerParams(collective_id=2, has_side_effects=True),
    )(blocks)


def _combine_kernel(terms_ref, out_ref, parts, sums, x_send, x_recv, x_local, ep_send, ep_recv, ep_local):
    chunks, replicas, groups = terms_ref.shape[:3]
    me_e = lax.axis_index("ep")
    me_r = lax.axis_index("rep")
    mesh_id = pl.DeviceIdType.MESH

    def x_copy(c, peer, slot):
        return pltpu.make_async_remote_copy(
            terms_ref.at[c, peer],
            parts.at[c, slot],
            x_send.at[c, peer],
            x_recv.at[c, slot],
            device_id=(me_e, peer),
            device_id_type=mesh_id,
        )

    def ep_copy(c, peer, slot):
        return pltpu.make_async_remote_copy(
            sums.at[c, peer],
            out_ref.at[c, slot],
            ep_send.at[c, peer],
            ep_recv.at[c, slot],
            device_id=(peer, me_r),
            device_id_type=mesh_id,
        )

    barrier = pltpu.get_barrier_semaphore()

    def greet(step, carry):
        pl.semaphore_signal(
            barrier, 1, device_id=(lax.rem(me_e + step, groups), me_r), device_id_type=mesh_id
        )
        return carry

    lax.fori_loop(1, groups, greet, 0)
    for step in range(1, replicas):
        pl.semaphore_signal(
            barrier, 1, device_id=(me_e, lax.rem(me_r + step, replicas)), device_id_type=mesh_id
        )
    pl.semaphore_wait(barrier, groups - 1 + replicas - 1)

    x_locals = []
    for c in range(chunks):
        local = pltpu.make_async_copy(terms_ref.at[c, me_r], parts.at[c, me_r], x_local.at[c])
        local.start()
        x_locals.append(local)
        for step in range(1, replicas):
            x_copy(c, lax.rem(me_r + step, replicas), me_r).start()

    ep_locals = []
    for c in range(chunks):
        x_locals[c].wait()
        for step in range(1, replicas):
            peer = lax.rem(me_r + step, replicas)
            x_copy(c, peer, peer).wait_recv()
        total = parts[c, 0].astype(jnp.float32)
        for source in range(1, replicas):
            total = total + parts[c, source].astype(jnp.float32)
        sums[c] = total.reshape(sums.shape[1:]).astype(sums.dtype)
        local = pltpu.make_async_copy(sums.at[c, me_e], out_ref.at[c, me_e], ep_local.at[c])
        local.start()
        ep_locals.append(local)

        def send(step, carry, c=c):
            ep_copy(c, lax.rem(me_e + step, groups), me_e).start()
            return carry

        lax.fori_loop(1, groups, send, 0)

    for c in range(chunks):
        for step in range(1, replicas):
            x_copy(c, lax.rem(me_r + step, replicas), me_r).wait_send()
        ep_locals[c].wait()

        def finish(step, carry, c=c):
            peer = lax.rem(me_e + step, groups)
            ep_copy(c, peer, me_e).wait_send()
            ep_copy(c, peer, peer).wait_recv()
            return carry

        lax.fori_loop(1, groups, finish, 0)


def combine_return(terms):
    chunks, replicas, groups, width = terms.shape
    lanes = 128
    tile = (width // lanes, lanes)
    return pl.pallas_call(
        _combine_kernel,
        out_shape=jax.ShapeDtypeStruct((chunks, groups) + tile, terms.dtype),
        in_specs=[pl.BlockSpec(memory_space=pl.ANY)],
        out_specs=pl.BlockSpec(memory_space=pl.ANY),
        scratch_shapes=[
            pltpu.VMEM(terms.shape, terms.dtype),
            pltpu.VMEM((chunks, groups) + tile, terms.dtype),
            pltpu.SemaphoreType.DMA((chunks, replicas)),
            pltpu.SemaphoreType.DMA((chunks, replicas)),
            pltpu.SemaphoreType.DMA((chunks,)),
            pltpu.SemaphoreType.DMA((chunks, groups)),
            pltpu.SemaphoreType.DMA((chunks, groups)),
            pltpu.SemaphoreType.DMA((chunks,)),
        ],
        compiler_params=pltpu.CompilerParams(collective_id=3, has_side_effects=True),
    )(terms)


def _hidden_kernel(terms_ref, resid_ref, out_ref, parts, own, t_send, t_recv, t_local, h_send, h_recv, h_local):
    replicas = terms_ref.shape[0]
    me_e = lax.axis_index("ep")
    me_r = lax.axis_index("rep")
    mesh_id = pl.DeviceIdType.MESH

    def t_copy(peer, slot):
        return pltpu.make_async_remote_copy(
            terms_ref.at[peer],
            parts.at[slot],
            t_send.at[peer],
            t_recv.at[slot],
            device_id=(me_e, peer),
            device_id_type=mesh_id,
        )

    def h_copy(peer, slot):
        return pltpu.make_async_remote_copy(
            own,
            out_ref.at[slot],
            h_send.at[peer],
            h_recv.at[slot],
            device_id=(me_e, peer),
            device_id_type=mesh_id,
        )

    barrier = pltpu.get_barrier_semaphore()
    for step in range(1, replicas):
        pl.semaphore_signal(
            barrier, 1, device_id=(me_e, lax.rem(me_r + step, replicas)), device_id_type=mesh_id
        )
    pl.semaphore_wait(barrier, replicas - 1)
    local = pltpu.make_async_copy(terms_ref.at[me_r], parts.at[me_r], t_local)
    local.start()
    for step in range(1, replicas):
        t_copy(lax.rem(me_r + step, replicas), me_r).start()
    local.wait()
    for step in range(1, replicas):
        peer = lax.rem(me_r + step, replicas)
        t_copy(peer, peer).wait_recv()
    total = parts[0].astype(jnp.float32)
    for source in range(1, replicas):
        total = total + parts[source].astype(jnp.float32)
    attended = total.astype(own.dtype).astype(jnp.float32)
    own[...] = (resid_ref[...].astype(jnp.float32) + attended).astype(own.dtype)
    keep = pltpu.make_async_copy(own, out_ref.at[me_r], h_local)
    keep.start()
    for step in range(1, replicas):
        h_copy(lax.rem(me_r + step, replicas), me_r).start()
    for step in range(1, replicas):
        peer = lax.rem(me_r + step, replicas)
        t_copy(peer, me_r).wait_send()
        h_copy(peer, me_r).wait_send()
        h_copy(peer, peer).wait_recv()
    keep.wait()


def hidden_rows(terms, residual_block):
    replicas = terms.shape[0]
    block = terms.shape[1:]
    return pl.pallas_call(
        _hidden_kernel,
        out_shape=jax.ShapeDtypeStruct(terms.shape, terms.dtype),
        in_specs=[pl.BlockSpec(memory_space=pl.ANY), pl.BlockSpec(memory_space=pltpu.VMEM)],
        out_specs=pl.BlockSpec(memory_space=pl.ANY),
        scratch_shapes=[
            pltpu.VMEM(terms.shape, terms.dtype),
            pltpu.VMEM(block, terms.dtype),
            pltpu.SemaphoreType.DMA((replicas,)),
            pltpu.SemaphoreType.DMA((replicas,)),
            pltpu.SemaphoreType.DMA(()),
            pltpu.SemaphoreType.DMA((replicas,)),
            pltpu.SemaphoreType.DMA((replicas,)),
            pltpu.SemaphoreType.DMA(()),
        ],
        compiler_params=pltpu.CompilerParams(collective_id=4, has_side_effects=True),
    )(terms, residual_block)


def rep_exchange(blocks):
    return lax.all_to_all(blocks, "rep", split_axis=0, concat_axis=0, tiled=True)


def per_device(
    residual,
    query_latent,
    query_rope,
    cache_latent,
    cache_rope,
    page_table,
    lengths,
    value_up,
    out_proj,
    routes,
    route_weight,
    placement,
    expert_gate,
    expert_up,
    expert_down,
    shared_gate,
    shared_up,
    shared_down,
    norm_gain,
):
    replicas = lax.axis_size("rep")
    expert_groups = lax.axis_size("ep")
    rep_index = lax.axis_index("rep")
    latent_out = attend_rows(
        query_latent, query_rope, cache_latent, cache_rope, page_table, lengths
    )
    own_count = latent_out.shape[0]
    swapped = lax.all_to_all(latent_out, "rep", split_axis=1, concat_axis=0, tiled=True)
    group_rows = swapped.shape[0]
    head_out = jnp.einsum(
        "thr,hrv->thv", swapped, value_up, preferred_element_type=jnp.float32
    ).astype(jnp.bfloat16)
    attn_terms = jnp.dot(
        head_out.reshape(group_rows, -1), out_proj, preferred_element_type=jnp.float32
    )
    model_width = attn_terms.shape[1]
    own_residual = lax.dynamic_slice_in_dim(residual, rep_index * own_count, own_count, 0)
    hidden = hidden_rows(
        attn_terms.astype(jnp.bfloat16).reshape(replicas, own_count, model_width), own_residual
    ).reshape(group_rows, model_width)
    own_hidden = lax.dynamic_slice_in_dim(hidden, rep_index * own_count, own_count, 0)
    shared_act = (
        jax.nn.silu(jnp.dot(hidden, shared_gate, preferred_element_type=jnp.float32))
        * jnp.dot(hidden, shared_up, preferred_element_type=jnp.float32)
    ).astype(jnp.bfloat16)
    shared_terms = jnp.dot(shared_act, shared_down, preferred_element_type=jnp.float32)
    experts = placement.shape[0]
    route_count = routes.shape[1]
    assert experts == expert_groups and replicas == 4
    capacity = max(
        replicas, min(group_rows, 2 * group_rows * route_count // experts // replicas * replicas)
    )
    share = capacity // replicas
    expert_ids = jnp.arange(experts, dtype=jnp.int32)
    slot_index = jnp.sum(jnp.where(routes[:, :, None] == expert_ids, placement, 0), axis=2).reshape(
        -1
    )
    one_hot = (slot_index[:, None] == expert_ids[None, :]).astype(jnp.int32)
    earlier = jnp.cumsum(one_hot, axis=0) - one_hot
    position = jnp.sum(earlier * one_hot, axis=1)
    assignments = slot_index.shape[0]
    row_tag = (jnp.arange(assignments, dtype=jnp.int32) // route_count + 1).astype(jnp.float32)
    own_pos = rep_index * share + jnp.arange(share, dtype=jnp.int32)
    filled = jnp.einsum(
        "ae,ac->ce",
        one_hot.astype(jnp.float32) * row_tag[:, None],
        (position[:, None] == own_pos[None, :]).astype(jnp.float32),
        precision=lax.Precision.HIGHEST,
        preferred_element_type=jnp.float32,
    )
    own_source = jnp.where(filled > 0, filled.astype(jnp.int32) - 1, group_rows).reshape(-1)
    lanes = 128
    hidden_tiles = hidden.reshape(group_rows, model_width // lanes, lanes)
    outgoing = jnp.where(
        (own_source < group_rows)[:, None, None],
        hidden_tiles[jnp.minimum(own_source, group_rows - 1)],
        jnp.zeros((), jnp.bfloat16),
    ).reshape(share, experts, model_width // lanes, lanes)
    gathered = dispatch(outgoing, replicas)
    gate_values = jnp.einsum(
        "cqgd,df->cqgf", gathered, expert_gate[0], preferred_element_type=jnp.float32
    )
    up_values = jnp.einsum(
        "cqgd,df->cqgf", gathered, expert_up[0], preferred_element_type=jnp.float32
    )
    activated = (jax.nn.silu(gate_values) * up_values).astype(jnp.bfloat16)
    expert_terms = jnp.einsum(
        "cqgf,fd->cqgd", activated, expert_down[0], preferred_element_type=jnp.float32
    ).astype(jnp.bfloat16)
    returned = combine_return(expert_terms).reshape(share * experts, model_width)
    local_pos = position - rep_index * share
    mine = (local_pos >= 0) & (local_pos < share)
    column = jnp.clip(local_pos, 0, share - 1) * experts + slot_index
    weight_used = jnp.where(mine, route_weight.reshape(-1), 0.0)
    combine = jnp.sum(
        jnp.where(
            column[:, None] == jnp.arange(experts * share, dtype=jnp.int32)[None, :],
            weight_used[:, None],
            0.0,
        ).reshape(group_rows, route_count, experts * share),
        axis=1,
    )
    routed = jnp.dot(
        combine, returned.astype(jnp.float32), precision=lax.Precision.HIGHEST,
        preferred_element_type=jnp.float32,
    )
    row_sums = jnp.sum(
        rep_exchange(
            (routed + shared_terms).astype(jnp.bfloat16).reshape(replicas, own_count, model_width)
        ).astype(jnp.float32),
        axis=0,
    )
    mixed = row_sums + own_hidden.astype(jnp.float32)
    inverse = lax.rsqrt(jnp.mean(mixed * mixed, axis=1, keepdims=True) + EPSILON)
    return (mixed * inverse * norm_gain).astype(jnp.bfloat16)


def solution(mesh):
    in_specs = (
        P("ep", None),
        P(("ep", "rep"), None),
        P(("ep", "rep"), None),
        P(("ep", "rep"), None, None),
        P(("ep", "rep"), None),
        P(("ep", "rep"), None),
        P(("ep", "rep")),
        P("rep", None, None),
        P("rep", None),
        P("ep", None),
        P("ep", None),
        P(),
        P("ep", None, "rep"),
        P("ep", None, "rep"),
        P("ep", "rep", None),
        P(None, "rep"),
        P(None, "rep"),
        P("rep", None),
        P(),
    )
    out_specs = P(("ep", "rep"), None)
    return jax.shard_map(
        per_device, mesh=mesh, in_specs=in_specs, out_specs=out_specs, check_vma=False
    )
```

```python
import functools
import math

import jax
import jax.numpy as jnp
from jax import lax
from jax.experimental import pallas as pl
from jax.experimental.pallas import tpu as pltpu
from jax.sharding import PartitionSpec as P

ROPE = 64
VHEAD = 128


EPSILON = 1e-06


def attend_rows(query_latent, query_rope, cache_latent, cache_rope, page_table, lengths):
    row_count, table_len = page_table.shape
    page_count, page_len, latent_width = cache_latent.shape
    rope_width = cache_rope.shape[1] // page_len
    head_count = query_rope.shape[1] // rope_width
    positions = page_count * page_len
    keys_lat = cache_latent.reshape(positions, latent_width)
    keys_rope = cache_rope.reshape(positions, rope_width)
    query_lat = query_latent.reshape(row_count, head_count, latent_width)
    query_rot = query_rope.reshape(row_count, head_count, rope_width)
    score_scale = 1.0 / math.sqrt(VHEAD + ROPE)
    scores = (
        jnp.einsum("thr,pr->thp", query_lat, keys_lat, preferred_element_type=jnp.float32)
        + jnp.einsum("thr,pr->thp", query_rot, keys_rope, preferred_element_type=jnp.float32)
    ) * score_scale
    page_hit = (
        page_table[:, :, None] == jnp.arange(page_count, dtype=jnp.int32)[None, None, :]
    ).astype(jnp.float32)
    context_pos = (
        jnp.arange(table_len, dtype=jnp.int32)[:, None] * page_len
        + jnp.arange(page_len, dtype=jnp.int32)[None, :]
    )
    live = (context_pos[None, :, :] < lengths[:, None, None]).astype(jnp.float32)
    count = jnp.einsum("tkp,tks->tps", page_hit, live).reshape(row_count, 1, positions)
    present = count > 0
    masked = jnp.where(present, scores, -jnp.inf)
    row_peak = jnp.max(masked, axis=2, keepdims=True)
    expons = jnp.where(present, jnp.exp(scores - row_peak), 0.0)
    total = jnp.sum(expons * count, axis=2, keepdims=True)
    probs = (expons / total).astype(jnp.bfloat16)
    weighted = (probs.astype(jnp.float32) * count).astype(jnp.bfloat16)
    latent_out = jnp.einsum("thp,pr->thr", weighted, keys_lat, preferred_element_type=jnp.float32)
    return latent_out.astype(jnp.bfloat16)


def _greet_all(me_e, me_r, groups, replicas):
    mesh_id = pl.DeviceIdType.MESH
    barrier = pltpu.get_barrier_semaphore()

    def greet(step, carry):
        pl.semaphore_signal(
            barrier, 1, device_id=(lax.rem(me_e + step, groups), me_r), device_id_type=mesh_id
        )
        return carry

    lax.fori_loop(1, groups, greet, 0)
    for step in range(1, replicas):
        pl.semaphore_signal(
            barrier, 1, device_id=(me_e, lax.rem(me_r + step, replicas)), device_id_type=mesh_id
        )
    pl.semaphore_wait(barrier, groups - 1 + replicas - 1)


def _dispatch_kernel(src_ref, out_ref, land, ep_send, ep_recv, local_sem, x_send, x_recv, f_send, f_recv):
    chunks, groups = src_ref.shape[:2]
    replicas = land.shape[1]
    half = groups // 2
    me_e = lax.axis_index("ep")
    me_r = lax.axis_index("rep")
    right = lax.rem(me_r + 1, replicas)
    left = lax.rem(me_r + replicas - 1, replicas)
    across = lax.rem(me_r + 2, replicas)
    mesh_id = pl.DeviceIdType.MESH

    def ep_copy(c, peer, slot):
        return pltpu.make_async_remote_copy(
            src_ref.at[c, peer],
            land.at[c, me_r, slot],
            ep_send.at[c, peer],
            ep_recv.at[c, slot],
            device_id=(peer, me_r),
            device_id_type=mesh_id,
        )

    def x_copy(c, side, slot):
        return pltpu.make_async_remote_copy(
            land.at[c, slot],
            land.at[c, slot],
            x_send.at[c, side],
            x_recv.at[c, side],
            device_id=(me_e, right if side == 0 else left),
            device_id_type=mesh_id,
        )

    def f_copy(c, side, slot, part):
        rows = pl.ds(part * half, half)
        return pltpu.make_async_remote_copy(
            land.at[c, slot, rows],
            land.at[c, slot, rows],
            f_send.at[c, side],
            f_recv.at[c, side],
            device_id=(me_e, right if side == 0 else left),
            device_id_type=mesh_id,
        )

    _greet_all(me_e, me_r, groups, replicas)

    locals_ = []
    for c in range(chunks):
        local = pltpu.make_async_copy(src_ref.at[c, me_e], land.at[c, me_r, me_e], local_sem.at[c])
        local.start()
        locals_.append(local)

        def send(step, carry, c=c):
            ep_copy(c, lax.rem(me_e + step, groups), me_e).start()
            return carry

        lax.fori_loop(1, groups, send, 0)

    def forward(c):
        x_copy(c, 0, left).wait_recv()
        f_copy(c, 0, left, 1).start()
        x_copy(c, 1, right).wait_recv()
        f_copy(c, 1, right, 0).start()

    for c in range(chunks):
        locals_[c].wait()

        def arrive(step, carry, c=c):
            peer = lax.rem(me_e + step, groups)
            ep_copy(c, peer, peer).wait_recv()
            return carry

        lax.fori_loop(1, groups, arrive, 0)
        x_copy(c, 0, me_r).start()
        x_copy(c, 1, me_r).start()
        if c >= 1:
            forward(c - 1)
    forward(chunks - 1)

    for c in range(chunks):
        f_copy(c, 0, across, 1).wait_recv()
        f_copy(c, 1, across, 0).wait_recv()
        for slot in range(replicas):
            out_ref[c, slot] = land[c, slot].reshape(out_ref.shape[2:])
        for side in range(2):
            x_copy(c, side, me_r).wait_send()
        f_copy(c, 0, left, 1).wait_send()
        f_copy(c, 1, right, 0).wait_send()

        def sent(step, carry, c=c):
            ep_copy(c, lax.rem(me_e + step, groups), me_e).wait_send()
            return carry

        lax.fori_loop(1, groups, sent, 0)


def dispatch(blocks, replicas):
    chunks, groups = blocks.shape[:2]
    tile = blocks.shape[2:]
    out_shape = (chunks, replicas, groups, tile[0] * tile[1])
    return pl.pallas_call(
        _dispatch_kernel,
        out_shape=jax.ShapeDtypeStruct(out_shape, blocks.dtype),
        in_specs=[pl.BlockSpec(memory_space=pl.ANY)],
        out_specs=pl.BlockSpec(memory_space=pltpu.VMEM),
        scratch_shapes=[
            pltpu.VMEM((chunks, replicas) + blocks.shape[1:], blocks.dtype),
            pltpu.SemaphoreType.DMA((chunks, groups)),
            pltpu.SemaphoreType.DMA((chunks, groups)),
            pltpu.SemaphoreType.DMA((chunks,)),
            pltpu.SemaphoreType.DMA((chunks, 2)),
            pltpu.SemaphoreType.DMA((chunks, 2)),
            pltpu.SemaphoreType.DMA((chunks, 2)),
            pltpu.SemaphoreType.DMA((chunks, 2)),
        ],
        compiler_params=pltpu.CompilerParams(collective_id=2, has_side_effects=True),
    )(blocks)


def _combine_kernel(terms_ref, out_ref, parts, sums, land, x_send, x_recv, x_local, ep_send, ep_recv, ep_local):
    chunks, replicas, groups = terms_ref.shape[:3]
    me_e = lax.axis_index("ep")
    me_r = lax.axis_index("rep")
    mesh_id = pl.DeviceIdType.MESH

    def x_copy(c, peer, slot):
        return pltpu.make_async_remote_copy(
            terms_ref.at[c, peer],
            parts.at[c, slot],
            x_send.at[c, peer],
            x_recv.at[c, slot],
            device_id=(me_e, peer),
            device_id_type=mesh_id,
        )

    def ep_copy(c, peer, slot):
        return pltpu.make_async_remote_copy(
            sums.at[c, peer],
            land.at[c, slot],
            ep_send.at[c, peer],
            ep_recv.at[c, slot],
            device_id=(peer, me_r),
            device_id_type=mesh_id,
        )

    barrier = pltpu.get_barrier_semaphore()

    def greet(step, carry):
        pl.semaphore_signal(
            barrier, 1, device_id=(lax.rem(me_e + step, groups), me_r), device_id_type=mesh_id
        )
        return carry

    lax.fori_loop(1, groups, greet, 0)
    for step in range(1, replicas):
        pl.semaphore_signal(
            barrier, 1, device_id=(me_e, lax.rem(me_r + step, replicas)), device_id_type=mesh_id
        )
    pl.semaphore_wait(barrier, groups - 1 + replicas - 1)

    x_locals = []
    for c in range(chunks):
        local = pltpu.make_async_copy(terms_ref.at[c, me_r], parts.at[c, me_r], x_local.at[c])
        local.start()
        x_locals.append(local)
        for step in range(1, replicas):
            x_copy(c, lax.rem(me_r + step, replicas), me_r).start()

    ep_locals = []
    for c in range(chunks):
        x_locals[c].wait()
        for step in range(1, replicas):
            peer = lax.rem(me_r + step, replicas)
            x_copy(c, peer, peer).wait_recv()
        total = parts[c, 0].astype(jnp.float32)
        for source in range(1, replicas):
            total = total + parts[c, source].astype(jnp.float32)
        sums[c] = total.reshape(sums.shape[1:]).astype(sums.dtype)
        local = pltpu.make_async_copy(sums.at[c, me_e], land.at[c, me_e], ep_local.at[c])
        local.start()
        ep_locals.append(local)

        def send(step, carry, c=c):
            ep_copy(c, lax.rem(me_e + step, groups), me_e).start()
            return carry

        lax.fori_loop(1, groups, send, 0)

    for c in range(chunks):
        for step in range(1, replicas):
            x_copy(c, lax.rem(me_r + step, replicas), me_r).wait_send()
        ep_locals[c].wait()

        def finish(step, carry, c=c):
            peer = lax.rem(me_e + step, groups)
            ep_copy(c, peer, me_e).wait_send()
            ep_copy(c, peer, peer).wait_recv()
            return carry

        lax.fori_loop(1, groups, finish, 0)
        out_ref[c] = land[c].reshape(out_ref.shape[1:])


def combine_return(terms):
    chunks, replicas, groups, width = terms.shape
    lanes = 128
    tile = (width // lanes, lanes)
    return pl.pallas_call(
        _combine_kernel,
        out_shape=jax.ShapeDtypeStruct((chunks, groups, width), terms.dtype),
        in_specs=[pl.BlockSpec(memory_space=pl.ANY)],
        out_specs=pl.BlockSpec(memory_space=pltpu.VMEM),
        scratch_shapes=[
            pltpu.VMEM(terms.shape, terms.dtype),
            pltpu.VMEM((chunks, groups) + tile, terms.dtype),
            pltpu.VMEM((chunks, groups) + tile, terms.dtype),
            pltpu.SemaphoreType.DMA((chunks, replicas)),
            pltpu.SemaphoreType.DMA((chunks, replicas)),
            pltpu.SemaphoreType.DMA((chunks,)),
            pltpu.SemaphoreType.DMA((chunks, groups)),
            pltpu.SemaphoreType.DMA((chunks, groups)),
            pltpu.SemaphoreType.DMA((chunks,)),
        ],
        compiler_params=pltpu.CompilerParams(collective_id=3, has_side_effects=True),
    )(terms)


def _hidden_kernel(terms_ref, resid_ref, out_ref, parts, own, t_send, t_recv, t_local, h_send, h_recv, h_local):
    replicas = terms_ref.shape[0]
    me_e = lax.axis_index("ep")
    me_r = lax.axis_index("rep")
    mesh_id = pl.DeviceIdType.MESH

    def t_copy(peer, slot):
        return pltpu.make_async_remote_copy(
            terms_ref.at[peer],
            parts.at[slot],
            t_send.at[peer],
            t_recv.at[slot],
            device_id=(me_e, peer),
            device_id_type=mesh_id,
        )

    def h_copy(peer, slot):
        return pltpu.make_async_remote_copy(
            own,
            out_ref.at[slot],
            h_send.at[peer],
            h_recv.at[slot],
            device_id=(me_e, peer),
            device_id_type=mesh_id,
        )

    barrier = pltpu.get_barrier_semaphore()
    for step in range(1, replicas):
        pl.semaphore_signal(
            barrier, 1, device_id=(me_e, lax.rem(me_r + step, replicas)), device_id_type=mesh_id
        )
    pl.semaphore_wait(barrier, replicas - 1)
    local = pltpu.make_async_copy(terms_ref.at[me_r], parts.at[me_r], t_local)
    local.start()
    for step in range(1, replicas):
        t_copy(lax.rem(me_r + step, replicas), me_r).start()
    local.wait()
    for step in range(1, replicas):
        peer = lax.rem(me_r + step, replicas)
        t_copy(peer, peer).wait_recv()
    total = parts[0].astype(jnp.float32)
    for source in range(1, replicas):
        total = total + parts[source].astype(jnp.float32)
    attended = total.astype(own.dtype).astype(jnp.float32)
    own[...] = (resid_ref[...].astype(jnp.float32) + attended).astype(own.dtype)
    keep = pltpu.make_async_copy(own, out_ref.at[me_r], h_local)
    keep.start()
    for step in range(1, replicas):
        h_copy(lax.rem(me_r + step, replicas), me_r).start()
    for step in range(1, replicas):
        peer = lax.rem(me_r + step, replicas)
        t_copy(peer, me_r).wait_send()
        h_copy(peer, me_r).wait_send()
        h_copy(peer, peer).wait_recv()
    keep.wait()


def hidden_rows(terms, residual_block):
    replicas = terms.shape[0]
    block = terms.shape[1:]
    return pl.pallas_call(
        _hidden_kernel,
        out_shape=jax.ShapeDtypeStruct(terms.shape, terms.dtype),
        in_specs=[pl.BlockSpec(memory_space=pl.ANY), pl.BlockSpec(memory_space=pltpu.VMEM)],
        out_specs=pl.BlockSpec(memory_space=pl.ANY),
        scratch_shapes=[
            pltpu.VMEM(terms.shape, terms.dtype),
            pltpu.VMEM(block, terms.dtype),
            pltpu.SemaphoreType.DMA((replicas,)),
            pltpu.SemaphoreType.DMA((replicas,)),
            pltpu.SemaphoreType.DMA(()),
            pltpu.SemaphoreType.DMA((replicas,)),
            pltpu.SemaphoreType.DMA((replicas,)),
            pltpu.SemaphoreType.DMA(()),
        ],
        compiler_params=pltpu.CompilerParams(collective_id=4, has_side_effects=True),
    )(terms, residual_block)


def rep_exchange(blocks):
    return lax.all_to_all(blocks, "rep", split_axis=0, concat_axis=0, tiled=True)


def per_device(
    residual,
    query_latent,
    query_rope,
    cache_latent,
    cache_rope,
    page_table,
    lengths,
    value_up,
    out_proj,
    routes,
    route_weight,
    placement,
    expert_gate,
    expert_up,
    expert_down,
    shared_gate,
    shared_up,
    shared_down,
    norm_gain,
):
    replicas = lax.axis_size("rep")
    expert_groups = lax.axis_size("ep")
    rep_index = lax.axis_index("rep")
    latent_out = attend_rows(
        query_latent, query_rope, cache_latent, cache_rope, page_table, lengths
    )
    own_count = latent_out.shape[0]
    swapped = lax.all_to_all(latent_out, "rep", split_axis=1, concat_axis=0, tiled=True)
    group_rows = swapped.shape[0]
    head_out = jnp.einsum(
        "thr,hrv->thv", swapped, value_up, preferred_element_type=jnp.float32
    ).astype(jnp.bfloat16)
    attn_terms = jnp.dot(
        head_out.reshape(group_rows, -1), out_proj, preferred_element_type=jnp.float32
    )
    model_width = attn_terms.shape[1]
    own_residual = lax.dynamic_slice_in_dim(residual, rep_index * own_count, own_count, 0)
    hidden = hidden_rows(
        attn_terms.astype(jnp.bfloat16).reshape(replicas, own_count, model_width), own_residual
    ).reshape(group_rows, model_width)
    own_hidden = lax.dynamic_slice_in_dim(hidden, rep_index * own_count, own_count, 0)
    shared_act = (
        jax.nn.silu(jnp.dot(hidden, shared_gate, preferred_element_type=jnp.float32))
        * jnp.dot(hidden, shared_up, preferred_element_type=jnp.float32)
    ).astype(jnp.bfloat16)
    shared_terms = jnp.dot(shared_act, shared_down, preferred_element_type=jnp.float32)
    experts = placement.shape[0]
    route_count = routes.shape[1]
    assert experts == expert_groups and replicas == 4
    capacity = max(
        replicas, min(group_rows, 2 * group_rows * route_count // experts // replicas * replicas)
    )
    share = capacity // replicas
    expert_ids = jnp.arange(experts, dtype=jnp.int32)
    slot_index = jnp.sum(jnp.where(routes[:, :, None] == expert_ids, placement, 0), axis=2).reshape(
        -1
    )
    one_hot = (slot_index[:, None] == expert_ids[None, :]).astype(jnp.int32)
    earlier = jnp.cumsum(one_hot, axis=0) - one_hot
    position = jnp.sum(earlier * one_hot, axis=1)
    assignments = slot_index.shape[0]
    row_tag = (jnp.arange(assignments, dtype=jnp.int32) // route_count + 1).astype(jnp.float32)
    own_pos = rep_index * share + jnp.arange(share, dtype=jnp.int32)
    filled = jnp.einsum(
        "ae,ac->ce",
        one_hot.astype(jnp.float32) * row_tag[:, None],
        (position[:, None] == own_pos[None, :]).astype(jnp.float32),
        precision=lax.Precision.HIGHEST,
        preferred_element_type=jnp.float32,
    )
    own_source = jnp.where(filled > 0, filled.astype(jnp.int32) - 1, group_rows).reshape(-1)
    padded = jnp.concatenate([hidden, jnp.zeros((1, model_width), jnp.bfloat16)], axis=0)
    lanes = 128
    outgoing = padded[own_source].reshape(share, experts, model_width // lanes, lanes)
    gathered = dispatch(outgoing, replicas)
    gate_values = jnp.einsum(
        "cqgd,df->cqgf", gathered, expert_gate[0], preferred_element_type=jnp.float32
    )
    up_values = jnp.einsum(
        "cqgd,df->cqgf", gathered, expert_up[0], preferred_element_type=jnp.float32
    )
    activated = (jax.nn.silu(gate_values) * up_values).astype(jnp.bfloat16)
    expert_terms = jnp.einsum(
        "cqgf,fd->cqgd", activated, expert_down[0], preferred_element_type=jnp.float32
    ).astype(jnp.bfloat16)
    returned = combine_return(expert_terms).reshape(share * experts, model_width)
    local_pos = position - rep_index * share
    mine = (local_pos >= 0) & (local_pos < share)
    column = jnp.clip(local_pos, 0, share - 1) * experts + slot_index
    weight_used = jnp.where(mine, route_weight.reshape(-1), 0.0)
    combine = jnp.sum(
        jnp.where(
            column[:, None] == jnp.arange(experts * share, dtype=jnp.int32)[None, :],
            weight_used[:, None],
            0.0,
        ).reshape(group_rows, route_count, experts * share),
        axis=1,
    )
    routed = jnp.dot(
        combine, returned.astype(jnp.float32), precision=lax.Precision.HIGHEST,
        preferred_element_type=jnp.float32,
    )
    row_sums = jnp.sum(
        rep_exchange(
            (routed + shared_terms).astype(jnp.bfloat16).reshape(replicas, own_count, model_width)
        ).astype(jnp.float32),
        axis=0,
    )
    mixed = row_sums + own_hidden.astype(jnp.float32)
    inverse = lax.rsqrt(jnp.mean(mixed * mixed, axis=1, keepdims=True) + EPSILON)
    return (mixed * inverse * norm_gain).astype(jnp.bfloat16)


def solution(mesh):
    in_specs = (
        P("ep", None),
        P(("ep", "rep"), None),
        P(("ep", "rep"), None),
        P(("ep", "rep"), None, None),
        P(("ep", "rep"), None),
        P(("ep", "rep"), None),
        P(("ep", "rep")),
        P("rep", None, None),
        P("rep", None),
        P("ep", None),
        P("ep", None),
        P(),
        P("ep", None, "rep"),
        P("ep", None, "rep"),
        P("ep", "rep", None),
        P(None, "rep"),
        P(None, "rep"),
        P("rep", None),
        P(),
    )
    out_specs = P(("ep", "rep"), None)
    return jax.shard_map(
        per_device, mesh=mesh, in_specs=in_specs, out_specs=out_specs, check_vma=False
    )
```
